256 devices in a mesh: blk: 32 (over y, z_hi, core), ij: 8 (over z_lo, x).
Axes of the slice: x: 4, y: 4, z: 8 (z_hi: 4, z_lo: 2; z = z_hi * 2 + z_lo), core: 2. Of those that a mesh axis runs over, the one named last changes fastest.
Arguments:
- density: float32 [32, 6, 256, 128], P('blk', None, 'ij'), may hold values from 0.8 to 1.2
- momentum: float32 [32, 3, 6, 256, 128], P('blk', None, None, 'ij'), may hold values from -2.5 to 2.5
- energy: float32 [32, 6, 256, 128], P('blk', None, 'ij'), may hold values from 2.5 to 4
- metrics: float32 [32, 4, 256, 128], P('blk', None, 'ij'), may hold values from -1 to 1
- volume: float32 [32, 256, 128], P('blk', 'ij'), may hold values from 0.5 to 2
- placed: int32 [32], replicated, may hold values from 0 to 31, each once
- neighbour: int32 [32, 2], replicated, may hold values from 0 to 31, as said below
- face: int32 [32, 2], replicated, may hold values from 0 to 1, as said below
- orient: int32 [32, 2], replicated, may hold values from 0 to 1, as said below
Outputs:
- next_density: float32 [32, 6, 256, 128], P('blk', None, 'ij')
- next_momentum: float32 [32, 3, 6, 256, 128], P('blk', None, None, 'ij')
- next_energy: float32 [32, 6, 256, 128], P('blk', None, 'ij')
The draws below stay inside these ranges and needn't reach their ends.
Inputs may be any that keep to these rules, and one draw needn't show every extreme that they name: If face f of block b meets face g of block c with orientation o, then face g of c meets face f of b with orientation o; every block id appears as a neighbour. `face`: consistent with neighbour as stated there. `orient`: consistent with neighbour as stated there.
All inputs are finite; a program needn't handle non-finite values.
Results may differ from the reference program's by a relative error of at most 0.00002.
Values sent between devices are 32-bit elements; how exact they have to be, the bound alone decides.
A program may use at most 128 MiB of HBM per device.

```python
import math
import jax
import jax.numpy as jnp
from jax import lax

NI = 256
NJ = 128
PLANES = 6
BLOCKS = 32


def face_pairing(key):
    order = jax.random.permutation(jax.random.fold_in(key, 7), 2 * BLOCKS).astype(jnp.int32)
    first_half = order[0::2]
    second_half = order[1::2]
    partner = jnp.zeros((2 * BLOCKS,), jnp.int32).at[first_half].set(second_half).at[second_half].set(first_half)
    flips = jax.random.randint(jax.random.fold_in(key, 11), (BLOCKS,), 0, 2, dtype=jnp.int32)
    twisted = jnp.zeros((2 * BLOCKS,), jnp.int32).at[first_half].set(flips).at[second_half].set(flips)
    return (partner.reshape(BLOCKS, 2), twisted.reshape(BLOCKS, 2))


def draw_neighbour(key, part):
    partner, twisted = face_pairing(key)
    return partner // 2


def draw_face(key, part):
    partner, twisted = face_pairing(key)
    return partner % 2


def draw_orient(key, part):
    partner, twisted = face_pairing(key)
    return twisted


def shard_levels(key, dims, pieces, smallest, high):
    level, own = 1.0, jax.random.fold_in(key, 6)
    for dim, parts in pieces:
        heights = jnp.exp(jax.random.uniform(jax.random.fold_in(own, dim), (parts,), jnp.float32, smallest / len(pieces), high / len(pieces)))
        level = level * jnp.repeat(heights, dims[dim] // parts).reshape([-1 if axis == dim else 1 for axis in range(len(dims))])
    return level


def bell_draw(key, extent, width, most, pieces=(), kind=jnp.bfloat16):
    entries = jax.random.normal(key, extent, jnp.float32) * width
    if len(pieces) > 0:
        entries = shard_levels(key, extent, pieces, -0.22, 0.18) * entries
    return jnp.clip(entries, min=-most, max=most).astype(kind)


def setup_inputs(seed: int = 0) -> dict:
    streams_of = jax.random.split(jax.random.key(seed), 10)
    density = jnp.clip(0.8 + 0.40000004 * jax.random.uniform(streams_of[0], (BLOCKS, PLANES, NI, NJ), jnp.float32) ** shard_levels(streams_of[0], (BLOCKS, PLANES, NI, NJ), ((0, 32), (2, 8)), -0.2, 0.2), 0.8, 1.2)
    momentum = bell_draw(streams_of[1], (BLOCKS, 3, PLANES, NI, NJ), 0.3, 2.5, ((0, 32), (3, 8)), jnp.float32)
    energy = jnp.clip(2.5 + 1.5 * jax.random.uniform(streams_of[2], (BLOCKS, PLANES, NI, NJ), jnp.float32) ** shard_levels(streams_of[2], (BLOCKS, PLANES, NI, NJ), ((0, 32), (2, 8)), -0.2, 0.2), 2.5, 4.0)
    metrics = jnp.clip(jax.random.uniform(streams_of[3], (BLOCKS, 4, NI, NJ), jnp.float32, -1.0, 1.0) * shard_levels(streams_of[3], (BLOCKS, 4, NI, NJ), ((0, 32), (2, 8)), -0.4, 0.0), -1.0, 1.0)
    volume = jnp.clip(jnp.exp(math.log(2.0) - 1.3862944 * jax.random.uniform(streams_of[4], (BLOCKS, NI, NJ), jnp.float32) ** shard_levels(streams_of[4], (BLOCKS, NI, NJ), ((0, 32), (1, 8)), -0.2, 0.2)), 0.5, 2.0)
    placed = jax.random.permutation(streams_of[5], BLOCKS).astype(jnp.int32)
    neighbour = draw_neighbour(jax.random.fold_in(streams_of[9], 71), 0)
    face = draw_face(jax.random.fold_in(streams_of[9], 71), 0)
    orient = draw_orient(jax.random.fold_in(streams_of[9], 71), 0)
    return dict(density=density, momentum=momentum, energy=energy, metrics=metrics, volume=volume, placed=placed, neighbour=neighbour, face=face, orient=orient)


pressure_factor = 0.4
viscosity = 0.05
conduction = 0.1
time_step = 0.03


def slope_rows(f):
    return (f[..., 0:-4, 2:-2] - 8.0 * f[..., 1:-3, 2:-2] + 8.0 * f[..., 3:-1, 2:-2] - f[..., 4:, 2:-2]) / 12.0


def slope_cols(f):
    return (f[..., 2:-2, 0:-4] - 8.0 * f[..., 2:-2, 1:-3] + 8.0 * f[..., 2:-2, 3:-1] - f[..., 2:-2, 4:]) / 12.0


def slope_planes(f):
    return (jnp.roll(f, 2, -3) - 8.0 * jnp.roll(f, 1, -3) + 8.0 * jnp.roll(f, -1, -3) - jnp.roll(f, -2, -3)) / 12.0


def curve_rows(f):
    return (-f[..., 0:-4, 2:-2] + 16.0 * f[..., 1:-3, 2:-2] - 30.0 * f[..., 2:-2, 2:-2] + 16.0 * f[..., 3:-1, 2:-2] - f[..., 4:, 2:-2]) / 12.0


def curve_cols(f):
    return (-f[..., 2:-2, 0:-4] + 16.0 * f[..., 2:-2, 1:-3] - 30.0 * f[..., 2:-2, 2:-2] + 16.0 * f[..., 2:-2, 3:-1] - f[..., 2:-2, 4:]) / 12.0


def curve_planes(f):
    return (-jnp.roll(f, 2, -3) + 16.0 * jnp.roll(f, 1, -3) - 30.0 * f + 16.0 * jnp.roll(f, -1, -3) - jnp.roll(f, -2, -3)) / 12.0


def interior(f):
    return f[..., 2:-2, 2:-2]


def residual(ext):
    planes = ext.shape[1] - 1
    fields = ext[:, :planes]
    metric = ext[:, planes]
    dens = fields[0]
    moment = fields[1:4]
    energy_now = fields[4]
    velocity = moment / dens
    kinetic = 0.5 * jnp.sum(moment * velocity, axis=0)
    pressure = pressure_factor * (energy_now - kinetic)
    thermal = pressure / dens
    total_head = energy_now + pressure
    row_ax, row_ay, col_bx, col_by, cell_vol = metric[0], metric[1], metric[2], metric[3], metric[4]
    along_rows = row_ax * velocity[0] + row_ay * velocity[1]
    along_cols = col_bx * velocity[0] + col_by * velocity[1]
    flux_rows = cell_vol * jnp.stack([dens * along_rows, moment[0] * along_rows + row_ax * pressure,
                                      moment[1] * along_rows + row_ay * pressure, moment[2] * along_rows,
                                      total_head * along_rows])
    flux_cols = cell_vol * jnp.stack([dens * along_cols, moment[0] * along_cols + col_bx * pressure,
                                      moment[1] * along_cols + col_by * pressure, moment[2] * along_cols,
                                      total_head * along_cols])
    flux_planes = jnp.stack([moment[2], moment[0] * velocity[2], moment[1] * velocity[2],
                             moment[2] * velocity[2] + pressure, total_head * velocity[2]])
    inviscid = -(slope_rows(flux_rows) + slope_cols(flux_cols)) / interior(cell_vol) - slope_planes(interior(flux_planes))
    row_weight = interior(row_ax * row_ax + row_ay * row_ay)
    col_weight = interior(col_bx * col_bx + col_by * col_by)

    def laplace(w):
        return row_weight * curve_rows(w) + col_weight * curve_cols(w) + curve_planes(interior(w))

    half_speed = kinetic / dens
    diffuse = jnp.stack([jnp.zeros_like(inviscid[0]), viscosity * laplace(velocity[0]),
                         viscosity * laplace(velocity[1]), viscosity * laplace(velocity[2]),
                         viscosity * laplace(half_speed) + conduction * laplace(thermal)])
    return inviscid + diffuse


def wall_signs(planes):
    channel = jnp.arange(5)[:, None]
    plane_index = jnp.arange(planes)[None, :]
    flipped = (channel >= 1) & (channel <= 3) & (plane_index < planes - 1)
    return jnp.where(flipped, -1.0, 1.0)[:, :, None, None]


def ghost_factors(twisted, facing, planes):
    own_face = jnp.arange(2)[None, :]
    turn = jnp.where(twisted == 1, -1.0, 1.0)
    same = jnp.where(facing == own_face, -1.0, 1.0)
    channel = jnp.arange(5)[None, None, :]
    by_channel = jnp.where(channel < 2, turn[:, :, None], jnp.where(channel < 4, same[:, :, None], 1.0))
    metric_plane = (jnp.arange(planes) == planes - 1)[None, None, None, :]
    return jnp.where(metric_plane, by_channel[:, :, :, None], 1.0)


def locate(placed):
    blocks = placed.shape[0]
    slots = jnp.arange(blocks, dtype=jnp.int32)
    return jnp.sum(jnp.where(placed[:, None] == slots[None, :], slots[:, None], 0), axis=0).astype(jnp.int32)


def extend(base, placed, neighbour, face, orient):
    planes = base.shape[2]
    low_wall = base[:, :, :, 1::-1] * wall_signs(planes)
    high_wall = base[:, :, :, -1:-3:-1]
    rowed = jnp.concatenate([low_wall, base, high_wall], axis=3)
    strips = jnp.stack([base[..., 0:2], base[..., -1:-3:-1]], axis=1)
    position_of = locate(placed)
    next_ids = neighbour[placed]
    facing = face[placed]
    twisted = orient[placed]
    partner = position_of[next_ids]
    ghosts = strips[partner, facing]
    ghosts = jnp.where(twisted[:, :, None, None, None, None] == 1, ghosts[..., ::-1, :], ghosts)
    ghosts = ghosts * ghost_factors(twisted, facing, planes)[..., None, None]
    left = jnp.pad(ghosts[:, 0][..., ::-1], ((0, 0), (0, 0), (0, 0), (2, 2), (0, 0)), constant_values=1.0)
    right = jnp.pad(ghosts[:, 1], ((0, 0), (0, 0), (0, 0), (2, 2), (0, 0)), constant_values=1.0)
    return jnp.concatenate([left, rowed, right], axis=-1)


def reference(density, momentum, energy, metrics, volume, placed, neighbour, face, orient):
    fields = jnp.concatenate([density[:, None], momentum, energy[:, None]], axis=1)
    metric_plane = jnp.concatenate([metrics, volume[:, None]], axis=1)[:, :, None]

    def tendency(state):
        ext = extend(jnp.concatenate([state, metric_plane], axis=2), placed, neighbour, face, orient)
        return lax.map(residual, ext)

    section = fields + time_step * tendency(fields)
    result = 0.5 * fields + 0.5 * (section + time_step * tendency(section))
    return result[:, 0], result[:, 1:4], result[:, 4]
```

```python
import functools

import jax
import jax.numpy as jnp
from jax import lax
from jax.experimental import pallas as pl
from jax.experimental.pallas import tpu as pltpu
from jax.sharding import PartitionSpec as P

MESH = pl.DeviceIdType.MESH
pressure_factor = 0.4
viscosity = 0.05
conduction = 0.1
time_step = 0.03
ROWS, COLS, PLANES, CHUNK = 32, 128, 6, 8
Y, Z, CORES, IJ, BLOCKS = 4, 4, 2, 8, 32
STRIP = (ROWS, COLS)


def lanes(shape):
    return lax.broadcasted_iota(jnp.int32, shape, len(shape) - 1)


def shift_lanes(x, by):
    by = by % COLS
    return x if by == 0 else pltpu.roll(x, by, x.ndim - 1)


def primitives(rho, m1, m2, m3, energy, dt):
    inv = 1.0 / rho
    u1, u2, u3 = m1 * inv, m2 * inv, m3 * inv
    kinetic = 0.5 * (m1 * u1 + m2 * u2 + m3 * u3)
    p = pressure_factor * (energy - kinetic)
    head = energy + p
    soft = dt * viscosity / 12.0
    warm = dt * conduction / 12.0
    curved = (soft * u1, soft * u2, soft * u3, inv * (soft * kinetic + warm * p))
    return u1, u2, u3, p, head, curved


def flux(rho, m1, m2, m3, prim, gx, gy):
    u1, u2, u3, p, head, _ = prim
    speed = gx * u1 + gy * u2
    return (rho * speed, m1 * speed + gx * p, m2 * speed + gy * p, m3 * speed, head * speed)


def slope(b2, b1, a1, a2):
    return 8.0 * (a1 - b1) - (a2 - b2)


def curve(b2, b1, a1, a2):
    return 16.0 * (a1 + b1) - (a2 + b2)


def plane_shift(f, by):
    by = by % PLANES
    return jnp.concatenate([f[by:], f[:by]], axis=0)


def chunk_metrics(met, vol, c, dt):
    rows = slice(c * CHUNK, (c + 1) * CHUNK)
    ax, ay, bx, by = (met[0, n, rows, :] for n in range(4))
    v = vol[0, rows, :]
    return (v * ax, v * ay, v * bx, v * by, (dt / 12.0) / v, ax * ax + ay * ay, bx * bx + by * by)


def before_ghosts(get, met, vol, fi, wi, part, dt):
    for c in range(ROWS // CHUNK):
        rows = slice(c * CHUNK, (c + 1) * CHUNK)
        gax, gay, gbx, gby, iv, rw, cw = chunk_metrics(met, vol, c, dt)
        center = -30.0 * (rw + cw + 1.0)
        rho, m1, m2, m3, energy = (get(ch, rows) for ch in range(5))
        prim = primitives(rho, m1, m2, m3, energy, dt)
        u1, u2, u3, p, head, curved = prim
        inner = slice(CHUNK + c * CHUNK, 2 * CHUNK + c * CHUNK)
        for ch, f in enumerate(flux(rho, m1, m2, m3, prim, gax, gay)):
            fi[ch, :, inner, :] = f
        for n, w in enumerate(curved):
            wi[n, :, inner, :] = w
        fj = flux(rho, m1, m2, m3, prim, gbx, gby)
        fk = (m3, m1 * u3, m2 * u3, m3 * u3 + p, head * u3)
        for ch in range(5):
            f, g = fj[ch], fk[ch]
            dj = slope(*(shift_lanes(f, by) for by in (2, 1, -1, -2)))
            dk = slope(*(plane_shift(g, by) for by in (-2, -1, 1, 2)))
            total = -(dj * iv) - (dt / 12.0) * dk
            if ch > 0:
                w = curved[ch - 1]
                sj = curve(*(shift_lanes(w, by) for by in (2, 1, -1, -2)))
                sk = curve(*(plane_shift(w, by) for by in (-2, -1, 1, 2)))
                total = total + cw * sj + sk + center * w
            part[ch, :, rows, :] = total


def halo_rows(get_halo, fi, wi, dt):
    for n in range(4):
        at = (CHUNK - 2, CHUNK - 1, CHUNK + ROWS, CHUNK + ROWS + 1)[n]
        block = get_halo(n)
        rho, m1, m2, m3, energy = (block[6 * ch : 6 * ch + 6, :] for ch in range(5))
        gax, gay = block[30:31, :], block[31:32, :]
        prim = primitives(rho, m1, m2, m3, energy, dt)
        for ch, f in enumerate(flux(rho, m1, m2, m3, prim, gax, gay)):
            for k in range(PLANES):
                fi[ch, k, at : at + 1, :] = f[k : k + 1, :]
        for m, w in enumerate(prim[5]):
            for k in range(PLANES):
                wi[m, k, at : at + 1, :] = w[k : k + 1, :]


def spread(x):
    x = jnp.where(lanes(x.shape) < 4, x, 0.0)
    pair = x + shift_lanes(x, 4)
    return pair + shift_lanes(pair, 8) + shift_lanes(pair, 16)


def edge_values(strip, dt):
    rho, m1, m2, m3, energy = (shift_lanes(strip, -24 * ch) for ch in range(5))
    gbx, gby = spread(shift_lanes(strip, -120)), spread(shift_lanes(strip, -124))
    prim = primitives(rho, m1, m2, m3, energy, dt)
    return flux(rho, m1, m2, m3, prim, gbx, gby) + prim[5]


def edge_terms(own, ghost, edge, dt):
    upper = (lanes(STRIP) & 3) >= 2
    mine, theirs = edge_values(own, dt), edge_values(ghost, dt)
    for n in range(9):
        h = theirs[n] - mine[n]
        high, low = jnp.where(upper, h, 0.0), jnp.where(upper, 0.0, h)
        if n < 5:
            left = 8.0 * shift_lanes(high, -1) - shift_lanes(high, -2)
            right = shift_lanes(low, 2) - 8.0 * shift_lanes(low, 1)
        else:
            left = 16.0 * shift_lanes(high, -1) - shift_lanes(high, -2)
            right = 16.0 * shift_lanes(low, 1) - shift_lanes(low, 2)
        edge[n] = jnp.where(upper, right, left)


def after_ghosts(put, met, vol, fi, wi, part, edge, dt):
    at = lanes((CHUNK, COLS))
    border = (at < 2) | (at >= COLS - 2)
    for c in range(ROWS // CHUNK):
        rows = slice(c * CHUNK, (c + 1) * CHUNK)
        gax, gay, gbx, gby, iv, rw, cw = chunk_metrics(met, vol, c, dt)
        base = CHUNK + c * CHUNK
        for ch in range(5):
            di = slope(*(fi[ch, :, base + d : base + d + CHUNK, :] for d in (-2, -1, 1, 2)))
            total = part[ch, :, rows, :] - di * iv
            if ch > 0:
                si = curve(*(wi[ch - 1, :, base + d : base + d + CHUNK, :] for d in (-2, -1, 1, 2)))
                total = total + rw * si
            terms = []
            for k in range(PLANES):
                term = -(shift_lanes(edge[ch, rows, :], -4 * k - 2) * iv)
                if ch > 0:
                    term = term + cw * shift_lanes(edge[4 + ch, rows, :], -4 * k - 2)
                terms.append(jnp.where(border, term, 0.0))
            put(ch, rows, total + jnp.stack(terms, axis=0))


def pack(get, met, vol, strips, rows_out):
    at = lanes(STRIP) >> 2
    every = slice(0, ROWS)
    v = vol[0]
    acc = jnp.zeros(STRIP, jnp.float32)
    for q in range(32):
        x = get(q // 6, every, q % 6) if q < 30 else v * met[0, q - 28]
        acc = jnp.where(at == q, shift_lanes(x, 2 + 4 * q), acc)
    strips[0] = acc
    for r in range(ROWS):
        strips[1, ROWS - 1 - r : ROWS - r, :] = strips[0, r : r + 1, :]
    for n, r in enumerate((0, 1, ROWS - 2, ROWS - 1)):
        row = slice(r, r + 1)
        for q in range(32):
            x = get(q // 6, row, q % 6) if q < 30 else vol[0, row, :] * met[0, q - 30, row, :]
            rows_out[n, q : q + 1, :] = x


def peers_first(y, z, c, s):
    out = []
    for dz in range(Z):
        for m in range(2):
            blk = (y * Z + lax.rem(z + dz, Z)) * CORES + c
            out.append({"blk": blk, "ij": (IJ - 1 - s) if m else s})
    return out


def peers_second(y, z, c, s):
    out = []
    for dy in range(Y):
        for dc in range(2):
            blk = (lax.rem(y + dy, Y) * Z + z) * CORES + (1 - c if dc else c)
            out.append({"blk": blk, "ij": s})
    return out


def routes(placed, neighbour, face, orient, targets):
    ids = [placed[t["blk"]] for t in targets]
    wanted = [(b, f) for b in ids for f in range(2)]
    nids = [neighbour[b, f] for b, f in wanted]

    def find(p, found):
        held = placed[p]
        return tuple(jnp.where(n == held, p, a) for n, a in zip(nids, found))

    found = lax.fori_loop(0, BLOCKS, find, tuple(jnp.int32(0) for _ in nids))
    return [(q, face[b, f], orient[b, f]) for q, (b, f) in zip(found, wanted)]


def body(
    placed, neighbour, face, orient, dens, mom, ener, met, vol,
    out_d, out_m, out_e,
    sec, fi, wi, part, edge, strips, rows_out, rows_in, got, both, picked, got2a, got2b,
    send1, recv1, send2, recv2, send_r, recv_r,
):
    b, s = lax.axis_index("blk"), lax.axis_index("ij")
    c = lax.rem(b, CORES)
    z = lax.rem(b // CORES, Z)
    y = b // (CORES * Z)
    first, second = peers_first(y, z, c, s), peers_second(y, z, c, s)
    below = {"blk": b, "ij": lax.rem(s + IJ - 1, IJ)}
    above = {"blk": b, "ij": lax.rem(s + 1, IJ)}
    everyone = first[1:] + second[1:] + [below, above]
    barrier = pltpu.get_barrier_semaphore()
    for peer in everyone:
        pl.semaphore_signal(barrier, inc=1, device_id=peer, device_id_type=MESH)

    def get_input(ch, rows, plane=slice(None)):
        if ch == 0:
            return dens[0, plane, rows, :]
        if ch == 4:
            return ener[0, plane, rows, :]
        return mom[0, ch - 1, plane, rows, :]

    def get_section(ch, rows, plane=slice(None)):
        return sec[ch, plane, rows, :]

    def put_section(ch, rows, change):
        sec[ch, :, rows, :] = get_input(ch, rows) + change

    def put_result(ch, rows, change):
        value = 0.5 * (get_input(ch, rows) + get_section(ch, rows)) + change
        if ch == 0:
            out_d[0, :, rows, :] = value
        elif ch == 4:
            out_e[0, :, rows, :] = value
        else:
            out_m[0, ch - 1, :, rows, :] = value

    wall_sign = jnp.where(
        (lax.broadcasted_iota(jnp.int32, STRIP, 0) >= 6)
        & (lax.broadcasted_iota(jnp.int32, STRIP, 0) < 24),
        -1.0,
        1.0,
    )
    group = lanes(STRIP) & 3
    metric_sign = jnp.where(lanes(STRIP) >= 120, -1.0, 1.0)
    table = []

    for turn, (get, put, dt) in enumerate(
        ((get_input, put_section, time_step), (get_section, put_result, 0.5 * time_step))
    ):
        got2 = (got2a, got2b)[turn]
        pack(get, met, vol, strips.at[turn], rows_out.at[turn])
        if turn == 0:
            pl.semaphore_wait(barrier, len(everyone))
        hop1 = [
            pltpu.make_async_remote_copy(
                src_ref=strips.at[turn, k % 2],
                dst_ref=got.at[turn, k],
                send_sem=send1.at[turn, k],
                recv_sem=recv1.at[turn, k],
                device_id=first[k],
                device_id_type=MESH,
            )
            for k in range(1, 8)
        ]
        for copy in hop1:
            copy.start()
        slide = [
            pltpu.make_async_remote_copy(
                src_ref=rows_out.at[turn, pl.ds(2 * side, 2)],
                dst_ref=rows_in.at[turn, pl.ds(2 - 2 * side, 2)],
                send_sem=send_r.at[turn, side],
                recv_sem=recv_r.at[turn, side],
                device_id=(below, above)[side],
                device_id_type=MESH,
            )
            for side in range(2)
        ]
        for copy in slide:
            copy.start()
        if turn == 0:
            table.extend(routes(placed, neighbour, face, orient, second))
        before_ghosts(get, met, vol, fi, wi, part, dt)
        for k in range(8):
            if k > 0:
                hop1[k - 1].wait_recv()
                x = got[turn, k]
            else:
                x = strips[turn, 0]
            both[turn, k] = x
            flipped = jnp.where(group == 0, shift_lanes(x, -3), shift_lanes(x, -1))
            flipped = jnp.where(group == 2, shift_lanes(x, 1), flipped)
            flipped = jnp.where(group == 3, shift_lanes(x, 3), flipped)
            both[turn, 8 + k] = flipped * metric_sign
        hop2 = []
        for k in range(8):
            parts = []
            for f in range(2):
                q, g, o = table[2 * k + f]
                dz = lax.rem(z - lax.rem(q // CORES, Z) + Z, Z)
                parts.append(both[turn, jnp.where(g == f, 8, 0) + 2 * dz + o])
            message = jnp.where(group < 2, parts[0], parts[1])
            if k == 0:
                got2[0] = message
            else:
                picked[turn, k] = message
                copy = pltpu.make_async_remote_copy(
                    src_ref=picked.at[turn, k],
                    dst_ref=got2.at[k],
                    send_sem=send2.at[turn, k],
                    recv_sem=recv2.at[turn, k],
                    device_id=second[k],
                    device_id_type=MESH,
                )
                copy.start()
                hop2.append(copy)
        for copy in slide:
            copy.wait_recv()

        def get_halo(n):
            own = rows_out[turn, (1, 0, 3, 2)[n]]
            if n < 2:
                return jnp.where(s == 0, wall_sign * own, rows_in[turn, n])
            return jnp.where(s == IJ - 1, own, rows_in[turn, n])

        halo_rows(get_halo, fi, wi, dt)
        for copy in hop2:
            copy.wait_recv()
        sides = []
        for f in range(2):
            q, g, o = table[f]
            dy = lax.rem(y - q // (CORES * Z) + Y, Y)
            dc = jnp.where(lax.rem(q, CORES) == c, 0, 1)
            sides.append(got2[2 * dy + dc])
        ghost = jnp.where(group < 2, sides[0], sides[1])
        edge_terms(strips[turn, 0], ghost, edge, dt)
        after_ghosts(put, met, vol, fi, wi, part, edge, dt)
        for copy in hop1 + slide + hop2:
            copy.wait_send()


def local(density, momentum, energy, metrics, volume, placed, neighbour, face, orient):
    smem = pl.BlockSpec(memory_space=pltpu.SMEM)
    vmem = pl.BlockSpec(memory_space=pltpu.VMEM)
    f32 = jnp.float32
    dma = pltpu.SemaphoreType.DMA
    padded = ROWS + 2 * CHUNK
    return pl.pallas_call(
        body,
        out_shape=tuple(jax.ShapeDtypeStruct(x.shape, f32) for x in (density, momentum, energy)),
        in_specs=[smem] * 4 + [vmem] * 5,
        out_specs=(vmem, vmem, vmem),
        scratch_shapes=[
            pltpu.VMEM((5, PLANES, ROWS, COLS), f32),
            pltpu.VMEM((5, PLANES, padded, COLS), f32),
            pltpu.VMEM((4, PLANES, padded, COLS), f32),
            pltpu.VMEM((5, PLANES, ROWS, COLS), f32),
            pltpu.VMEM((9, ROWS, COLS), f32),
            pltpu.VMEM((2, 2, ROWS, COLS), f32),
            pltpu.VMEM((2, 4, ROWS, COLS), f32),
            pltpu.VMEM((2, 4, ROWS, COLS), f32),
            pltpu.VMEM((2, 8, ROWS, COLS), f32),
            pltpu.VMEM((2, 16, ROWS, COLS), f32),
            pltpu.VMEM((2, 8, ROWS, COLS), f32),
            pltpu.VMEM((8, ROWS, COLS), f32),
            pltpu.VMEM((8, ROWS, COLS), f32),
            dma((2, 8)), dma((2, 8)), dma((2, 8)), dma((2, 8)), dma((2, 2)), dma((2, 2)),
        ],
        compiler_params=pltpu.CompilerParams(
            collective_id=0, has_side_effects=True, vmem_limit_bytes=32 << 20
        ),
    )(placed, neighbour, face, orient, density, momentum, energy, metrics, volume)


def solution(mesh):
    return jax.shard_map(
        local,
        mesh=mesh,
        in_specs=(
            P("blk", None, "ij", None),
            P("blk", None, None, "ij", None),
            P("blk", None, "ij", None),
            P("blk", None, "ij", None),
            P("blk", "ij", None),
            P(),
            P(),
            P(),
            P(),
        ),
        out_specs=(
            P("blk", None, "ij", None),
            P("blk", None, None, "ij", None),
            P("blk", None, "ij", None),
        ),
        check_vma=False,
    )
```

```python
import functools

import jax
import jax.numpy as jnp
from jax import lax
from jax.experimental import pallas as pl
from jax.experimental.pallas import tpu as pltpu
from jax.sharding import PartitionSpec as P

MESH = pl.DeviceIdType.MESH
pressure_factor = 0.4
viscosity = 0.05
conduction = 0.1
time_step = 0.03
ROWS, COLS, PLANES, CHUNK = 32, 128, 6, 8
Y, Z, CORES, IJ, BLOCKS = 4, 4, 2, 8, 32
STRIP = (ROWS, COLS)


def lanes(shape):
    return lax.broadcasted_iota(jnp.int32, shape, len(shape) - 1)


def shift_lanes(x, by):
    by = by % COLS
    return x if by == 0 else pltpu.roll(x, by, x.ndim - 1)


def primitives(rho, m1, m2, m3, energy, dt):
    inv = 1.0 / rho
    u1, u2, u3 = m1 * inv, m2 * inv, m3 * inv
    kinetic = 0.5 * (m1 * u1 + m2 * u2 + m3 * u3)
    p = pressure_factor * (energy - kinetic)
    head = energy + p
    soft = dt * viscosity / 12.0
    warm = dt * conduction / 12.0
    curved = (soft * u1, soft * u2, soft * u3, inv * (soft * kinetic + warm * p))
    return u1, u2, u3, p, head, curved


def flux(rho, m1, m2, m3, prim, gx, gy):
    u1, u2, u3, p, head, _ = prim
    speed = gx * u1 + gy * u2
    return (rho * speed, m1 * speed + gx * p, m2 * speed + gy * p, m3 * speed, head * speed)


def slope(b2, b1, a1, a2):
    return 8.0 * (a1 - b1) - (a2 - b2)


def curve(b2, b1, a1, a2):
    return 16.0 * (a1 + b1) - (a2 + b2)


def plane_shift(f, by):
    by = by % PLANES
    return jnp.concatenate([f[by:], f[:by]], axis=0)


def chunk_metrics(met, vol, c, dt):
    rows = slice(c * CHUNK, (c + 1) * CHUNK)
    ax, ay, bx, by = (met[0, n, rows, :] for n in range(4))
    v = vol[0, rows, :]
    return (v * ax, v * ay, v * bx, v * by, (dt / 12.0) / v, ax * ax + ay * ay, bx * bx + by * by)


def before_ghosts(get, met, vol, fi, wi, part, dt):
    for c in range(ROWS // CHUNK):
        rows = slice(c * CHUNK, (c + 1) * CHUNK)
        gax, gay, gbx, gby, iv, rw, cw = chunk_metrics(met, vol, c, dt)
        center = -30.0 * (rw + cw + 1.0)
        rho, m1, m2, m3, energy = (get(ch, rows) for ch in range(5))
        prim = primitives(rho, m1, m2, m3, energy, dt)
        u1, u2, u3, p, head, curved = prim
        inner = slice(CHUNK + c * CHUNK, 2 * CHUNK + c * CHUNK)
        for ch, f in enumerate(flux(rho, m1, m2, m3, prim, gax, gay)):
            fi[ch, :, inner, :] = f
        for n, w in enumerate(curved):
            wi[n, :, inner, :] = w
        fj = flux(rho, m1, m2, m3, prim, gbx, gby)
        fk = (m3, m1 * u3, m2 * u3, m3 * u3 + p, head * u3)
        for ch in range(5):
            f, g = fj[ch], fk[ch]
            dj = slope(*(shift_lanes(f, by) for by in (2, 1, -1, -2)))
            dk = slope(*(plane_shift(g, by) for by in (-2, -1, 1, 2)))
            total = -(dj * iv) - (dt / 12.0) * dk
            if ch > 0:
                w = curved[ch - 1]
                sj = curve(*(shift_lanes(w, by) for by in (2, 1, -1, -2)))
                sk = curve(*(plane_shift(w, by) for by in (-2, -1, 1, 2)))
                total = total + cw * sj + sk + center * w
            part[ch, :, rows, :] = total


def halo_rows(get_halo, fi, wi, dt):
    for n in range(4):
        at = (CHUNK - 2, CHUNK - 1, CHUNK + ROWS, CHUNK + ROWS + 1)[n]
        block = get_halo(n)
        rho, m1, m2, m3, energy = (block[6 * ch : 6 * ch + 6, :] for ch in range(5))
        gax, gay = block[30:31, :], block[31:32, :]
        prim = primitives(rho, m1, m2, m3, energy, dt)
        for ch, f in enumerate(flux(rho, m1, m2, m3, prim, gax, gay)):
            for k in range(PLANES):
                fi[ch, k, at : at + 1, :] = f[k : k + 1, :]
        for m, w in enumerate(prim[5]):
            for k in range(PLANES):
                wi[m, k, at : at + 1, :] = w[k : k + 1, :]


def spread(x):
    x = jnp.where(lanes(x.shape) < 4, x, 0.0)
    pair = x + shift_lanes(x, 4)
    return pair + shift_lanes(pair, 8) + shift_lanes(pair, 16)


def edge_values(strip, dt):
    rho, m1, m2, m3, energy = (shift_lanes(strip, -24 * ch) for ch in range(5))
    gbx, gby = spread(shift_lanes(strip, -120)), spread(shift_lanes(strip, -124))
    prim = primitives(rho, m1, m2, m3, energy, dt)
    return flux(rho, m1, m2, m3, prim, gbx, gby) + prim[5]


def edge_terms(own, ghost, edge, dt):
    upper = (lanes(STRIP) & 3) >= 2
    mine, theirs = edge_values(own, dt), edge_values(ghost, dt)
    for n in range(9):
        h = theirs[n] - mine[n]
        high, low = jnp.where(upper, h, 0.0), jnp.where(upper, 0.0, h)
        if n < 5:
            left = 8.0 * shift_lanes(high, -1) - shift_lanes(high, -2)
            right = shift_lanes(low, 2) - 8.0 * shift_lanes(low, 1)
        else:
            left = 16.0 * shift_lanes(high, -1) - shift_lanes(high, -2)
            right = 16.0 * shift_lanes(low, 1) - shift_lanes(low, 2)
        edge[n] = jnp.where(upper, right, left)


def after_ghosts(put, met, vol, fi, wi, part, edge, dt):
    at = lanes((CHUNK, COLS))
    border = (at < 2) | (at >= COLS - 2)
    for c in range(ROWS // CHUNK):
        rows = slice(c * CHUNK, (c + 1) * CHUNK)
        gax, gay, gbx, gby, iv, rw, cw = chunk_metrics(met, vol, c, dt)
        base = CHUNK + c * CHUNK
        for ch in range(5):
            di = slope(*(fi[ch, :, base + d : base + d + CHUNK, :] for d in (-2, -1, 1, 2)))
            total = part[ch, :, rows, :] - di * iv
            if ch > 0:
                si = curve(*(wi[ch - 1, :, base + d : base + d + CHUNK, :] for d in (-2, -1, 1, 2)))
                total = total + rw * si
            terms = []
            for k in range(PLANES):
                term = -(shift_lanes(edge[ch, rows, :], -4 * k - 2) * iv)
                if ch > 0:
                    term = term + cw * shift_lanes(edge[4 + ch, rows, :], -4 * k - 2)
                terms.append(jnp.where(border, term, 0.0))
            put(ch, rows, total + jnp.stack(terms, axis=0))


def pack(get, met, vol, strips, rows_out):
    at = lanes(STRIP) >> 2
    every = slice(0, ROWS)
    v = vol[0]
    acc = jnp.zeros(STRIP, jnp.float32)
    for q in range(32):
        x = get(q // 6, every, q % 6) if q < 30 else v * met[0, q - 28]
        acc = jnp.where(at == q, shift_lanes(x, 2 + 4 * q), acc)
    strips[0] = acc
    for r in range(ROWS):
        strips[1, ROWS - 1 - r : ROWS - r, :] = strips[0, r : r + 1, :]
    for n, r in enumerate((0, 1, ROWS - 2, ROWS - 1)):
        row = slice(r, r + 1)
        for q in range(32):
            x = get(q // 6, row, q % 6) if q < 30 else vol[0, row, :] * met[0, q - 30, row, :]
            rows_out[n, q : q + 1, :] = x


def peers_first(y, z, c, s):
    out = []
    for dz in range(Z):
        for m in range(2):
            blk = (y * Z + lax.rem(z + dz, Z)) * CORES + c
            out.append({"blk": blk, "ij": (IJ - 1 - s) if m else s})
    return out


def peers_second(y, z, c, s):
    out = []
    for dy in range(Y):
        for dc in range(2):
            blk = (lax.rem(y + dy, Y) * Z + z) * CORES + (1 - c if dc else c)
            out.append({"blk": blk, "ij": s})
    return out


def routes(placed, neighbour, face, orient, targets):
    ids = [placed[t["blk"]] for t in targets]
    wanted = [(b, f) for b in ids for f in range(2)]
    nids = [neighbour[f, b] for b, f in wanted]

    def find(p, found):
        held = placed[p]
        return tuple(jnp.where(n == held, p, a) for n, a in zip(nids, found))

    found = lax.fori_loop(0, BLOCKS, find, tuple(jnp.int32(0) for _ in nids))
    return [(q, face[f, b], orient[f, b]) for q, (b, f) in zip(found, wanted)]


def body(
    placed_hbm, neighbour_hbm, face_hbm, orient_hbm, dens_hbm, mom_hbm, ener_hbm, met_hbm, vol_hbm,
    out_d, out_m, out_e,
    placed, neighbour, face, orient, dens, mom, ener, met, vol, load,
    sec, fi, wi, part, edge, strips, rows_out, rows_in, got, both, picked, got2a, got2b,
    send1, recv1, send2, recv2, send_r, recv_r,
):
    fetch = [
        pltpu.make_async_copy(src, dst, load.at[n])
        for n, (src, dst) in enumerate(
            (
                (mom_hbm, mom), (dens_hbm, dens), (ener_hbm, ener), (met_hbm, met), (vol_hbm, vol),
                (placed_hbm, placed), (neighbour_hbm, neighbour), (face_hbm, face), (orient_hbm, orient),
            )
        )
    ]
    for copy in fetch:
        copy.start()
    b, s = lax.axis_index("blk"), lax.axis_index("ij")
    c = lax.rem(b, CORES)
    z = lax.rem(b // CORES, Z)
    y = b // (CORES * Z)
    first, second = peers_first(y, z, c, s), peers_second(y, z, c, s)
    below = {"blk": b, "ij": lax.rem(s + IJ - 1, IJ)}
    above = {"blk": b, "ij": lax.rem(s + 1, IJ)}
    everyone = first[1:] + second[1:] + [below, above]
    barrier = pltpu.get_barrier_semaphore()
    for peer in everyone:
        pl.semaphore_signal(barrier, inc=1, device_id=peer, device_id_type=MESH)

    for copy in fetch:
        copy.wait()

    def get_input(ch, rows, plane=slice(None)):
        if ch == 0:
            return dens[0, plane, rows, :]
        if ch == 4:
            return ener[0, plane, rows, :]
        return mom[0, ch - 1, plane, rows, :]

    def get_section(ch, rows, plane=slice(None)):
        return sec[ch, plane, rows, :]

    def put_section(ch, rows, change):
        sec[ch, :, rows, :] = get_input(ch, rows) + change

    def put_result(ch, rows, change):
        value = 0.5 * (get_input(ch, rows) + get_section(ch, rows)) + change
        if ch == 0:
            out_d[0, :, rows, :] = value
        elif ch == 4:
            out_e[0, :, rows, :] = value
        else:
            out_m[0, ch - 1, :, rows, :] = value

    wall_sign = jnp.where(
        (lax.broadcasted_iota(jnp.int32, STRIP, 0) >= 6)
        & (lax.broadcasted_iota(jnp.int32, STRIP, 0) < 24),
        -1.0,
        1.0,
    )
    group = lanes(STRIP) & 3
    metric_sign = jnp.where(lanes(STRIP) >= 120, -1.0, 1.0)
    table = []

    for turn, (get, put, dt) in enumerate(
        ((get_input, put_section, time_step), (get_section, put_result, 0.5 * time_step))
    ):
        got2 = (got2a, got2b)[turn]
        pack(get, met, vol, strips.at[turn], rows_out.at[turn])
        if turn == 0:
            pl.semaphore_wait(barrier, len(everyone))
        hop1 = [
            pltpu.make_async_remote_copy(
                src_ref=strips.at[turn, k % 2],
                dst_ref=got.at[turn, k],
                send_sem=send1.at[turn, k],
                recv_sem=recv1.at[turn, k],
                device_id=first[k],
                device_id_type=MESH,
            )
            for k in range(1, 8)
        ]
        for copy in hop1:
            copy.start()
        slide = [
            pltpu.make_async_remote_copy(
                src_ref=rows_out.at[turn, pl.ds(2 * side, 2)],
                dst_ref=rows_in.at[turn, pl.ds(2 - 2 * side, 2)],
                send_sem=send_r.at[turn, side],
                recv_sem=recv_r.at[turn, side],
                device_id=(below, above)[side],
                device_id_type=MESH,
            )
            for side in range(2)
        ]
        for copy in slide:
            copy.start()
        if turn == 0:
            table.extend(routes(placed, neighbour, face, orient, second))
        before_ghosts(get, met, vol, fi, wi, part, dt)
        for k in range(8):
            if k > 0:
                hop1[k - 1].wait_recv()
                x = got[turn, k]
            else:
                x = strips[turn, 0]
            both[turn, k] = x
            flipped = jnp.where(group == 0, shift_lanes(x, -3), shift_lanes(x, -1))
            flipped = jnp.where(group == 2, shift_lanes(x, 1), flipped)
            flipped = jnp.where(group == 3, shift_lanes(x, 3), flipped)
            both[turn, 8 + k] = flipped * metric_sign
        hop2 = []
        for k in range(8):
            parts = []
            for f in range(2):
                q, g, o = table[2 * k + f]
                dz = lax.rem(z - lax.rem(q // CORES, Z) + Z, Z)
                parts.append(both[turn, jnp.where(g == f, 8, 0) + 2 * dz + o])
            message = jnp.where(group < 2, parts[0], parts[1])
            if k == 0:
                got2[0] = message
            else:
                picked[turn, k] = message
                copy = pltpu.make_async_remote_copy(
                    src_ref=picked.at[turn, k],
                    dst_ref=got2.at[k],
                    send_sem=send2.at[turn, k],
                    recv_sem=recv2.at[turn, k],
                    device_id=second[k],
                    device_id_type=MESH,
                )
                copy.start()
                hop2.append(copy)
        for copy in slide:
            copy.wait_recv()

        def get_halo(n):
            own = rows_out[turn, (1, 0, 3, 2)[n]]
            if n < 2:
                return jnp.where(s == 0, wall_sign * own, rows_in[turn, n])
            return jnp.where(s == IJ - 1, own, rows_in[turn, n])

        halo_rows(get_halo, fi, wi, dt)
        for copy in hop2:
            copy.wait_recv()
        sides = []
        for f in range(2):
            q, g, o = table[f]
            dy = lax.rem(y - q // (CORES * Z) + Y, Y)
            dc = jnp.where(lax.rem(q, CORES) == c, 0, 1)
            sides.append(got2[2 * dy + dc])
        ghost = jnp.where(group < 2, sides[0], sides[1])
        edge_terms(strips[turn, 0], ghost, edge, dt)
        after_ghosts(put, met, vol, fi, wi, part, edge, dt)
        for copy in hop1 + slide + hop2:
            copy.wait_send()


def hand_over(d, m, e, out_d, out_m, out_e, sems):
    copies = [
        pltpu.make_async_copy(src, dst, sems.at[n])
        for n, (src, dst) in enumerate(((m, out_m), (d, out_d), (e, out_e)))
    ]
    for copy in copies:
        copy.start()
    for copy in copies:
        copy.wait()


def local(density, momentum, energy, metrics, volume, placed, neighbour, face, orient):
    smem, vmem, i32, f32 = pltpu.SMEM, pltpu.VMEM, jnp.int32, jnp.float32
    anywhere = pl.BlockSpec(memory_space=pltpu.HBM)
    inside = pl.BlockSpec(memory_space=pltpu.VMEM)
    dma = pltpu.SemaphoreType.DMA
    padded = ROWS + 2 * CHUNK
    shapes = tuple(jax.ShapeDtypeStruct(x.shape, f32) for x in (density, momentum, energy))
    results = pl.pallas_call(
        body,
        out_shape=shapes,
        in_specs=[anywhere] * 9,
        out_specs=(inside,) * 3,
        scratch_shapes=[
            smem((BLOCKS,), i32), smem((2, BLOCKS), i32), smem((2, BLOCKS), i32), smem((2, BLOCKS), i32),
            vmem(density.shape, f32), vmem(momentum.shape, f32), vmem(energy.shape, f32),
            vmem(metrics.shape, f32), vmem(volume.shape, f32), dma((9,)),
            vmem((5, PLANES, ROWS, COLS), f32),
            vmem((5, PLANES, padded, COLS), f32),
            vmem((4, PLANES, padded, COLS), f32),
            vmem((5, PLANES, ROWS, COLS), f32),
            vmem((9, ROWS, COLS), f32),
            vmem((2, 2, ROWS, COLS), f32),
            vmem((2, 4, ROWS, COLS), f32),
            vmem((2, 4, ROWS, COLS), f32),
            vmem((2, 8, ROWS, COLS), f32),
            vmem((2, 16, ROWS, COLS), f32),
            vmem((2, 8, ROWS, COLS), f32),
            vmem((8, ROWS, COLS), f32),
            vmem((8, ROWS, COLS), f32),
            dma((2, 8)), dma((2, 8)), dma((2, 8)), dma((2, 8)), dma((2, 2)), dma((2, 2)),
        ],
        compiler_params=pltpu.CompilerParams(
            collective_id=0, has_side_effects=True, vmem_limit_bytes=48 << 20
        ),
    )(
        *(
            pltpu.with_memory_space_constraint(x, pltpu.HBM)
            for x in (placed, neighbour.T, face.T, orient.T, density, momentum, energy, metrics, volume)
        )
    )
    return pl.pallas_call(
        hand_over,
        out_shape=shapes,
        in_specs=[inside] * 3,
        out_specs=(anywhere,) * 3,
        scratch_shapes=[dma((3,))],
    )(*(pltpu.with_memory_space_constraint(x, pltpu.VMEM) for x in results))


def solution(mesh):
    return jax.shard_map(
        local,
        mesh=mesh,
        in_specs=(
            P("blk", None, "ij", None),
            P("blk", None, None, "ij", None),
            P("blk", None, "ij", None),
            P("blk", None, "ij", None),
            P("blk", "ij", None),
            P(),
            P(),
            P(),
            P(),
        ),
        out_specs=(
            P("blk", None, "ij", None),
            P("blk", None, None, "ij", None),
            P("blk", None, "ij", None),
        ),
        check_vma=False,
    )
```

```python
import functools

import jax
import jax.numpy as jnp
from jax import lax
from jax.experimental import pallas as pl
from jax.experimental.pallas import tpu as pltpu
from jax.sharding import PartitionSpec as P

MESH = pl.DeviceIdType.MESH
pressure_factor = 0.4
viscosity = 0.05
conduction = 0.1
time_step = 0.03
ROWS, COLS, PLANES, CHUNK = 32, 128, 6, 8
Y, Z, CORES, IJ, BLOCKS = 4, 4, 2, 8, 32
LOW, HIGH = slice(6, 8), slice(40, 42)


def lanes(shape):
    return lax.broadcasted_iota(jnp.int32, shape, len(shape) - 1)


def rows_of(shape):
    return lax.broadcasted_iota(jnp.int32, shape, len(shape) - 2)


def shift_lanes(x, by):
    by = by % COLS
    return x if by == 0 else pltpu.roll(x, by, x.ndim - 1)


def primitives(rho, m1, m2, m3, energy, dt):
    inv = 1.0 / rho
    u1, u2, u3 = m1 * inv, m2 * inv, m3 * inv
    kinetic = 0.5 * (m1 * u1 + m2 * u2 + m3 * u3)
    p = pressure_factor * (energy - kinetic)
    head = energy + p
    soft = dt * viscosity / 12.0
    warm = dt * conduction / 12.0
    curved = (soft * u1, soft * u2, soft * u3, inv * (soft * kinetic + warm * p))
    return u1, u2, u3, p, head, curved


def flux(rho, m1, m2, m3, prim, gx, gy):
    u1, u2, u3, p, head, _ = prim
    speed = gx * u1 + gy * u2
    return (rho * speed, m1 * speed + gx * p, m2 * speed + gy * p, m3 * speed, head * speed)


def flux_planes(m1, m2, m3, prim):
    u1, u2, u3, p, head, _ = prim
    return (m3, m1 * u3, m2 * u3, m3 * u3 + p, head * u3)


def slope(b2, b1, a1, a2):
    return 8.0 * (a1 - b1) - (a2 - b2)


def curve(b2, b1, a1, a2):
    return 16.0 * (a1 + b1) - (a2 + b2)


def plane_shift(f, by):
    by = by % PLANES
    return jnp.concatenate([f[by:], f[:by]], axis=0)


def span(c):
    return slice(CHUNK + c * CHUNK, 2 * CHUNK + c * CHUNK)


def chunk_metrics(exm, c, dt):
    ax, ay, bx, by, v = (exm[n, span(c), :] for n in range(5))
    return (v * ax, v * ay, v * bx, v * by, (dt / 12.0) / v, ax * ax + ay * ay, bx * bx + by * by)


def before_ghosts(state, exm, fi, wi, part, dt, chunks):
    for c in chunks:
        gax, gay, gbx, gby, iv, rw, cw = chunk_metrics(exm, c, dt)
        center = -30.0 * (rw + cw + 1.0)
        rho, m1, m2, m3, energy = (state[ch, :, span(c), :] for ch in range(5))
        prim = primitives(rho, m1, m2, m3, energy, dt)
        curved = prim[5]
        inner = span(c + 1)
        for ch, f in enumerate(flux(rho, m1, m2, m3, prim, gax, gay)):
            fi[ch, :, inner, :] = f
        for n, w in enumerate(curved):
            wi[n, :, inner, :] = w
        fj = flux(rho, m1, m2, m3, prim, gbx, gby)
        fk = flux_planes(m1, m2, m3, prim)
        for ch in range(5):
            f, g = fj[ch], fk[ch]
            dj = slope(*(shift_lanes(f, by) for by in (2, 1, -1, -2)))
            dk = slope(*(plane_shift(g, by) for by in (-2, -1, 1, 2)))
            total = -(dj * iv) - (dt / 12.0) * dk
            if ch > 0:
                w = curved[ch - 1]
                sj = curve(*(shift_lanes(w, by) for by in (2, 1, -1, -2)))
                sk = curve(*(plane_shift(w, by) for by in (-2, -1, 1, 2)))
                total = total + cw * sj + sk + center * w
            part[ch, :, span(c), :] = total


def row_terms(exm, fi, wi, part, c, ch, dt):
    gax, gay, gbx, gby, iv, rw, cw = chunk_metrics(exm, c, dt)
    base = 2 * CHUNK + c * CHUNK
    di = slope(*(fi[ch, :, base + d : base + d + CHUNK, :] for d in (-2, -1, 1, 2)))
    total = part[ch, :, span(c), :] - di * iv
    if ch > 0:
        si = curve(*(wi[ch - 1, :, base + d : base + d + CHUNK, :] for d in (-2, -1, 1, 2)))
        total = total + rw * si
    return total


def edge_columns(edge, exm, c, ch, dt):
    at = lanes((CHUNK, COLS))
    border = (at < 2) | (at >= COLS - 2)
    gax, gay, gbx, gby, iv, rw, cw = chunk_metrics(exm, c, dt)
    terms = []
    for k in range(PLANES):
        term = -(shift_lanes(edge[ch, span(c), :], -8 * k - 4) * iv)
        if ch > 0:
            term = term + cw * shift_lanes(edge[4 + ch, span(c), :], -8 * k - 4)
        terms.append(jnp.where(border, term, 0.0))
    return jnp.stack(terms, axis=0)


def apart(a, b):
    third = jnp.where(lanes(a.shape) < 32, shift_lanes(a, -96), shift_lanes(b, 32))
    return [a, shift_lanes(a, -48), third, shift_lanes(b, -16), shift_lanes(b, -64)]


def spread(x):
    x = jnp.where((lanes(x.shape) & 63) < 8, x, 0.0)
    pair = x + shift_lanes(x, 8)
    return pair + shift_lanes(pair, 16) + shift_lanes(pair, 32)


def lines(own, ghost):
    near = (lanes(own.shape) & 7) < 4
    first = jnp.where(near, ghost, own)
    second = jnp.where(near, own, ghost)
    return jnp.where(lanes(own.shape) < 64, first, shift_lanes(second, 64))


def line_planes(x, by):
    m = lanes(x.shape) & 63
    if by > 0:
        return jnp.where(m < 48 - 8 * by, shift_lanes(x, -8 * by), shift_lanes(x, 48 - 8 * by))
    return jnp.where(m >= -8 * by, shift_lanes(x, -8 * by), shift_lanes(x, -48 - 8 * by))


def edge_terms(mine, theirs):
    upper = (lanes(mine[0].shape) & 7) >= 4
    out = []
    for n in range(9):
        h = theirs[n] - mine[n]
        high, low = jnp.where(upper, h, 0.0), jnp.where(upper, 0.0, h)
        if n < 5:
            left = 8.0 * shift_lanes(high, -1) - shift_lanes(high, -2)
            right = shift_lanes(low, 2) - 8.0 * shift_lanes(low, 1)
        else:
            left = 16.0 * shift_lanes(high, -1) - shift_lanes(high, -2)
            right = 16.0 * shift_lanes(low, 1) - shift_lanes(low, 2)
        out.append(jnp.where(upper, right, left))
    return out


def edge_values(fields, gx, gy, dt):
    rho, m1, m2, m3, energy = fields
    prim = primitives(rho, m1, m2, m3, energy, dt)
    return flux(rho, m1, m2, m3, prim, gx, gy) + prim[5]


def column_metric(c, e):
    return jnp.concatenate([shift_lanes(c, -32 * g - 8 * e) for g in range(4)], axis=0)


def line_section(own, ghost, lf, own_edge, ghost_edge, edge, dt):
    a, b, c = slice(0, 32), slice(32, 64), slice(64, 72)
    ob, gb = own[b, :], ghost[b, :]
    fields = [lines(o, g) for o, g in zip(apart(own[a, :], ob), apart(ghost[a, :], gb))]
    gbx, gby = (spread(lines(shift_lanes(ob, -n), shift_lanes(gb, -n))) for n in (112, 120))
    oc, gc = own[c, :], ghost[c, :]
    gax, gay, v = (spread(lines(column_metric(oc, e), column_metric(gc, e))) for e in range(3))
    rho, m1, m2, m3, energy = fields
    prim = primitives(rho, m1, m2, m3, energy, dt)
    curved = prim[5]
    for n, f in enumerate(flux(rho, m1, m2, m3, prim, gax, gay) + curved):
        lf[n, span(0).start : span(3).stop, :] = f
    h = (slice(72, 76), slice(76, 80), slice(80, 84))
    oa, ob, od = (own[n, :] for n in h)
    ga, gb, gd = (ghost[n, :] for n in h)
    mine, theirs = apart(oa, ob), apart(ga, gb)
    hax, hay = (spread(lines(shift_lanes(od, -n), shift_lanes(gd, -n))) for n in (0, 8))
    ends = [lines(o, g) for o, g in zip(mine, theirs)]
    end_prim = primitives(*ends, dt)
    for n, f in enumerate(flux(*ends[:4], end_prim, hax, hay) + end_prim[5]):
        lf[n, LOW, :] = f[0:2]
        lf[n, HIGH, :] = f[2:4]
    ends = edge_terms(
        edge_values(mine, *(spread(shift_lanes(ob, -n)) for n in (112, 120)), dt),
        edge_values(theirs, *(spread(shift_lanes(gb, -n)) for n in (112, 120)), dt),
    )
    for n, f in enumerate(ends):
        edge[n, LOW, :] = f[0:2]
        edge[n, HIGH, :] = f[2:4]
    inv = 1.0 / v
    iv = (dt / 12.0) * inv
    rw = (gax * gax + gay * gay) * (inv * inv)
    cw = (gbx * gbx + gby * gby) * (inv * inv)
    center = -30.0 * (rw + cw + 1.0)
    fj = flux(rho, m1, m2, m3, prim, gbx, gby)
    fk = flux_planes(m1, m2, m3, prim)
    near = (lanes((ROWS, COLS)) & 7) < 4
    for ch in range(7):
        if ch < 5:
            di = slope(*(lf[ch, CHUNK + d : CHUNK + d + ROWS, :] for d in (-2, -1, 1, 2)))
            dj = slope(*(shift_lanes(fj[ch], by) for by in (2, 1, -1, -2)))
            dk = slope(*(line_planes(fk[ch], by) for by in (-2, -1, 1, 2)))
            value = fields[ch] - (di + dj) * iv - (dt / 12.0) * dk
            if ch > 0:
                w = curved[ch - 1]
                si = curve(*(lf[4 + ch, CHUNK + d : CHUNK + d + ROWS, :] for d in (-2, -1, 1, 2)))
                sj = curve(*(shift_lanes(w, by) for by in (2, 1, -1, -2)))
                sk = curve(*(line_planes(w, by) for by in (-2, -1, 1, 2)))
                value = value + rw * si + cw * sj + sk + center * w
        else:
            value = (gbx, gby)[ch - 5]
        other = shift_lanes(value, 64)
        own_edge[ch] = jnp.where(near, other, value)
        ghost_edge[ch] = jnp.where(near, value, other)


def pack(ex, exm, strips, relay):
    at = lanes((ROWS, COLS)) >> 3
    inside = slice(CHUNK, CHUNK + ROWS)
    v = exm[4, inside, :]
    for half in range(2):
        acc = jnp.zeros((ROWS, COLS), jnp.float32)
        for n in range(16):
            q = 16 * half + n
            x = ex[q // 6, q % 6, inside, :] if q < 30 else v * exm[q - 28, inside, :]
            acc = jnp.where(at == n, shift_lanes(x, 4 + 8 * n), acc)
        strips[0, 32 * half : 32 * half + 32, :] = acc
    slot = lanes((CHUNK, COLS)) >> 3
    acc = jnp.zeros((CHUNK, COLS), jnp.float32)
    for g in range(4):
        part = exm[4, span(g), :]
        for e in range(3):
            x = part * exm[e, span(g), :] if e < 2 else part
            acc = jnp.where(slot == 4 * g + e, shift_lanes(x, 4 + 32 * g + 8 * e), acc)
    strips[0, 64:72, :] = acc
    for r in range(ROWS):
        for half in (0, 32):
            strips[1, half + 31 - r : half + 32 - r, :] = strips[0, half + r : half + r + 1, :]
    turned = jnp.where((lanes(acc.shape) & 32) == 0, shift_lanes(acc, 32), shift_lanes(acc, -32))
    turned = jnp.where((lanes(acc.shape) & 31) < 16, -turned, turned)
    for r in range(CHUNK):
        strips[1, 71 - r : 72 - r, :] = turned[r : r + 1, :]
    for side, r in ((0, 0), (1, ROWS - 2)):
        relay[side, 0:2, :] = strips[0, r : r + 2, :]
        relay[side, 2:4, :] = strips[0, 32 + r : 34 + r, :]
        relay[side, 4:6, :] = shift_lanes(acc[r % CHUNK : r % CHUNK + 2], -32 * (r // CHUNK))
        relay[side, 6:8, :] = jnp.zeros((2, COLS), jnp.float32)


def pack_ends(relay, arrived, strips, at_start, at_end):
    turn = lanes((1, COLS))
    signs = (
        jnp.where(turn >= 48, -1.0, 1.0),
        jnp.where(turn < 64, -1.0, 1.0),
        jnp.ones((1, COLS), jnp.float32),
    )
    for n in range(3):
        base = 72 + 4 * n
        for r in range(4):
            near = 2 * n + r % 2
            wall = 2 * n + 1 - r % 2
            side = r // 2
            mirror = relay[side, wall : wall + 1, :]
            if side == 0:
                row = jnp.where(at_start, signs[n] * mirror, arrived[side, near : near + 1, :])
            else:
                row = jnp.where(at_end, mirror, arrived[side, near : near + 1, :])
            strips[0, base + r : base + r + 1, :] = row
            strips[1, base + 3 - r : base + 4 - r, :] = -row if n == 2 else row
    for m in range(2):
        strips[m, 84:88, :] = jnp.zeros((4, COLS), jnp.float32)


def walls(state, at_start, at_end):
    for ch in range(5):
        sign = -1.0 if 1 <= ch <= 3 else 1.0
        for r in range(2):
            low, high = slice(7 - r, 8 - r), slice(40 + r, 41 + r)
            mirror = state[ch, :, 8 + r : 9 + r, :]
            state[ch, :, low, :] = jnp.where(at_start, sign * mirror, state[ch, :, low, :])
            mirror = state[ch, :, 39 - r : 40 - r, :]
            state[ch, :, high, :] = jnp.where(at_end, mirror, state[ch, :, high, :])


def metric_walls(exm, at_start, at_end):
    for r in range(2):
        low, high = slice(7 - r, 8 - r), slice(40 + r, 41 + r)
        exm[:, low, :] = jnp.where(at_start, exm[:, 8 + r : 9 + r, :], exm[:, low, :])
        exm[:, high, :] = jnp.where(at_end, exm[:, 39 - r : 40 - r, :], exm[:, high, :])


def halo_rows(state, exm, fi, wi, dt):
    for rows in (LOW, HIGH):
        rho, m1, m2, m3, energy = (state[ch, :, rows, :] for ch in range(5))
        v = exm[4, rows, :]
        prim = primitives(rho, m1, m2, m3, energy, dt)
        target = slice(rows.start + CHUNK, rows.stop + CHUNK)
        for ch, f in enumerate(flux(rho, m1, m2, m3, prim, v * exm[0, rows, :], v * exm[1, rows, :])):
            fi[ch, :, target, :] = f
        for n, w in enumerate(prim[5]):
            wi[n, :, target, :] = w


def flip(x):
    t = lanes(x.shape) & 7
    for d in (4, 2, 1):
        x = jnp.where((t & d) == 0, shift_lanes(x, -d), shift_lanes(x, d))
    return x


def peers_first(y, z, c, s):
    out = []
    for dz in range(Z):
        for m in range(2):
            blk = (y * Z + lax.rem(z + dz, Z)) * CORES + c
            out.append({"blk": blk, "ij": (IJ - 1 - s) if m else s})
    return out


def peers_second(y, z, c, s):
    out = []
    for dy in range(Y):
        for dc in range(2):
            blk = (lax.rem(y + dy, Y) * Z + z) * CORES + (1 - c if dc else c)
            out.append({"blk": blk, "ij": s})
    return out


def routes(placed, neighbour, face, orient, targets):
    ids = [placed[t["blk"]] for t in targets]
    wanted = [(b, f) for b in ids for f in range(2)]
    nids = [neighbour[f, b] for b, f in wanted]

    def find(p, found):
        held = placed[p]
        return tuple(jnp.where(n == held, p, a) for n, a in zip(nids, found))

    found = lax.fori_loop(0, BLOCKS, find, tuple(jnp.int32(0) for _ in nids))
    return [(q, face[f, b], orient[f, b]) for q, (b, f) in zip(found, wanted)]


def body(
    placed_hbm, neighbour_hbm, face_hbm, orient_hbm, dens_hbm, mom_hbm, ener_hbm, met_hbm, vol_hbm,
    out_d, out_m, out_e,
    placed, neighbour, face, orient, load,
    ex, exm, sec, fi, wi, part, edge, lf, own_edge, ghost_edge,
    strips, relay, arrived, got, both, picked, got2, ghost,
    send1, recv1, send_h, recv_h, send2, recv2, send_e, recv_e, send_r, recv_r, send_m, recv_m,
):
    inside = pl.ds(CHUNK, ROWS)
    fetch = [
        pltpu.make_async_copy(src, dst, load.at[n])
        for n, (src, dst) in enumerate(
            (
                (mom_hbm.at[0], ex.at[pl.ds(1, 3), :, inside]),
                (dens_hbm.at[0], ex.at[0, :, inside]),
                (ener_hbm.at[0], ex.at[4, :, inside]),
                (met_hbm.at[0], exm.at[pl.ds(0, 4), inside]),
                (vol_hbm.at[0], exm.at[4, inside]),
                (placed_hbm, placed),
                (neighbour_hbm, neighbour),
                (face_hbm, face),
                (orient_hbm, orient),
            )
        )
    ]
    for copy in fetch:
        copy.start()
    b, s = lax.axis_index("blk"), lax.axis_index("ij")
    c = lax.rem(b, CORES)
    z = lax.rem(b // CORES, Z)
    y = b // (CORES * Z)
    first, second = peers_first(y, z, c, s), peers_second(y, z, c, s)
    below = {"blk": b, "ij": lax.rem(s + IJ - 1, IJ)}
    above = {"blk": b, "ij": lax.rem(s + 1, IJ)}
    everyone = first[1:] + second[1:] + [below, above]
    barrier = pltpu.get_barrier_semaphore()
    for peer in everyone:
        pl.semaphore_signal(barrier, inc=1, device_id=peer, device_id_type=MESH)
    at_start, at_end = s == 0, s == IJ - 1
    for copy in fetch:
        copy.wait()
    pack(ex, exm, strips, relay)
    pl.semaphore_wait(barrier, len(everyone))

    def send(src, dst, out_sem, in_sem, peer):
        copy = pltpu.make_async_remote_copy(
            src_ref=src, dst_ref=dst, send_sem=out_sem, recv_sem=in_sem,
            device_id=peer, device_id_type=MESH,
        )
        copy.start()
        return copy

    main, ends = pl.ds(0, 72), pl.ds(72, 16)
    beside = (below, above)
    order = (2, 4, 1, 3, 5, 6, 7)
    edges = [
        send(relay.at[n], arrived.at[1 - n], send_e.at[n], recv_e.at[1 - n], beside[n]) for n in range(2)
    ]
    hop1 = {
        k: send(strips.at[k % 2, main], got.at[k, main], send1.at[k], recv1.at[k], first[k]) for k in order
    }
    slide = []
    for n in range(2):
        src, dst = pl.ds((CHUNK, ROWS)[n], CHUNK), pl.ds((CHUNK + ROWS, 0)[n], CHUNK)
        slide.append(send(exm.at[:, src], exm.at[:, dst], send_m.at[n], recv_m.at[1 - n], beside[n]))
        slide.append(send(ex.at[:, :, src], ex.at[:, :, dst], send_r.at[n], recv_r.at[1 - n], beside[n]))
    table = routes(placed, neighbour, face, orient, second)
    before_ghosts(ex, exm, fi, wi, part, time_step, range(4))
    for copy in edges:
        copy.wait_send()
    for n in range(2):
        pltpu.make_async_remote_copy(
            src_ref=relay.at[n], dst_ref=arrived.at[n], send_sem=send_e.at[n], recv_sem=recv_e.at[n],
            device_id=beside[n], device_id_type=MESH,
        ).wait_recv()
    pack_ends(relay, arrived, strips, at_start, at_end)
    hop_ends = {
        k: send(strips.at[k % 2, ends], got.at[k, ends], send_h.at[k], recv_h.at[k], first[k]) for k in order
    }
    main_sign = jnp.where((rows_of((72, COLS)) >= 32) & (rows_of((72, COLS)) < 64) & (lanes((72, COLS)) >= 112), -1.0, 1.0)
    ends_sign = jnp.where(
        (rows_of((16, COLS)) >= 4) & (rows_of((16, COLS)) < 8) & (lanes((16, COLS)) >= 112), -1.0, 1.0
    )
    for piece, sign, copies in ((slice(0, 72), main_sign, hop1), (slice(72, 88), ends_sign, hop_ends)):
        for k in (0, 1, 2, 3, 6, 7, 4, 5):
            if k > 0:
                copies[k].wait_recv()
                x = got[k, piece, :]
            else:
                x = strips[0, piece, :]
            both[k, piece, :] = x
            both[8 + k, piece, :] = flip(x) * sign
    near = (lanes((88, COLS)) & 7) < 4
    hop2 = []
    for k in (4, 5, 2, 3, 6, 7, 1, 0):
        parts = []
        for f in range(2):
            q, g, o = table[2 * k + f]
            dz = lax.rem(z - lax.rem(q // CORES, Z) + Z, Z)
            parts.append(both[jnp.where(g == f, 8, 0) + 2 * dz + o])
        message = jnp.where(near, parts[0], parts[1])
        if k == 0:
            got2[0] = message
        else:
            picked[k] = message
            hop2.append(send(picked.at[k], got2.at[k], send2.at[k], recv2.at[k], second[k]))
    for copy in slide:
        copy.wait_send()
    for n in range(2):
        dst = pl.ds((0, CHUNK + ROWS)[n], CHUNK)
        pltpu.make_async_remote_copy(
            src_ref=exm.at[:, dst], dst_ref=exm.at[:, dst], send_sem=send_m.at[n], recv_sem=recv_m.at[n],
            device_id=beside[n], device_id_type=MESH,
        ).wait_recv()
        pltpu.make_async_remote_copy(
            src_ref=ex.at[:, :, dst], dst_ref=ex.at[:, :, dst], send_sem=send_r.at[n], recv_sem=recv_r.at[n],
            device_id=beside[n], device_id_type=MESH,
        ).wait_recv()
    walls(ex, at_start, at_end)
    metric_walls(exm, at_start, at_end)
    before_ghosts(ex, exm, fi, wi, part, time_step, (-1, 4))
    for n in range(-1, 5):
        for ch in range(5):
            sec[ch, :, span(n), :] = ex[ch, :, span(n), :] + row_terms(exm, fi, wi, part, n, ch, time_step)
    for copy in hop2:
        copy.wait_recv()
    sides = []
    for f in range(2):
        q, g, o = table[f]
        dy = lax.rem(y - q // (CORES * Z) + Y, Y)
        dc = jnp.where(lax.rem(q, CORES) == c, 0, 1)
        sides.append(got2[2 * dy + dc])
    ghost[...] = jnp.where(near, sides[0], sides[1])
    line_section(strips.at[0], ghost, lf, own_edge, ghost_edge, edge, time_step)
    at = lanes((CHUNK, COLS))
    border = (at < 2) | (at >= COLS - 2)
    for ch in range(5):
        for n in range(4):
            rows = slice(n * CHUNK, (n + 1) * CHUNK)
            for k in range(PLANES):
                x = shift_lanes(own_edge[ch, rows, :], -8 * k - 4)
                sec[ch, k, span(n), :] = jnp.where(border, x, sec[ch, k, span(n), :])
        for n in (-1, 4):
            sec[ch, :, span(n), :] = sec[ch, :, span(n), :] + edge_columns(edge, exm, n, ch, time_step)
    walls(sec, at_start, at_end)
    half = 0.5 * time_step
    before_ghosts(sec, exm, fi, wi, part, half, range(4))
    halo_rows(sec, exm, fi, wi, half)
    changes = edge_terms(
        edge_values([own_edge[n] for n in range(5)], own_edge[5], own_edge[6], half),
        edge_values([ghost_edge[n] for n in range(5)], ghost_edge[5], ghost_edge[6], half),
    )
    for n, x in enumerate(changes):
        edge[n, CHUNK : CHUNK + ROWS, :] = x
    for n in range(4):
        rows = slice(n * CHUNK, (n + 1) * CHUNK)
        for ch in range(5):
            value = 0.5 * (ex[ch, :, span(n), :] + sec[ch, :, span(n), :])
            value = value + row_terms(exm, fi, wi, part, n, ch, half)
            value = value + edge_columns(edge, exm, n, ch, half)
            if ch == 0:
                out_d[0, :, rows, :] = value
            elif ch == 4:
                out_e[0, :, rows, :] = value
            else:
                out_m[0, ch - 1, :, rows, :] = value
    for copy in list(hop1.values()) + list(hop_ends.values()) + hop2:
        copy.wait_send()


def hand_over(d, m, e, out_d, out_m, out_e, sems):
    copies = [
        pltpu.make_async_copy(src, dst, sems.at[n])
        for n, (src, dst) in enumerate(((m, out_m), (d, out_d), (e, out_e)))
    ]
    for copy in copies:
        copy.start()
    for copy in copies:
        copy.wait()


def local(density, momentum, energy, metrics, volume, placed, neighbour, face, orient):
    smem, vmem, i32, f32 = pltpu.SMEM, pltpu.VMEM, jnp.int32, jnp.float32
    anywhere = pl.BlockSpec(memory_space=pltpu.HBM)
    inside = pl.BlockSpec(memory_space=pltpu.VMEM)
    dma = pltpu.SemaphoreType.DMA
    padded = ROWS + 2 * CHUNK
    shapes = tuple(jax.ShapeDtypeStruct(x.shape, f32) for x in (density, momentum, energy))
    results = pl.pallas_call(
        body,
        out_shape=shapes,
        in_specs=[anywhere] * 9,
        out_specs=(inside,) * 3,
        scratch_shapes=[
            smem((BLOCKS,), i32), smem((2, BLOCKS), i32), smem((2, BLOCKS), i32), smem((2, BLOCKS), i32),
            dma((9,)),
            vmem((5, PLANES, padded, COLS), f32),
            vmem((5, padded, COLS), f32),
            vmem((5, PLANES, padded, COLS), f32),
            vmem((5, PLANES, padded + 2 * CHUNK, COLS), f32),
            vmem((4, PLANES, padded + 2 * CHUNK, COLS), f32),
            vmem((5, PLANES, padded, COLS), f32),
            vmem((9, padded, COLS), f32),
            vmem((9, padded, COLS), f32),
            vmem((7, ROWS, COLS), f32),
            vmem((7, ROWS, COLS), f32),
            vmem((2, 88, COLS), f32),
            vmem((2, CHUNK, COLS), f32),
            vmem((2, CHUNK, COLS), f32),
            vmem((8, 88, COLS), f32),
            vmem((16, 88, COLS), f32),
            vmem((8, 88, COLS), f32),
            vmem((8, 88, COLS), f32),
            vmem((88, COLS), f32),
            dma((8,)), dma((8,)), dma((8,)), dma((8,)), dma((8,)), dma((8,)),
            dma((2,)), dma((2,)), dma((2,)), dma((2,)), dma((2,)), dma((2,)),
        ],
        compiler_params=pltpu.CompilerParams(
            collective_id=0, has_side_effects=True, vmem_limit_bytes=48 << 20
        ),
    )(
        *(
            pltpu.with_memory_space_constraint(x, pltpu.HBM)
            for x in (placed, neighbour.T, face.T, orient.T, density, momentum, energy, metrics, volume)
        )
    )
    return pl.pallas_call(
        hand_over,
        out_shape=shapes,
        in_specs=[inside] * 3,
        out_specs=(anywhere,) * 3,
        scratch_shapes=[dma((3,))],
    )(*(pltpu.with_memory_space_constraint(x, pltpu.VMEM) for x in results))


def solution(mesh):
    return jax.shard_map(
        local,
        mesh=mesh,
        in_specs=(
            P("blk", None, "ij", None),
            P("blk", None, None, "ij", None),
            P("blk", None, "ij", None),
            P("blk", None, "ij", None),
            P("blk", "ij", None),
            P(),
            P(),
            P(),
            P(),
        ),
        out_specs=(
            P("blk", None, "ij", None),
            P("blk", None, None, "ij", None),
            P("blk", None, "ij", None),
        ),
        check_vma=False,
    )
```

```python
import functools

import jax
import jax.numpy as jnp
from jax import lax
from jax.experimental import pallas as pl
from jax.experimental.pallas import tpu as pltpu
from jax.sharding import PartitionSpec as P

MESH = pl.DeviceIdType.MESH
pressure_factor = 0.4
viscosity = 0.05
conduction = 0.1
time_step = 0.03
ROWS, COLS, PLANES, CHUNK = 32, 128, 6, 8
Y, Z, CORES, IJ, BLOCKS = 4, 4, 2, 8, 32
LOW, HIGH = slice(6, 8), slice(40, 42)


def lanes(shape):
    return lax.broadcasted_iota(jnp.int32, shape, len(shape) - 1)


def rows_of(shape):
    return lax.broadcasted_iota(jnp.int32, shape, len(shape) - 2)


def shift_lanes(x, by):
    by = by % COLS
    return x if by == 0 else pltpu.roll(x, by, x.ndim - 1)


def primitives(rho, m1, m2, m3, energy, dt):
    inv = 1.0 / rho
    u1, u2, u3 = m1 * inv, m2 * inv, m3 * inv
    kinetic = 0.5 * (m1 * u1 + m2 * u2 + m3 * u3)
    p = pressure_factor * (energy - kinetic)
    head = energy + p
    soft = dt * viscosity / 12.0
    warm = dt * conduction / 12.0
    curved = (soft * u1, soft * u2, soft * u3, inv * (soft * kinetic + warm * p))
    return u1, u2, u3, p, head, curved


def flux(rho, m1, m2, m3, prim, gx, gy):
    u1, u2, u3, p, head, _ = prim
    speed = gx * u1 + gy * u2
    return (rho * speed, m1 * speed + gx * p, m2 * speed + gy * p, m3 * speed, head * speed)


def flux_planes(m1, m2, m3, prim):
    u1, u2, u3, p, head, _ = prim
    return (m3, m1 * u3, m2 * u3, m3 * u3 + p, head * u3)


def slope(b2, b1, a1, a2):
    return 8.0 * (a1 - b1) - (a2 - b2)


def curve(b2, b1, a1, a2):
    return 16.0 * (a1 + b1) - (a2 + b2)


def plane_shift(f, by):
    by = by % PLANES
    return jnp.concatenate([f[by:], f[:by]], axis=0)


def span(c):
    return slice(CHUNK + c * CHUNK, 2 * CHUNK + c * CHUNK)


def chunk_metrics(exm, c, dt):
    ax, ay, bx, by, v = (exm[n, span(c), :] for n in range(5))
    return (v * ax, v * ay, v * bx, v * by, (dt / 12.0) / v, ax * ax + ay * ay, bx * bx + by * by)


def before_ghosts(state, exm, fi, wi, part, dt, chunks):
    for c in chunks:
        gax, gay, gbx, gby, iv, rw, cw = chunk_metrics(exm, c, dt)
        center = -30.0 * (rw + cw + 1.0)
        rho, m1, m2, m3, energy = (state[ch, :, span(c), :] for ch in range(5))
        prim = primitives(rho, m1, m2, m3, energy, dt)
        curved = prim[5]
        inner = span(c + 1)
        for ch, f in enumerate(flux(rho, m1, m2, m3, prim, gax, gay)):
            fi[ch, :, inner, :] = f
        for n, w in enumerate(curved):
            wi[n, :, inner, :] = w
        fj = flux(rho, m1, m2, m3, prim, gbx, gby)
        fk = flux_planes(m1, m2, m3, prim)
        for ch in range(5):
            f, g = fj[ch], fk[ch]
            dj = slope(*(shift_lanes(f, by) for by in (2, 1, -1, -2)))
            dk = slope(*(plane_shift(g, by) for by in (-2, -1, 1, 2)))
            total = -(dj * iv) - (dt / 12.0) * dk
            if ch > 0:
                w = curved[ch - 1]
                sj = curve(*(shift_lanes(w, by) for by in (2, 1, -1, -2)))
                sk = curve(*(plane_shift(w, by) for by in (-2, -1, 1, 2)))
                total = total + cw * sj + sk + center * w
            part[ch, :, span(c), :] = total


def row_terms(exm, fi, wi, part, c, ch, dt):
    gax, gay, gbx, gby, iv, rw, cw = chunk_metrics(exm, c, dt)
    base = 2 * CHUNK + c * CHUNK
    di = slope(*(fi[ch, :, base + d : base + d + CHUNK, :] for d in (-2, -1, 1, 2)))
    total = part[ch, :, span(c), :] - di * iv
    if ch > 0:
        si = curve(*(wi[ch - 1, :, base + d : base + d + CHUNK, :] for d in (-2, -1, 1, 2)))
        total = total + rw * si
    return total


def edge_columns(edge, exm, c, ch, dt):
    at = lanes((CHUNK, COLS))
    border = (at < 2) | (at >= COLS - 2)
    gax, gay, gbx, gby, iv, rw, cw = chunk_metrics(exm, c, dt)
    terms = []
    for k in range(PLANES):
        term = -(shift_lanes(edge[ch, span(c), :], -8 * k - 4) * iv)
        if ch > 0:
            term = term + cw * shift_lanes(edge[4 + ch, span(c), :], -8 * k - 4)
        terms.append(jnp.where(border, term, 0.0))
    return jnp.stack(terms, axis=0)


def apart(a, b):
    third = jnp.where(lanes(a.shape) < 32, shift_lanes(a, -96), shift_lanes(b, 32))
    return [a, shift_lanes(a, -48), third, shift_lanes(b, -16), shift_lanes(b, -64)]


def spread(x):
    x = jnp.where((lanes(x.shape) & 63) < 8, x, 0.0)
    pair = x + shift_lanes(x, 8)
    return pair + shift_lanes(pair, 16) + shift_lanes(pair, 32)


def lines(own, ghost):
    near = (lanes(own.shape) & 7) < 4
    first = jnp.where(near, ghost, own)
    second = jnp.where(near, own, ghost)
    return jnp.where(lanes(own.shape) < 64, first, shift_lanes(second, 64))


def line_planes(x, by):
    m = lanes(x.shape) & 63
    if by > 0:
        return jnp.where(m < 48 - 8 * by, shift_lanes(x, -8 * by), shift_lanes(x, 48 - 8 * by))
    return jnp.where(m >= -8 * by, shift_lanes(x, -8 * by), shift_lanes(x, -48 - 8 * by))


def edge_terms(mine, theirs):
    upper = (lanes(mine[0].shape) & 7) >= 4
    out = []
    for n in range(9):
        h = theirs[n] - mine[n]
        high, low = jnp.where(upper, h, 0.0), jnp.where(upper, 0.0, h)
        if n < 5:
            left = 8.0 * shift_lanes(high, -1) - shift_lanes(high, -2)
            right = shift_lanes(low, 2) - 8.0 * shift_lanes(low, 1)
        else:
            left = 16.0 * shift_lanes(high, -1) - shift_lanes(high, -2)
            right = 16.0 * shift_lanes(low, 1) - shift_lanes(low, 2)
        out.append(jnp.where(upper, right, left))
    return out


def edge_values(fields, gx, gy, dt):
    rho, m1, m2, m3, energy = fields
    prim = primitives(rho, m1, m2, m3, energy, dt)
    return flux(rho, m1, m2, m3, prim, gx, gy) + prim[5]


def column_metric(c, e):
    return jnp.concatenate([shift_lanes(c, -32 * g - 8 * e) for g in range(4)], axis=0)


def line_section(own, ghost, lf, own_edge, ghost_edge, edge, dt):
    a, b, c = slice(0, 32), slice(32, 64), slice(64, 72)
    ob, gb = own[b, :], ghost[b, :]
    fields = [lines(o, g) for o, g in zip(apart(own[a, :], ob), apart(ghost[a, :], gb))]
    gbx, gby = (spread(lines(shift_lanes(ob, -n), shift_lanes(gb, -n))) for n in (112, 120))
    oc, gc = own[c, :], ghost[c, :]
    gax, gay, v = (spread(lines(column_metric(oc, e), column_metric(gc, e))) for e in range(3))
    rho, m1, m2, m3, energy = fields
    prim = primitives(rho, m1, m2, m3, energy, dt)
    curved = prim[5]
    for n, f in enumerate(flux(rho, m1, m2, m3, prim, gax, gay) + curved):
        lf[n, span(0).start : span(3).stop, :] = f
    h = (slice(72, 76), slice(76, 80), slice(80, 84))
    oa, ob, od = (own[n, :] for n in h)
    ga, gb, gd = (ghost[n, :] for n in h)
    mine, theirs = apart(oa, ob), apart(ga, gb)
    hax, hay = (spread(lines(shift_lanes(od, -n), shift_lanes(gd, -n))) for n in (0, 8))
    ends = [lines(o, g) for o, g in zip(mine, theirs)]
    end_prim = primitives(*ends, dt)
    for n, f in enumerate(flux(*ends[:4], end_prim, hax, hay) + end_prim[5]):
        lf[n, LOW, :] = f[0:2]
        lf[n, HIGH, :] = f[2:4]
    ends = edge_terms(
        edge_values(mine, *(spread(shift_lanes(ob, -n)) for n in (112, 120)), dt),
        edge_values(theirs, *(spread(shift_lanes(gb, -n)) for n in (112, 120)), dt),
    )
    for n, f in enumerate(ends):
        edge[n, LOW, :] = f[0:2]
        edge[n, HIGH, :] = f[2:4]
    inv = 1.0 / v
    iv = (dt / 12.0) * inv
    rw = (gax * gax + gay * gay) * (inv * inv)
    cw = (gbx * gbx + gby * gby) * (inv * inv)
    center = -30.0 * (rw + cw + 1.0)
    fj = flux(rho, m1, m2, m3, prim, gbx, gby)
    fk = flux_planes(m1, m2, m3, prim)
    near = (lanes((ROWS, COLS)) & 7) < 4
    for ch in range(7):
        if ch < 5:
            di = slope(*(lf[ch, CHUNK + d : CHUNK + d + ROWS, :] for d in (-2, -1, 1, 2)))
            dj = slope(*(shift_lanes(fj[ch], by) for by in (2, 1, -1, -2)))
            dk = slope(*(line_planes(fk[ch], by) for by in (-2, -1, 1, 2)))
            value = fields[ch] - (di + dj) * iv - (dt / 12.0) * dk
            if ch > 0:
                w = curved[ch - 1]
                si = curve(*(lf[4 + ch, CHUNK + d : CHUNK + d + ROWS, :] for d in (-2, -1, 1, 2)))
                sj = curve(*(shift_lanes(w, by) for by in (2, 1, -1, -2)))
                sk = curve(*(line_planes(w, by) for by in (-2, -1, 1, 2)))
                value = value + rw * si + cw * sj + sk + center * w
        else:
            value = (gbx, gby)[ch - 5]
        other = shift_lanes(value, 64)
        own_edge[ch] = jnp.where(near, other, value)
        ghost_edge[ch] = jnp.where(near, value, other)


def pack(ex, exm, strips, relay):
    at = lanes((ROWS, COLS)) >> 3
    inside = slice(CHUNK, CHUNK + ROWS)
    v = exm[4, inside, :]
    for half in range(2):
        acc = jnp.zeros((ROWS, COLS), jnp.float32)
        for n in range(16):
            q = 16 * half + n
            x = ex[q // 6, q % 6, inside, :] if q < 30 else v * exm[q - 28, inside, :]
            acc = jnp.where(at == n, shift_lanes(x, 4 + 8 * n), acc)
        strips[0, 32 * half : 32 * half + 32, :] = acc
    slot = lanes((CHUNK, COLS)) >> 3
    acc = jnp.zeros((CHUNK, COLS), jnp.float32)
    for g in range(4):
        part = exm[4, span(g), :]
        for e in range(3):
            x = part * exm[e, span(g), :] if e < 2 else part
            acc = jnp.where(slot == 4 * g + e, shift_lanes(x, 4 + 32 * g + 8 * e), acc)
    strips[0, 64:72, :] = acc
    for r in range(ROWS):
        for half in (0, 32):
            strips[1, half + 31 - r : half + 32 - r, :] = strips[0, half + r : half + r + 1, :]
    turned = jnp.where((lanes(acc.shape) & 32) == 0, shift_lanes(acc, 32), shift_lanes(acc, -32))
    turned = jnp.where((lanes(acc.shape) & 31) < 16, -turned, turned)
    for r in range(CHUNK):
        strips[1, 71 - r : 72 - r, :] = turned[r : r + 1, :]
    for side, r in ((0, 0), (1, ROWS - 2)):
        relay[side, 0:2, :] = strips[0, r : r + 2, :]
        relay[side, 2:4, :] = strips[0, 32 + r : 34 + r, :]
        relay[side, 4:6, :] = shift_lanes(acc[r % CHUNK : r % CHUNK + 2], -32 * (r // CHUNK))
        relay[side, 6:8, :] = jnp.zeros((2, COLS), jnp.float32)


def pack_ends(relay, arrived, strips, at_start, at_end):
    turn = lanes((1, COLS))
    signs = (
        jnp.where(turn >= 48, -1.0, 1.0),
        jnp.where(turn < 64, -1.0, 1.0),
        jnp.ones((1, COLS), jnp.float32),
    )
    for n in range(3):
        base = 72 + 4 * n
        for r in range(4):
            near = 2 * n + r % 2
            wall = 2 * n + 1 - r % 2
            side = r // 2
            mirror = relay[side, wall : wall + 1, :]
            if side == 0:
                row = jnp.where(at_start, signs[n] * mirror, arrived[side, near : near + 1, :])
            else:
                row = jnp.where(at_end, mirror, arrived[side, near : near + 1, :])
            strips[0, base + r : base + r + 1, :] = row
            strips[1, base + 3 - r : base + 4 - r, :] = -row if n == 2 else row
    for m in range(2):
        strips[m, 84:88, :] = jnp.zeros((4, COLS), jnp.float32)


def walls(state, at_start, at_end):
    for ch in range(5):
        sign = -1.0 if 1 <= ch <= 3 else 1.0
        for r in range(2):
            low, high = slice(7 - r, 8 - r), slice(40 + r, 41 + r)
            mirror = state[ch, :, 8 + r : 9 + r, :]
            state[ch, :, low, :] = jnp.where(at_start, sign * mirror, state[ch, :, low, :])
            mirror = state[ch, :, 39 - r : 40 - r, :]
            state[ch, :, high, :] = jnp.where(at_end, mirror, state[ch, :, high, :])


def metric_walls(exm, at_start, at_end):
    for r in range(2):
        low, high = slice(7 - r, 8 - r), slice(40 + r, 41 + r)
        exm[:, low, :] = jnp.where(at_start, exm[:, 8 + r : 9 + r, :], exm[:, low, :])
        exm[:, high, :] = jnp.where(at_end, exm[:, 39 - r : 40 - r, :], exm[:, high, :])


def halo_rows(state, exm, fi, wi, dt):
    for rows in (LOW, HIGH):
        rho, m1, m2, m3, energy = (state[ch, :, rows, :] for ch in range(5))
        v = exm[4, rows, :]
        prim = primitives(rho, m1, m2, m3, energy, dt)
        target = slice(rows.start + CHUNK, rows.stop + CHUNK)
        for ch, f in enumerate(flux(rho, m1, m2, m3, prim, v * exm[0, rows, :], v * exm[1, rows, :])):
            fi[ch, :, target, :] = f
        for n, w in enumerate(prim[5]):
            wi[n, :, target, :] = w


def flip(x):
    t = lanes(x.shape) & 7
    for d in (4, 2, 1):
        x = jnp.where((t & d) == 0, shift_lanes(x, -d), shift_lanes(x, d))
    return x


def peers_first(y, z, c, s):
    out = []
    for dz in range(Z):
        for m in range(2):
            blk = (y * Z + lax.rem(z + dz, Z)) * CORES + c
            out.append({"blk": blk, "ij": (IJ - 1 - s) if m else s})
    return out


def peers_second(y, z, c, s):
    out = []
    for dy in range(Y):
        for dc in range(2):
            blk = (lax.rem(y + dy, Y) * Z + z) * CORES + (1 - c if dc else c)
            out.append({"blk": blk, "ij": s})
    return out


def routes(placed, neighbour, face, orient, targets):
    ids = [placed[t["blk"]] for t in targets]
    wanted = [(b, f) for b in ids for f in range(2)]
    nids = [neighbour[f, b] for b, f in wanted]

    def find(p, found):
        held = placed[p]
        return tuple(jnp.where(n == held, p, a) for n, a in zip(nids, found))

    found = lax.fori_loop(0, BLOCKS, find, tuple(jnp.int32(0) for _ in nids))
    return [(q, face[f, b], orient[f, b]) for q, (b, f) in zip(found, wanted)]


def body(
    placed_hbm, neighbour_hbm, face_hbm, orient_hbm, dens_hbm, mom_hbm, ener_hbm, met_hbm, vol_hbm,
    out_d, out_m, out_e,
    placed, neighbour, face, orient, load,
    ex, exm, sec, fi, wi, part, edge, lf, own_edge, ghost_edge,
    strips, relay, arrived, got, both, picked, got2, both_e, picked_e, got2_e, ghost,
    send1, recv1, send_h, recv_h, send2, recv2, send_f, recv_f, send_e, recv_e, send_r, recv_r, send_m, recv_m,
):
    inside = pl.ds(CHUNK, ROWS)
    fetch = [
        pltpu.make_async_copy(src, dst, load.at[n])
        for n, (src, dst) in enumerate(
            (
                (mom_hbm.at[0], ex.at[pl.ds(1, 3), :, inside]),
                (dens_hbm.at[0], ex.at[0, :, inside]),
                (ener_hbm.at[0], ex.at[4, :, inside]),
                (met_hbm.at[0], exm.at[pl.ds(0, 4), inside]),
                (vol_hbm.at[0], exm.at[4, inside]),
                (placed_hbm, placed),
                (neighbour_hbm, neighbour),
                (face_hbm, face),
                (orient_hbm, orient),
            )
        )
    ]
    for copy in fetch:
        copy.start()
    b, s = lax.axis_index("blk"), lax.axis_index("ij")
    c = lax.rem(b, CORES)
    z = lax.rem(b // CORES, Z)
    y = b // (CORES * Z)
    first, second = peers_first(y, z, c, s), peers_second(y, z, c, s)
    below = {"blk": b, "ij": lax.rem(s + IJ - 1, IJ)}
    above = {"blk": b, "ij": lax.rem(s + 1, IJ)}
    everyone = first[1:] + second[1:] + [below, above]
    barrier = pltpu.get_barrier_semaphore()
    for peer in everyone:
        pl.semaphore_signal(barrier, inc=1, device_id=peer, device_id_type=MESH)
    at_start, at_end = s == 0, s == IJ - 1
    for copy in fetch:
        copy.wait()
    pack(ex, exm, strips, relay)
    pl.semaphore_wait(barrier, len(everyone))

    def send(src, dst, out_sem, in_sem, peer):
        copy = pltpu.make_async_remote_copy(
            src_ref=src, dst_ref=dst, send_sem=out_sem, recv_sem=in_sem,
            device_id=peer, device_id_type=MESH,
        )
        copy.start()
        return copy

    main, ends = pl.ds(0, 72), pl.ds(72, 16)
    beside = (below, above)
    order = (2, 4, 1, 3, 5, 6, 7)
    edges = [
        send(relay.at[n], arrived.at[1 - n], send_e.at[n], recv_e.at[1 - n], beside[n]) for n in range(2)
    ]
    hop1 = {
        k: send(strips.at[k % 2, main], got.at[k, main], send1.at[k], recv1.at[k], first[k]) for k in order
    }
    table = routes(placed, neighbour, face, orient, second)
    before_ghosts(ex, exm, fi, wi, part, time_step, range(4))
    for copy in edges:
        copy.wait_send()
    for n in range(2):
        pltpu.make_async_remote_copy(
            src_ref=relay.at[n], dst_ref=arrived.at[n], send_sem=send_e.at[n], recv_sem=recv_e.at[n],
            device_id=beside[n], device_id_type=MESH,
        ).wait_recv()
    pack_ends(relay, arrived, strips, at_start, at_end)
    hop_ends = {
        k: send(strips.at[k % 2, ends], got.at[k, ends], send_h.at[k], recv_h.at[k], first[k]) for k in order
    }
    slide = []
    for n in range(2):
        src, dst = pl.ds((CHUNK, ROWS + 4)[n], 4), pl.ds((CHUNK + ROWS, 4)[n], 4)
        slide.append(send(exm.at[:, src], exm.at[:, dst], send_m.at[n], recv_m.at[1 - n], beside[n]))
        slide.append(send(ex.at[:, :, src], ex.at[:, :, dst], send_r.at[n], recv_r.at[1 - n], beside[n]))
    main_sign = jnp.where((rows_of((72, COLS)) >= 32) & (rows_of((72, COLS)) < 64) & (lanes((72, COLS)) >= 112), -1.0, 1.0)
    ends_sign = jnp.where(
        (rows_of((16, COLS)) >= 4) & (rows_of((16, COLS)) < 8) & (lanes((16, COLS)) >= 112), -1.0, 1.0
    )
    slots = []
    for q, g, o in table:
        slots.append((lax.rem(z - lax.rem(q // CORES, Z) + Z, Z) * 2 + o, g))
    near = (lanes((72, COLS)) & 7) < 4
    hop2 = []
    for piece, size, sign, copies, variants, chosen, landed, sems in (
        (slice(0, 72), 72, main_sign, hop1, both, picked, got2, (send2, recv2)),
        (slice(72, 88), 16, ends_sign, hop_ends, both_e, picked_e, got2_e, (send_f, recv_f)),
    ):
        for k in (0, 1, 2, 3, 6, 7, 4, 5):
            if k > 0:
                copies[k].wait_recv()
                x = got[k, piece, :]
            else:
                x = strips[0, piece, :]
            variants[k] = x
            variants[8 + k] = flip(x) * sign
        for k in (4, 5, 2, 3, 6, 7, 1, 0):
            parts = []
            for f in range(2):
                slot, g = slots[2 * k + f]
                parts.append(variants[jnp.where(g == f, 8, 0) + slot])
            message = jnp.where(near[:size], parts[0], parts[1])
            if k == 0:
                landed[0] = message
            else:
                chosen[k] = message
                hop2.append(send(chosen.at[k], landed.at[k], sems[0].at[k], sems[1].at[k], second[k]))
    for copy in slide:
        copy.wait_send()
    for n in range(2):
        dst = pl.ds((4, CHUNK + ROWS)[n], 4)
        pltpu.make_async_remote_copy(
            src_ref=exm.at[:, dst], dst_ref=exm.at[:, dst], send_sem=send_m.at[n], recv_sem=recv_m.at[n],
            device_id=beside[n], device_id_type=MESH,
        ).wait_recv()
        pltpu.make_async_remote_copy(
            src_ref=ex.at[:, :, dst], dst_ref=ex.at[:, :, dst], send_sem=send_r.at[n], recv_sem=recv_r.at[n],
            device_id=beside[n], device_id_type=MESH,
        ).wait_recv()
    walls(ex, at_start, at_end)
    metric_walls(exm, at_start, at_end)
    before_ghosts(ex, exm, fi, wi, part, time_step, (-1, 4))
    for n in range(-1, 5):
        for ch in range(5):
            sec[ch, :, span(n), :] = ex[ch, :, span(n), :] + row_terms(exm, fi, wi, part, n, ch, time_step)
    origin = []
    for f in range(2):
        q, g, o = table[f]
        dy = lax.rem(y - q // (CORES * Z) + Y, Y)
        dc = jnp.where(lax.rem(q, CORES) == c, 0, 1)
        origin.append(2 * dy + dc)
    for copy in hop2[:7]:
        copy.wait_recv()
    ghost[0:72, :] = jnp.where(near, got2[origin[0]], got2[origin[1]])
    for copy in hop2[7:]:
        copy.wait_recv()
    ghost[72:88, :] = jnp.where(near[:16], got2_e[origin[0]], got2_e[origin[1]])
    line_section(strips.at[0], ghost, lf, own_edge, ghost_edge, edge, time_step)
    at = lanes((CHUNK, COLS))
    border = (at < 2) | (at >= COLS - 2)
    for ch in range(5):
        for n in range(4):
            rows = slice(n * CHUNK, (n + 1) * CHUNK)
            for k in range(PLANES):
                x = shift_lanes(own_edge[ch, rows, :], -8 * k - 4)
                sec[ch, k, span(n), :] = jnp.where(border, x, sec[ch, k, span(n), :])
        for n in (-1, 4):
            sec[ch, :, span(n), :] = sec[ch, :, span(n), :] + edge_columns(edge, exm, n, ch, time_step)
    walls(sec, at_start, at_end)
    half = 0.5 * time_step
    before_ghosts(sec, exm, fi, wi, part, half, range(4))
    halo_rows(sec, exm, fi, wi, half)
    changes = edge_terms(
        edge_values([own_edge[n] for n in range(5)], own_edge[5], own_edge[6], half),
        edge_values([ghost_edge[n] for n in range(5)], ghost_edge[5], ghost_edge[6], half),
    )
    for n, x in enumerate(changes):
        edge[n, CHUNK : CHUNK + ROWS, :] = x
    for n in range(4):
        rows = slice(n * CHUNK, (n + 1) * CHUNK)
        for ch in range(5):
            value = 0.5 * (ex[ch, :, span(n), :] + sec[ch, :, span(n), :])
            value = value + row_terms(exm, fi, wi, part, n, ch, half)
            value = value + edge_columns(edge, exm, n, ch, half)
            if ch == 0:
                out_d[0, :, rows, :] = value
            elif ch == 4:
                out_e[0, :, rows, :] = value
            else:
                out_m[0, ch - 1, :, rows, :] = value
    for copy in list(hop1.values()) + list(hop_ends.values()) + hop2:
        copy.wait_send()


def hand_over(d, m, e, out_d, out_m, out_e, sems):
    copies = [
        pltpu.make_async_copy(src, dst, sems.at[n])
        for n, (src, dst) in enumerate(((m, out_m), (d, out_d), (e, out_e)))
    ]
    for copy in copies:
        copy.start()
    for copy in copies:
        copy.wait()


def local(density, momentum, energy, metrics, volume, placed, neighbour, face, orient):
    smem, vmem, i32, f32 = pltpu.SMEM, pltpu.VMEM, jnp.int32, jnp.float32
    anywhere = pl.BlockSpec(memory_space=pltpu.HBM)
    inside = pl.BlockSpec(memory_space=pltpu.VMEM)
    dma = pltpu.SemaphoreType.DMA
    padded = ROWS + 2 * CHUNK
    shapes = tuple(jax.ShapeDtypeStruct(x.shape, f32) for x in (density, momentum, energy))
    results = pl.pallas_call(
        body,
        out_shape=shapes,
        in_specs=[anywhere] * 9,
        out_specs=(inside,) * 3,
        scratch_shapes=[
            smem((BLOCKS,), i32), smem((2, BLOCKS), i32), smem((2, BLOCKS), i32), smem((2, BLOCKS), i32),
            dma((9,)),
            vmem((5, PLANES, padded, COLS), f32),
            vmem((5, padded, COLS), f32),
            vmem((5, PLANES, padded, COLS), f32),
            vmem((5, PLANES, padded + 2 * CHUNK, COLS), f32),
            vmem((4, PLANES, padded + 2 * CHUNK, COLS), f32),
            vmem((5, PLANES, padded, COLS), f32),
            vmem((9, padded, COLS), f32),
            vmem((9, padded, COLS), f32),
            vmem((7, ROWS, COLS), f32),
            vmem((7, ROWS, COLS), f32),
            vmem((2, 88, COLS), f32),
            vmem((2, CHUNK, COLS), f32),
            vmem((2, CHUNK, COLS), f32),
            vmem((8, 88, COLS), f32),
            vmem((16, 72, COLS), f32),
            vmem((8, 72, COLS), f32),
            vmem((8, 72, COLS), f32),
            vmem((16, 16, COLS), f32),
            vmem((8, 16, COLS), f32),
            vmem((8, 16, COLS), f32),
            vmem((88, COLS), f32),
            dma((8,)), dma((8,)), dma((8,)), dma((8,)), dma((8,)), dma((8,)), dma((8,)), dma((8,)),
            dma((2,)), dma((2,)), dma((2,)), dma((2,)), dma((2,)), dma((2,)),
        ],
        compiler_params=pltpu.CompilerParams(
            collective_id=0, has_side_effects=True, vmem_limit_bytes=48 << 20
        ),
    )(
        *(
            pltpu.with_memory_space_constraint(x, pltpu.HBM)
            for x in (placed, neighbour.T, face.T, orient.T, density, momentum, energy, metrics, volume)
        )
    )
    return pl.pallas_call(
        hand_over,
        out_shape=shapes,
        in_specs=[inside] * 3,
        out_specs=(anywhere,) * 3,
        scratch_shapes=[dma((3,))],
    )(*(pltpu.with_memory_space_constraint(x, pltpu.VMEM) for x in results))


def solution(mesh):
    return jax.shard_map(
        local,
        mesh=mesh,
        in_specs=(
            P("blk", None, "ij", None),
            P("blk", None, None, "ij", None),
            P("blk", None, "ij", None),
            P("blk", None, "ij", None),
            P("blk", "ij", None),
            P(),
            P(),
            P(),
            P(),
        ),
        out_specs=(
            P("blk", None, "ij", None),
            P("blk", None, None, "ij", None),
            P("blk", None, "ij", None),
        ),
        check_vma=False,
    )
```

```python
import functools

import jax
import jax.numpy as jnp
from jax import lax
from jax.experimental import pallas as pl
from jax.experimental.pallas import tpu as pltpu
from jax.sharding import PartitionSpec as P

MESH = pl.DeviceIdType.MESH
pressure_factor = 0.4
viscosity = 0.05
conduction = 0.1
time_step = 0.03
ROWS, COLS, PLANES, CHUNK = 32, 128, 6, 8
Y, Z, CORES, IJ, BLOCKS = 4, 4, 2, 8, 32
LOW, HIGH = slice(6, 8), slice(40, 42)


def lanes(shape):
    return lax.broadcasted_iota(jnp.int32, shape, len(shape) - 1)


def rows_of(shape):
    return lax.broadcasted_iota(jnp.int32, shape, len(shape) - 2)


def shift_lanes(x, by):
    by = by % COLS
    return x if by == 0 else pltpu.roll(x, by, x.ndim - 1)


def primitives(rho, m1, m2, m3, energy, dt):
    inv = 1.0 / rho
    u1, u2, u3 = m1 * inv, m2 * inv, m3 * inv
    kinetic = 0.5 * (m1 * u1 + m2 * u2 + m3 * u3)
    p = pressure_factor * (energy - kinetic)
    head = energy + p
    soft = dt * viscosity / 12.0
    warm = dt * conduction / 12.0
    curved = (soft * u1, soft * u2, soft * u3, inv * (soft * kinetic + warm * p))
    return u1, u2, u3, p, head, curved


def flux(rho, m1, m2, m3, prim, gx, gy):
    u1, u2, u3, p, head, _ = prim
    speed = gx * u1 + gy * u2
    return (rho * speed, m1 * speed + gx * p, m2 * speed + gy * p, m3 * speed, head * speed)


def flux_planes(m1, m2, m3, prim):
    u1, u2, u3, p, head, _ = prim
    return (m3, m1 * u3, m2 * u3, m3 * u3 + p, head * u3)


def slope(b2, b1, a1, a2):
    return 8.0 * (a1 - b1) - (a2 - b2)


def curve(b2, b1, a1, a2):
    return 16.0 * (a1 + b1) - (a2 + b2)


def plane_shift(f, by):
    by = by % PLANES
    return jnp.concatenate([f[by:], f[:by]], axis=0)


def span(c):
    return slice(CHUNK + c * CHUNK, 2 * CHUNK + c * CHUNK)


def chunk_metrics(exm, c, dt):
    ax, ay, bx, by, v = (exm[n, span(c), :] for n in range(5))
    return (v * ax, v * ay, v * bx, v * by, (dt / 12.0) / v, ax * ax + ay * ay, bx * bx + by * by)


def before_ghosts(state, exm, fi, wi, part, dt, chunks):
    for c in chunks:
        gax, gay, gbx, gby, iv, rw, cw = chunk_metrics(exm, c, dt)
        center = -30.0 * (rw + cw + 1.0)
        rho, m1, m2, m3, energy = (state[ch, :, span(c), :] for ch in range(5))
        prim = primitives(rho, m1, m2, m3, energy, dt)
        curved = prim[5]
        inner = span(c + 1)
        for ch, f in enumerate(flux(rho, m1, m2, m3, prim, gax, gay)):
            fi[ch, :, inner, :] = f
        for n, w in enumerate(curved):
            wi[n, :, inner, :] = w
        fj = flux(rho, m1, m2, m3, prim, gbx, gby)
        fk = flux_planes(m1, m2, m3, prim)
        for ch in range(5):
            f, g = fj[ch], fk[ch]
            dj = slope(*(shift_lanes(f, by) for by in (2, 1, -1, -2)))
            dk = slope(*(plane_shift(g, by) for by in (-2, -1, 1, 2)))
            total = -(dj * iv) - (dt / 12.0) * dk
            if ch > 0:
                w = curved[ch - 1]
                sj = curve(*(shift_lanes(w, by) for by in (2, 1, -1, -2)))
                sk = curve(*(plane_shift(w, by) for by in (-2, -1, 1, 2)))
                total = total + cw * sj + sk + center * w
            part[ch, :, span(c), :] = total


def row_terms(exm, fi, wi, part, c, ch, dt):
    gax, gay, gbx, gby, iv, rw, cw = chunk_metrics(exm, c, dt)
    base = 2 * CHUNK + c * CHUNK
    di = slope(*(fi[ch, :, base + d : base + d + CHUNK, :] for d in (-2, -1, 1, 2)))
    total = part[ch, :, span(c), :] - di * iv
    if ch > 0:
        si = curve(*(wi[ch - 1, :, base + d : base + d + CHUNK, :] for d in (-2, -1, 1, 2)))
        total = total + rw * si
    return total


def apart(a, b):
    third = jnp.where(lanes(a.shape) < 32, shift_lanes(a, -96), shift_lanes(b, 32))
    return [a, shift_lanes(a, -48), third, shift_lanes(b, -16), shift_lanes(b, -64)]


def spread(x):
    x = jnp.where((lanes(x.shape) & 63) < 8, x, 0.0)
    pair = x + shift_lanes(x, 8)
    return pair + shift_lanes(pair, 16) + shift_lanes(pair, 32)


def lines(own, ghost):
    near = (lanes(own.shape) & 7) < 4
    first = jnp.where(near, ghost, own)
    second = jnp.where(near, own, ghost)
    return jnp.where(lanes(own.shape) < 64, first, shift_lanes(second, 64))


def line_planes(x, by):
    m = lanes(x.shape) & 63
    if by > 0:
        return jnp.where(m < 48 - 8 * by, shift_lanes(x, -8 * by), shift_lanes(x, 48 - 8 * by))
    return jnp.where(m >= -8 * by, shift_lanes(x, -8 * by), shift_lanes(x, -48 - 8 * by))


def edge_terms(mine, theirs):
    upper = (lanes(mine[0].shape) & 7) >= 4
    out = []
    for n in range(9):
        h = theirs[n] - mine[n]
        high, low = jnp.where(upper, h, 0.0), jnp.where(upper, 0.0, h)
        if n < 5:
            left = 8.0 * shift_lanes(high, -1) - shift_lanes(high, -2)
            right = shift_lanes(low, 2) - 8.0 * shift_lanes(low, 1)
        else:
            left = 16.0 * shift_lanes(high, -1) - shift_lanes(high, -2)
            right = 16.0 * shift_lanes(low, 1) - shift_lanes(low, 2)
        out.append(jnp.where(upper, right, left))
    return out


def edge_values(fields, gx, gy, dt):
    rho, m1, m2, m3, energy = fields
    prim = primitives(rho, m1, m2, m3, energy, dt)
    return flux(rho, m1, m2, m3, prim, gx, gy) + prim[5]


def column_metric(c, e):
    return jnp.concatenate([shift_lanes(c, -32 * g - 8 * e) for g in range(4)], axis=0)


def line_section(own, ghost, lf, lines1, dt):
    a, b, c = slice(0, 32), slice(32, 64), slice(64, 72)
    ob, gb = own[b, :], ghost[b, :]
    fields = [lines(o, g) for o, g in zip(apart(own[a, :], ob), apart(ghost[a, :], gb))]
    gbx, gby = (spread(lines(shift_lanes(ob, -n), shift_lanes(gb, -n))) for n in (112, 120))
    oc, gc = own[c, :], ghost[c, :]
    gax, gay, v = (spread(lines(column_metric(oc, e), column_metric(gc, e))) for e in range(3))
    rho, m1, m2, m3, energy = fields
    prim = primitives(rho, m1, m2, m3, energy, dt)
    curved = prim[5]
    for n, f in enumerate(flux(rho, m1, m2, m3, prim, gax, gay) + curved):
        lf[n, span(0).start : span(3).stop, :] = f
    h = (slice(72, 76), slice(76, 80), slice(80, 84))
    oa, ob, od = (own[n, :] for n in h)
    ga, gb, gd = (ghost[n, :] for n in h)
    mine, theirs = apart(oa, ob), apart(ga, gb)
    hax, hay = (spread(lines(shift_lanes(od, -n), shift_lanes(gd, -n))) for n in (0, 8))
    ends = [lines(o, g) for o, g in zip(mine, theirs)]
    end_prim = primitives(*ends, dt)
    for n, f in enumerate(flux(*ends[:4], end_prim, hax, hay) + end_prim[5]):
        lf[n, LOW, :] = f[0:2]
        lf[n, HIGH, :] = f[2:4]
    terms = edge_terms(
        edge_values(mine, *(spread(shift_lanes(ob, -n)) for n in (112, 120)), dt),
        edge_values(theirs, *(spread(shift_lanes(gb, -n)) for n in (112, 120)), dt),
    )
    inv = 1.0 / v
    iv = (dt / 12.0) * inv
    rw = (gax * gax + gay * gay) * (inv * inv)
    cw = (gbx * gbx + gby * gby) * (inv * inv)
    center = -30.0 * (rw + cw + 1.0)
    fj = flux(rho, m1, m2, m3, prim, gbx, gby)
    fk = flux_planes(m1, m2, m3, prim)
    for ch in range(5):
        lines1[ch] = fields[ch] + line_rate(lf, fj, fk, curved, iv, rw, cw, center, ch, dt)
    lines1[5] = gbx
    lines1[6] = gby
    return terms


def pack(ex, exm, strips, relay):
    at = lanes((ROWS, COLS)) >> 3
    inside = slice(CHUNK, CHUNK + ROWS)
    v = exm[4, inside, :]
    for half in range(2):
        acc = jnp.zeros((ROWS, COLS), jnp.float32)
        for n in range(16):
            q = 16 * half + n
            x = ex[q // 6, q % 6, inside, :] if q < 30 else v * exm[q - 28, inside, :]
            acc = jnp.where(at == n, shift_lanes(x, 4 + 8 * n), acc)
        strips[0, 32 * half : 32 * half + 32, :] = acc
    slot = lanes((CHUNK, COLS)) >> 3
    acc = jnp.zeros((CHUNK, COLS), jnp.float32)
    for g in range(4):
        part = exm[4, span(g), :]
        for e in range(3):
            x = part * exm[e, span(g), :] if e < 2 else part
            acc = jnp.where(slot == 4 * g + e, shift_lanes(x, 4 + 32 * g + 8 * e), acc)
    strips[0, 64:72, :] = acc
    for r in range(ROWS):
        for half in (0, 32):
            strips[1, half + 31 - r : half + 32 - r, :] = strips[0, half + r : half + r + 1, :]
    turned = jnp.where((lanes(acc.shape) & 32) == 0, shift_lanes(acc, 32), shift_lanes(acc, -32))
    turned = jnp.where((lanes(acc.shape) & 31) < 16, -turned, turned)
    for r in range(CHUNK):
        strips[1, 71 - r : 72 - r, :] = turned[r : r + 1, :]
    for side, r in ((0, 0), (1, ROWS - 2)):
        relay[side, 0:2, :] = strips[0, r : r + 2, :]
        relay[side, 2:4, :] = strips[0, 32 + r : 34 + r, :]
        relay[side, 4:6, :] = shift_lanes(acc[r % CHUNK : r % CHUNK + 2], -32 * (r // CHUNK))
        relay[side, 6:8, :] = jnp.zeros((2, COLS), jnp.float32)


def pack_ends(relay, arrived, strips, at_start, at_end):
    turn = lanes((1, COLS))
    signs = (
        jnp.where(turn >= 48, -1.0, 1.0),
        jnp.where(turn < 64, -1.0, 1.0),
        jnp.ones((1, COLS), jnp.float32),
    )
    for n in range(3):
        base = 72 + 4 * n
        for r in range(4):
            near = 2 * n + r % 2
            wall = 2 * n + 1 - r % 2
            side = r // 2
            mirror = relay[side, wall : wall + 1, :]
            if side == 0:
                row = jnp.where(at_start, signs[n] * mirror, arrived[side, near : near + 1, :])
            else:
                row = jnp.where(at_end, mirror, arrived[side, near : near + 1, :])
            strips[0, base + r : base + r + 1, :] = row
            strips[1, base + 3 - r : base + 4 - r, :] = -row if n == 2 else row
    for m in range(2):
        strips[m, 84:88, :] = jnp.zeros((4, COLS), jnp.float32)


def walls(state, at_start, at_end):
    for ch in range(5):
        sign = -1.0 if 1 <= ch <= 3 else 1.0
        for r in range(2):
            low, high = slice(7 - r, 8 - r), slice(40 + r, 41 + r)
            mirror = state[ch, :, 8 + r : 9 + r, :]
            state[ch, :, low, :] = jnp.where(at_start, sign * mirror, state[ch, :, low, :])
            mirror = state[ch, :, 39 - r : 40 - r, :]
            state[ch, :, high, :] = jnp.where(at_end, mirror, state[ch, :, high, :])


def metric_walls(exm, at_start, at_end):
    for r in range(2):
        low, high = slice(7 - r, 8 - r), slice(40 + r, 41 + r)
        exm[:, low, :] = jnp.where(at_start, exm[:, 8 + r : 9 + r, :], exm[:, low, :])
        exm[:, high, :] = jnp.where(at_end, exm[:, 39 - r : 40 - r, :], exm[:, high, :])


def halo_rows(state, exm, fi, wi, dt):
    for rows in (LOW, HIGH):
        rho, m1, m2, m3, energy = (state[ch, :, rows, :] for ch in range(5))
        v = exm[4, rows, :]
        prim = primitives(rho, m1, m2, m3, energy, dt)
        target = slice(rows.start + CHUNK, rows.stop + CHUNK)
        for ch, f in enumerate(flux(rho, m1, m2, m3, prim, v * exm[0, rows, :], v * exm[1, rows, :])):
            fi[ch, :, target, :] = f
        for n, w in enumerate(prim[5]):
            wi[n, :, target, :] = w


def gather_lines(planes, shape):
    at = lanes(shape) >> 3
    acc = jnp.zeros(shape, jnp.float32)
    for k, x in enumerate(planes):
        acc = jnp.where(at == k, shift_lanes(x, 8 * k + 2), acc)
        acc = jnp.where(at == 8 + k, shift_lanes(x, 8 * k - 58), acc)
    return acc


def metric_line(x):
    return spread(jnp.where(lanes(x.shape) < 64, shift_lanes(x, 2), shift_lanes(x, -58)))


def line_prepare(sec, exm, inner, inner_ends, metric, metric_ends):
    inside = slice(CHUNK, CHUNK + ROWS)
    for ch in range(5):
        inner[ch] = gather_lines([sec[ch, k, inside, :] for k in range(PLANES)], (ROWS, COLS))
    ax, ay, bx, by, v = (exm[n, inside, :] for n in range(5))
    values = (v * ax, v * ay, v * bx, v * by, 1.0 / v, ax * ax + ay * ay, bx * bx + by * by)
    for n, x in enumerate(values):
        metric[n] = metric_line(x)
    for side, rows in enumerate((LOW, HIGH)):
        at = slice(2 * side, 2 * side + 2)
        for ch in range(5):
            inner_ends[ch, at, :] = gather_lines([sec[ch, k, rows, :] for k in range(PLANES)], (2, COLS))
        ax, ay, bx, by, v = (exm[n, rows, :] for n in range(5))
        for n, x in enumerate((v * ax, v * ay, 1.0 / v, bx * bx + by * by)):
            metric_ends[n, at, :] = metric_line(x)


def line_result(lines1, inner, inner_ends, metric, metric_ends, terms, lf, last, at_start, at_end, before, dt):
    shape = (ROWS, COLS)
    t, left = lanes(shape) & 7, lanes(shape) < 64
    near = t < 4

    def join(p, own):
        return jnp.where(left, jnp.where(near, shift_lanes(p, -2), own), jnp.where(near, own, shift_lanes(p, 2)))

    fields = [join(lines1[ch], inner[ch]) for ch in range(5)]
    gbx, gby = join(lines1[5], metric[2]), join(lines1[6], metric[3])
    gax, gay, inv, rw, cw = (metric[n] for n in (0, 1, 4, 5, 6))
    prim = primitives(*fields, dt)
    curved = prim[5]
    for n, f in enumerate(flux(*fields[:4], prim, gax, gay) + curved):
        lf[n, CHUNK : CHUNK + ROWS, :] = f
    few = slice(0, 4)
    te, le = lanes((4, COLS)) & 7, lanes((4, COLS)) < 64

    def place(e):
        here = jnp.where(le & ((te >> 1) == 1), shift_lanes(e, -2), 0.0)
        return jnp.where(jnp.logical_not(le) & ((te >> 1) == 2), shift_lanes(e, 66), here)

    inv_e, cw_e = metric_ends[2, few, :], metric_ends[3, few, :]
    ends = []
    for ch in range(5):
        h = inner_ends[ch, few, :] - place(terms[ch]) * ((before / 12.0) * inv_e)
        if ch > 0:
            h = h + cw_e * place(terms[4 + ch])
        sign = -1.0 if 1 <= ch <= 3 else 1.0
        f = fields[ch]
        wall = jnp.concatenate([sign * f[1:2], sign * f[0:1], f[31:32], f[30:31]], axis=0)
        r = rows_of((4, COLS))
        use = jnp.where(at_start, 1, 0) * jnp.where(r < 2, 1, 0) + jnp.where(at_end, 1, 0) * jnp.where(r >= 2, 1, 0)
        ends.append(jnp.where(use > 0, wall, h))
    end_prim = primitives(*ends, dt)
    for n, f in enumerate(
        flux(*ends[:4], end_prim, metric_ends[0, few, :], metric_ends[1, few, :]) + end_prim[5]
    ):
        lf[n, LOW, :] = f[0:2]
        lf[n, HIGH, :] = f[2:4]
    iv = (dt / 12.0) * inv
    center = -30.0 * (rw + cw + 1.0)
    fj = flux(*fields[:4], prim, gbx, gby)
    fk = flux_planes(*fields[1:4], prim)
    for ch in range(5):
        value = 0.5 * fields[ch] + line_rate(lf, fj, fk, curved, iv, rw, cw, center, ch, dt)
        last[ch] = jnp.where((t >= 2) & (t < 6), value, shift_lanes(value, -68))


def line_rate(lf, fj, fk, curved, iv, rw, cw, center, ch, dt):
    di = slope(*(lf[ch, CHUNK + d : CHUNK + d + ROWS, :] for d in (-2, -1, 1, 2)))
    dj = slope(*(shift_lanes(fj[ch], by) for by in (2, 1, -1, -2)))
    dk = slope(*(line_planes(fk[ch], by) for by in (-2, -1, 1, 2)))
    value = -((di + dj) * iv) - (dt / 12.0) * dk
    if ch > 0:
        w = curved[ch - 1]
        si = curve(*(lf[4 + ch, CHUNK + d : CHUNK + d + ROWS, :] for d in (-2, -1, 1, 2)))
        sj = curve(*(shift_lanes(w, by) for by in (2, 1, -1, -2)))
        sk = curve(*(line_planes(w, by) for by in (-2, -1, 1, 2)))
        value = value + rw * si + cw * sj + sk + center * w
    return value


def flip(x):
    t = lanes(x.shape) & 7
    for d in (4, 2, 1):
        x = jnp.where((t & d) == 0, shift_lanes(x, -d), shift_lanes(x, d))
    return x


def peers_first(y, z, c, s):
    out = []
    for dz in range(Z):
        for m in range(2):
            blk = (y * Z + lax.rem(z + dz, Z)) * CORES + c
            out.append({"blk": blk, "ij": (IJ - 1 - s) if m else s})
    return out


def peers_second(y, z, c, s):
    out = []
    for dy in range(Y):
        for dc in range(2):
            blk = (lax.rem(y + dy, Y) * Z + z) * CORES + (1 - c if dc else c)
            out.append({"blk": blk, "ij": s})
    return out


def routes(placed, neighbour, face, orient, targets):
    ids = [placed[t["blk"]] for t in targets]
    wanted = [(b, f) for b in ids for f in range(2)]
    nids = [neighbour[f, b] for b, f in wanted]

    def find(p, found):
        held = placed[p]
        return tuple(jnp.where(n == held, p, a) for n, a in zip(nids, found))

    found = lax.fori_loop(0, BLOCKS, find, tuple(jnp.int32(0) for _ in nids))
    return [(q, face[f, b], orient[f, b]) for q, (b, f) in zip(found, wanted)]


def body(
    placed_hbm, neighbour_hbm, face_hbm, orient_hbm, dens_hbm, mom_hbm, ener_hbm, met_hbm, vol_hbm,
    out_d, out_m, out_e,
    placed, neighbour, face, orient, load,
    ex, exm, sec, fi, wi, part, lf, lf2, lines1, last, inner, inner_ends, metric, metric_ends,
    strips, relay, arrived, got, both, picked, got2, both_e, picked_e, got2_e, ghost,
    send1, recv1, send_h, recv_h, send2, recv2, send_f, recv_f, send_e, recv_e, send_r, recv_r, send_m, recv_m,
):
    inside = pl.ds(CHUNK, ROWS)
    fetch = [
        pltpu.make_async_copy(src, dst, load.at[n])
        for n, (src, dst) in enumerate(
            (
                (mom_hbm.at[0], ex.at[pl.ds(1, 3), :, inside]),
                (dens_hbm.at[0], ex.at[0, :, inside]),
                (ener_hbm.at[0], ex.at[4, :, inside]),
                (met_hbm.at[0], exm.at[pl.ds(0, 4), inside]),
                (vol_hbm.at[0], exm.at[4, inside]),
                (placed_hbm, placed),
                (neighbour_hbm, neighbour),
                (face_hbm, face),
                (orient_hbm, orient),
            )
        )
    ]
    for copy in fetch:
        copy.start()
    b, s = lax.axis_index("blk"), lax.axis_index("ij")
    c = lax.rem(b, CORES)
    z = lax.rem(b // CORES, Z)
    y = b // (CORES * Z)
    first, second = peers_first(y, z, c, s), peers_second(y, z, c, s)
    below = {"blk": b, "ij": lax.rem(s + IJ - 1, IJ)}
    above = {"blk": b, "ij": lax.rem(s + 1, IJ)}
    everyone = first[1:] + second[1:] + [below, above]
    barrier = pltpu.get_barrier_semaphore()
    for peer in everyone:
        pl.semaphore_signal(barrier, inc=1, device_id=peer, device_id_type=MESH)
    at_start, at_end = s == 0, s == IJ - 1
    for copy in fetch:
        copy.wait()
    pack(ex, exm, strips, relay)
    pl.semaphore_wait(barrier, len(everyone))

    def send(src, dst, out_sem, in_sem, peer):
        copy = pltpu.make_async_remote_copy(
            src_ref=src, dst_ref=dst, send_sem=out_sem, recv_sem=in_sem,
            device_id=peer, device_id_type=MESH,
        )
        copy.start()
        return copy

    main, ends = pl.ds(0, 72), pl.ds(72, 16)
    beside = (below, above)
    order = (2, 4, 1, 3, 5, 6, 7)
    edges = [
        send(relay.at[n], arrived.at[1 - n], send_e.at[n], recv_e.at[1 - n], beside[n]) for n in range(2)
    ]
    hop1 = {
        k: send(strips.at[k % 2, main], got.at[k, main], send1.at[k], recv1.at[k], first[k]) for k in order
    }
    table = routes(placed, neighbour, face, orient, second)
    before_ghosts(ex, exm, fi, wi, part, time_step, range(4))
    for copy in edges:
        copy.wait_send()
    for n in range(2):
        pltpu.make_async_remote_copy(
            src_ref=relay.at[n], dst_ref=arrived.at[n], send_sem=send_e.at[n], recv_sem=recv_e.at[n],
            device_id=beside[n], device_id_type=MESH,
        ).wait_recv()
    pack_ends(relay, arrived, strips, at_start, at_end)
    hop_ends = {
        k: send(strips.at[k % 2, ends], got.at[k, ends], send_h.at[k], recv_h.at[k], first[k]) for k in order
    }
    slide = []
    for n in range(2):
        src, dst = pl.ds((CHUNK, ROWS + 4)[n], 4), pl.ds((CHUNK + ROWS, 4)[n], 4)
        slide.append(send(exm.at[:, src], exm.at[:, dst], send_m.at[n], recv_m.at[1 - n], beside[n]))
        slide.append(send(ex.at[:, :, src], ex.at[:, :, dst], send_r.at[n], recv_r.at[1 - n], beside[n]))
    main_sign = jnp.where((rows_of((72, COLS)) >= 32) & (rows_of((72, COLS)) < 64) & (lanes((72, COLS)) >= 112), -1.0, 1.0)
    ends_sign = jnp.where(
        (rows_of((16, COLS)) >= 4) & (rows_of((16, COLS)) < 8) & (lanes((16, COLS)) >= 112), -1.0, 1.0
    )
    slots = []
    for q, g, o in table:
        slots.append((lax.rem(z - lax.rem(q // CORES, Z) + Z, Z) * 2 + o, g))
    near = (lanes((72, COLS)) & 7) < 4
    hop2 = []
    for piece, size, sign, copies, variants, chosen, landed, sems in (
        (slice(0, 72), 72, main_sign, hop1, both, picked, got2, (send2, recv2)),
        (slice(72, 88), 16, ends_sign, hop_ends, both_e, picked_e, got2_e, (send_f, recv_f)),
    ):
        for k in (0, 1, 2, 3, 6, 7, 4, 5):
            if k > 0:
                copies[k].wait_recv()
                x = got[k, piece, :]
            else:
                x = strips[0, piece, :]
            variants[k] = x
            variants[8 + k] = flip(x) * sign
        for k in (4, 5, 2, 3, 6, 7, 1, 0):
            parts = []
            for f in range(2):
                slot, g = slots[2 * k + f]
                parts.append(variants[jnp.where(g == f, 8, 0) + slot])
            message = jnp.where(near[:size], parts[0], parts[1])
            if k == 0:
                landed[0] = message
            else:
                chosen[k] = message
                hop2.append(send(chosen.at[k], landed.at[k], sems[0].at[k], sems[1].at[k], second[k]))
    for copy in slide:
        copy.wait_send()
    for n in range(2):
        dst = pl.ds((4, CHUNK + ROWS)[n], 4)
        pltpu.make_async_remote_copy(
            src_ref=exm.at[:, dst], dst_ref=exm.at[:, dst], send_sem=send_m.at[n], recv_sem=recv_m.at[n],
            device_id=beside[n], device_id_type=MESH,
        ).wait_recv()
        pltpu.make_async_remote_copy(
            src_ref=ex.at[:, :, dst], dst_ref=ex.at[:, :, dst], send_sem=send_r.at[n], recv_sem=recv_r.at[n],
            device_id=beside[n], device_id_type=MESH,
        ).wait_recv()
    walls(ex, at_start, at_end)
    metric_walls(exm, at_start, at_end)
    before_ghosts(ex, exm, fi, wi, part, time_step, (-1, 4))
    for n in range(-1, 5):
        for ch in range(5):
            sec[ch, :, span(n), :] = ex[ch, :, span(n), :] + row_terms(exm, fi, wi, part, n, ch, time_step)
    walls(sec, at_start, at_end)
    half = 0.5 * time_step
    line_prepare(sec, exm, inner, inner_ends, metric, metric_ends)
    before_ghosts(sec, exm, fi, wi, part, half, range(4))
    halo_rows(sec, exm, fi, wi, half)

    def output(ch, plane, rows):
        if ch == 0:
            return out_d.at[0, plane, rows]
        if ch == 4:
            return out_e.at[0, plane, rows]
        return out_m.at[0, ch - 1, plane, rows]

    for n in range(4):
        rows = slice(n * CHUNK, (n + 1) * CHUNK)
        for ch in range(5):
            value = 0.5 * (ex[ch, :, span(n), :] + sec[ch, :, span(n), :])
            output(ch, slice(None), rows)[...] = value + row_terms(exm, fi, wi, part, n, ch, half)
    origin = []
    for f in range(2):
        q, g, o = table[f]
        dy = lax.rem(y - q // (CORES * Z) + Y, Y)
        dc = jnp.where(lax.rem(q, CORES) == c, 0, 1)
        origin.append(2 * dy + dc)
    for copy in hop2[:7]:
        copy.wait_recv()
    ghost[0:72, :] = jnp.where(near, got2[origin[0]], got2[origin[1]])
    for copy in hop2[7:]:
        copy.wait_recv()
    ghost[72:88, :] = jnp.where(near[:16], got2_e[origin[0]], got2_e[origin[1]])
    terms = line_section(strips.at[0], ghost, lf, lines1, time_step)
    line_result(
        lines1, inner, inner_ends, metric, metric_ends, terms, lf2, last, at_start, at_end, time_step, half
    )
    at = lanes((CHUNK, COLS))
    border = (at < 4) | (at >= COLS - 4)
    for ch in range(5):
        for n in range(4):
            rows = slice(n * CHUNK, (n + 1) * CHUNK)
            for k in range(PLANES):
                x = shift_lanes(last[ch, rows, :], -8 * k - 2) + 0.5 * ex[ch, k, span(n), :]
                ref = output(ch, k, rows)
                ref[...] = jnp.where(border, x, ref[...])
    for copy in list(hop1.values()) + list(hop_ends.values()) + hop2:
        copy.wait_send()


def hand_over(d, m, e, out_d, out_m, out_e, sems):
    copies = [
        pltpu.make_async_copy(src, dst, sems.at[n])
        for n, (src, dst) in enumerate(((m, out_m), (d, out_d), (e, out_e)))
    ]
    for copy in copies:
        copy.start()
    for copy in copies:
        copy.wait()


def local(density, momentum, energy, metrics, volume, placed, neighbour, face, orient):
    smem, vmem, i32, f32 = pltpu.SMEM, pltpu.VMEM, jnp.int32, jnp.float32
    anywhere = pl.BlockSpec(memory_space=pltpu.HBM)
    inside = pl.BlockSpec(memory_space=pltpu.VMEM)
    dma = pltpu.SemaphoreType.DMA
    padded = ROWS + 2 * CHUNK
    shapes = tuple(jax.ShapeDtypeStruct(x.shape, f32) for x in (density, momentum, energy))
    results = pl.pallas_call(
        body,
        out_shape=shapes,
        in_specs=[anywhere] * 9,
        out_specs=(inside,) * 3,
        scratch_shapes=[
            smem((BLOCKS,), i32), smem((2, BLOCKS), i32), smem((2, BLOCKS), i32), smem((2, BLOCKS), i32),
            dma((9,)),
            vmem((5, PLANES, padded, COLS), f32),
            vmem((5, padded, COLS), f32),
            vmem((5, PLANES, padded, COLS), f32),
            vmem((5, PLANES, padded + 2 * CHUNK, COLS), f32),
            vmem((4, PLANES, padded + 2 * CHUNK, COLS), f32),
            vmem((5, PLANES, padded, COLS), f32),
            vmem((9, padded, COLS), f32),
            vmem((9, padded, COLS), f32),
            vmem((7, ROWS, COLS), f32),
            vmem((5, ROWS, COLS), f32),
            vmem((5, ROWS, COLS), f32),
            vmem((5, CHUNK, COLS), f32),
            vmem((7, ROWS, COLS), f32),
            vmem((4, CHUNK, COLS), f32),
            vmem((2, 88, COLS), f32),
            vmem((2, CHUNK, COLS), f32),
            vmem((2, CHUNK, COLS), f32),
            vmem((8, 88, COLS), f32),
            vmem((16, 72, COLS), f32),
            vmem((8, 72, COLS), f32),
            vmem((8, 72, COLS), f32),
            vmem((16, 16, COLS), f32),
            vmem((8, 16, COLS), f32),
            vmem((8, 16, COLS), f32),
            vmem((88, COLS), f32),
            dma((8,)), dma((8,)), dma((8,)), dma((8,)), dma((8,)), dma((8,)), dma((8,)), dma((8,)),
            dma((2,)), dma((2,)), dma((2,)), dma((2,)), dma((2,)), dma((2,)),
        ],
        compiler_params=pltpu.CompilerParams(
            collective_id=0, has_side_effects=True, vmem_limit_bytes=48 << 20
        ),
    )(
        *(
            pltpu.with_memory_space_constraint(x, pltpu.HBM)
            for x in (placed, neighbour.T, face.T, orient.T, density, momentum, energy, metrics, volume)
        )
    )
    return pl.pallas_call(
        hand_over,
        out_shape=shapes,
        in_specs=[inside] * 3,
        out_specs=(anywhere,) * 3,
        scratch_shapes=[dma((3,))],
    )(*(pltpu.with_memory_space_constraint(x, pltpu.VMEM) for x in results))


def solution(mesh):
    return jax.shard_map(
        local,
        mesh=mesh,
        in_specs=(
            P("blk", None, "ij", None),
            P("blk", None, None, "ij", None),
            P("blk", None, "ij", None),
            P("blk", None, "ij", None),
            P("blk", "ij", None),
            P(),
            P(),
            P(),
            P(),
        ),
        out_specs=(
            P("blk", None, "ij", None),
            P("blk", None, None, "ij", None),
            P("blk", None, "ij", None),
        ),
        check_vma=False,
    )
```

```python
import functools

import jax
import jax.numpy as jnp
from jax import lax
from jax.experimental import pallas as pl
from jax.experimental.pallas import tpu as pltpu
from jax.sharding import PartitionSpec as P

MESH = pl.DeviceIdType.MESH
pressure_factor = 0.4
viscosity = 0.05
conduction = 0.1
time_step = 0.03
ROWS, COLS, PLANES, CHUNK = 32, 128, 6, 8
Y, Z, CORES, IJ, BLOCKS = 4, 4, 2, 8, 32
LOW, HIGH = slice(6, 8), slice(40, 42)


def lanes(shape):
    return lax.broadcasted_iota(jnp.int32, shape, len(shape) - 1)


def rows_of(shape):
    return lax.broadcasted_iota(jnp.int32, shape, len(shape) - 2)


def shift_lanes(x, by):
    by = by % COLS
    return x if by == 0 else pltpu.roll(x, by, x.ndim - 1)


def primitives(rho, m1, m2, m3, energy, dt):
    inv = 1.0 / rho
    u1, u2, u3 = m1 * inv, m2 * inv, m3 * inv
    kinetic = 0.5 * (m1 * u1 + m2 * u2 + m3 * u3)
    p = pressure_factor * (energy - kinetic)
    head = energy + p
    soft = dt * viscosity / 12.0
    warm = dt * conduction / 12.0
    curved = (soft * u1, soft * u2, soft * u3, inv * (soft * kinetic + warm * p))
    return u1, u2, u3, p, head, curved


def flux(rho, m1, m2, m3, prim, gx, gy):
    u1, u2, u3, p, head, _ = prim
    speed = gx * u1 + gy * u2
    return (rho * speed, m1 * speed + gx * p, m2 * speed + gy * p, m3 * speed, head * speed)


def flux_planes(m1, m2, m3, prim):
    u1, u2, u3, p, head, _ = prim
    return (m3, m1 * u3, m2 * u3, m3 * u3 + p, head * u3)


def slope(b2, b1, a1, a2):
    return 8.0 * (a1 - b1) - (a2 - b2)


def curve(b2, b1, a1, a2):
    return 16.0 * (a1 + b1) - (a2 + b2)


def plane_shift(f, by):
    by = by % PLANES
    return jnp.concatenate([f[by:], f[:by]], axis=0)


def span(c):
    return slice(CHUNK + c * CHUNK, 2 * CHUNK + c * CHUNK)


def chunk_metrics(exm, c, dt):
    ax, ay, bx, by, v = (exm[n, span(c), :] for n in range(5))
    return (v * ax, v * ay, v * bx, v * by, (dt / 12.0) / v, ax * ax + ay * ay, bx * bx + by * by)


def before_ghosts(state, exm, fi, wi, part, dt, chunks):
    for c in chunks:
        gax, gay, gbx, gby, iv, rw, cw = chunk_metrics(exm, c, dt)
        center = -30.0 * (rw + cw + 1.0)
        rho, m1, m2, m3, energy = (state[ch, :, span(c), :] for ch in range(5))
        prim = primitives(rho, m1, m2, m3, energy, dt)
        curved = prim[5]
        inner = span(c + 1)
        for ch, f in enumerate(flux(rho, m1, m2, m3, prim, gax, gay)):
            fi[ch, :, inner, :] = f
        for n, w in enumerate(curved):
            wi[n, :, inner, :] = w
        fj = flux(rho, m1, m2, m3, prim, gbx, gby)
        fk = flux_planes(m1, m2, m3, prim)
        for ch in range(5):
            f, g = fj[ch], fk[ch]
            dj = slope(*(shift_lanes(f, by) for by in (2, 1, -1, -2)))
            dk = slope(*(plane_shift(g, by) for by in (-2, -1, 1, 2)))
            total = -(dj * iv) - (dt / 12.0) * dk
            if ch > 0:
                w = curved[ch - 1]
                sj = curve(*(shift_lanes(w, by) for by in (2, 1, -1, -2)))
                sk = curve(*(plane_shift(w, by) for by in (-2, -1, 1, 2)))
                total = total + cw * sj + sk + center * w
            part[ch, :, span(c), :] = total


def row_terms(exm, fi, wi, part, c, ch, dt):
    gax, gay, gbx, gby, iv, rw, cw = chunk_metrics(exm, c, dt)
    base = 2 * CHUNK + c * CHUNK
    di = slope(*(fi[ch, :, base + d : base + d + CHUNK, :] for d in (-2, -1, 1, 2)))
    total = part[ch, :, span(c), :] - di * iv
    if ch > 0:
        si = curve(*(wi[ch - 1, :, base + d : base + d + CHUNK, :] for d in (-2, -1, 1, 2)))
        total = total + rw * si
    return total


def apart(a, b):
    third = jnp.where(lanes(a.shape) < 32, shift_lanes(a, -96), shift_lanes(b, 32))
    return [a, shift_lanes(a, -48), third, shift_lanes(b, -16), shift_lanes(b, -64)]


def spread(x):
    x = jnp.where((lanes(x.shape) & 63) < 8, x, 0.0)
    pair = x + shift_lanes(x, 8)
    return pair + shift_lanes(pair, 16) + shift_lanes(pair, 32)


def lines(own, ghost):
    near = (lanes(own.shape) & 7) < 4
    first = jnp.where(near, ghost, own)
    second = jnp.where(near, own, ghost)
    return jnp.where(lanes(own.shape) < 64, first, shift_lanes(second, 64))


def line_planes(x, by):
    m = lanes(x.shape) & 63
    if by > 0:
        return jnp.where(m < 48 - 8 * by, shift_lanes(x, -8 * by), shift_lanes(x, 48 - 8 * by))
    return jnp.where(m >= -8 * by, shift_lanes(x, -8 * by), shift_lanes(x, -48 - 8 * by))


def edge_terms(mine, theirs):
    upper = (lanes(mine[0].shape) & 7) >= 4
    out = []
    for n in range(9):
        h = theirs[n] - mine[n]
        high, low = jnp.where(upper, h, 0.0), jnp.where(upper, 0.0, h)
        if n < 5:
            left = 8.0 * shift_lanes(high, -1) - shift_lanes(high, -2)
            right = shift_lanes(low, 2) - 8.0 * shift_lanes(low, 1)
        else:
            left = 16.0 * shift_lanes(high, -1) - shift_lanes(high, -2)
            right = 16.0 * shift_lanes(low, 1) - shift_lanes(low, 2)
        out.append(jnp.where(upper, right, left))
    return out


def edge_values(fields, gx, gy, dt):
    rho, m1, m2, m3, energy = fields
    prim = primitives(rho, m1, m2, m3, energy, dt)
    return flux(rho, m1, m2, m3, prim, gx, gy) + prim[5]


def column_metric(c, e):
    return jnp.concatenate([shift_lanes(c, -32 * g - 8 * e) for g in range(4)], axis=0)


def line_own(own, held, held_ends, dt):
    oa, ob, oc = own[0:32, :], own[32:64, :], own[64:72, :]
    for n, x in enumerate(apart(oa, ob)):
        held[n] = x
    held[5], held[6] = shift_lanes(ob, -112), shift_lanes(ob, -120)
    for e in range(3):
        held[7 + e] = column_metric(oc, e)
    few = slice(0, 4)
    oa, ob, od = own[72:76, :], own[76:80, :], own[80:84, :]
    mine = apart(oa, ob)
    values = edge_values(mine, *(spread(shift_lanes(ob, -n)) for n in (112, 120)), dt)
    for n, x in enumerate(tuple(mine) + (od, shift_lanes(od, -8)) + tuple(values)):
        held_ends[n, few, :] = x


def section_main(ghost, held, lf, lines1, keep, dt):
    ga, gb, gc = ghost[0:32, :], ghost[32:64, :], ghost[64:72, :]
    fields = [lines(held[n], x) for n, x in enumerate(apart(ga, gb))]
    gbx, gby = (spread(lines(held[5 + n], shift_lanes(gb, -112 - 8 * n))) for n in range(2))
    gax, gay, v = (spread(lines(held[7 + e], column_metric(gc, e))) for e in range(3))
    prim = primitives(*fields, dt)
    curved = prim[5]
    for n, f in enumerate(flux(*fields[:4], prim, gax, gay) + curved):
        lf[n, CHUNK : CHUNK + ROWS, :] = f
    inv = 1.0 / v
    iv = (dt / 12.0) * inv
    rw = (gax * gax + gay * gay) * (inv * inv)
    cw = (gbx * gbx + gby * gby) * (inv * inv)
    center = -30.0 * (rw + cw + 1.0)
    fj = flux(*fields[:4], prim, gbx, gby)
    fk = flux_planes(*fields[1:4], prim)
    for ch in range(5):
        lines1[ch] = fields[ch] + cross_rate(fj, fk, curved, iv, cw, center, ch, dt)
    lines1[5], lines1[6] = gbx, gby
    keep[0], keep[1] = iv, rw


def section_ends(ghost, held_ends, lf, lines1, keep, dt):
    few = slice(0, 4)
    ga, gb, gd = ghost[72:76, :], ghost[76:80, :], ghost[80:84, :]
    theirs = apart(ga, gb)
    hax, hay = (spread(lines(held_ends[5 + n, few, :], shift_lanes(gd, -8 * n))) for n in range(2))
    ends = [lines(held_ends[n, few, :], x) for n, x in enumerate(theirs)]
    prim = primitives(*ends, dt)
    for n, f in enumerate(flux(*ends[:4], prim, hax, hay) + prim[5]):
        lf[n, LOW, :] = f[0:2]
        lf[n, HIGH, :] = f[2:4]
    for ch in range(5):
        lines1[ch] = lines1[ch] + row_rate(lf, keep[0], keep[1], ch)
    return edge_terms(
        [held_ends[7 + n, few, :] for n in range(9)],
        edge_values(theirs, *(spread(shift_lanes(gb, -n)) for n in (112, 120)), dt),
    )


def pack(ex, exm, strips, relay):
    at = lanes((ROWS, COLS)) >> 3
    inside = slice(CHUNK, CHUNK + ROWS)
    v = exm[4, inside, :]
    for half in range(2):
        acc = jnp.zeros((ROWS, COLS), jnp.float32)
        for n in range(16):
            q = 16 * half + n
            x = ex[q // 6, q % 6, inside, :] if q < 30 else v * exm[q - 28, inside, :]
            acc = jnp.where(at == n, shift_lanes(x, 4 + 8 * n), acc)
        strips[0, 32 * half : 32 * half + 32, :] = acc
    slot = lanes((CHUNK, COLS)) >> 3
    acc = jnp.zeros((CHUNK, COLS), jnp.float32)
    for g in range(4):
        part = exm[4, span(g), :]
        for e in range(3):
            x = part * exm[e, span(g), :] if e < 2 else part
            acc = jnp.where(slot == 4 * g + e, shift_lanes(x, 4 + 32 * g + 8 * e), acc)
    strips[0, 64:72, :] = acc
    for r in range(ROWS):
        for half in (0, 32):
            strips[1, half + 31 - r : half + 32 - r, :] = strips[0, half + r : half + r + 1, :]
    turned = jnp.where((lanes(acc.shape) & 32) == 0, shift_lanes(acc, 32), shift_lanes(acc, -32))
    turned = jnp.where((lanes(acc.shape) & 31) < 16, -turned, turned)
    for r in range(CHUNK):
        strips[1, 71 - r : 72 - r, :] = turned[r : r + 1, :]
    for side, r in ((0, 0), (1, ROWS - 2)):
        relay[side, 0:2, :] = strips[0, r : r + 2, :]
        relay[side, 2:4, :] = strips[0, 32 + r : 34 + r, :]
        relay[side, 4:6, :] = shift_lanes(acc[r % CHUNK : r % CHUNK + 2], -32 * (r // CHUNK))
        relay[side, 6:8, :] = jnp.zeros((2, COLS), jnp.float32)


def pack_ends(relay, arrived, strips, at_start, at_end):
    turn = lanes((1, COLS))
    signs = (
        jnp.where(turn >= 48, -1.0, 1.0),
        jnp.where(turn < 64, -1.0, 1.0),
        jnp.ones((1, COLS), jnp.float32),
    )
    for n in range(3):
        base = 72 + 4 * n
        for r in range(4):
            near = 2 * n + r % 2
            wall = 2 * n + 1 - r % 2
            side = r // 2
            mirror = relay[side, wall : wall + 1, :]
            if side == 0:
                row = jnp.where(at_start, signs[n] * mirror, arrived[side, near : near + 1, :])
            else:
                row = jnp.where(at_end, mirror, arrived[side, near : near + 1, :])
            strips[0, base + r : base + r + 1, :] = row
            strips[1, base + 3 - r : base + 4 - r, :] = -row if n == 2 else row
    for m in range(2):
        strips[m, 84:88, :] = jnp.zeros((4, COLS), jnp.float32)


def walls(state, at_start, at_end):
    for ch in range(5):
        sign = -1.0 if 1 <= ch <= 3 else 1.0
        for r in range(2):
            low, high = slice(7 - r, 8 - r), slice(40 + r, 41 + r)
            mirror = state[ch, :, 8 + r : 9 + r, :]
            state[ch, :, low, :] = jnp.where(at_start, sign * mirror, state[ch, :, low, :])
            mirror = state[ch, :, 39 - r : 40 - r, :]
            state[ch, :, high, :] = jnp.where(at_end, mirror, state[ch, :, high, :])


def metric_walls(exm, at_start, at_end):
    for r in range(2):
        low, high = slice(7 - r, 8 - r), slice(40 + r, 41 + r)
        exm[:, low, :] = jnp.where(at_start, exm[:, 8 + r : 9 + r, :], exm[:, low, :])
        exm[:, high, :] = jnp.where(at_end, exm[:, 39 - r : 40 - r, :], exm[:, high, :])


def halo_rows(state, exm, fi, wi, dt):
    for rows in (LOW, HIGH):
        rho, m1, m2, m3, energy = (state[ch, :, rows, :] for ch in range(5))
        v = exm[4, rows, :]
        prim = primitives(rho, m1, m2, m3, energy, dt)
        target = slice(rows.start + CHUNK, rows.stop + CHUNK)
        for ch, f in enumerate(flux(rho, m1, m2, m3, prim, v * exm[0, rows, :], v * exm[1, rows, :])):
            fi[ch, :, target, :] = f
        for n, w in enumerate(prim[5]):
            wi[n, :, target, :] = w


def gather_lines(planes, shape):
    at = lanes(shape) >> 3
    acc = jnp.zeros(shape, jnp.float32)
    for k, x in enumerate(planes):
        acc = jnp.where(at == k, shift_lanes(x, 8 * k + 2), acc)
        acc = jnp.where(at == 8 + k, shift_lanes(x, 8 * k - 58), acc)
    return acc


def metric_line(x):
    return spread(jnp.where(lanes(x.shape) < 64, shift_lanes(x, 2), shift_lanes(x, -58)))


def line_prepare(sec, exm, inner, inner_ends, metric, metric_ends):
    inside = slice(CHUNK, CHUNK + ROWS)
    for ch in range(5):
        inner[ch] = gather_lines([sec[ch, k, inside, :] for k in range(PLANES)], (ROWS, COLS))
    ax, ay, bx, by, v = (exm[n, inside, :] for n in range(5))
    values = (v * ax, v * ay, v * bx, v * by, 1.0 / v, ax * ax + ay * ay, bx * bx + by * by)
    for n, x in enumerate(values):
        metric[n] = metric_line(x)
    for side, rows in enumerate((LOW, HIGH)):
        at = slice(2 * side, 2 * side + 2)
        for ch in range(5):
            inner_ends[ch, at, :] = gather_lines([sec[ch, k, rows, :] for k in range(PLANES)], (2, COLS))
        ax, ay, bx, by, v = (exm[n, rows, :] for n in range(5))
        for n, x in enumerate((v * ax, v * ay, 1.0 / v, bx * bx + by * by)):
            metric_ends[n, at, :] = metric_line(x)


def line_result(lines1, inner, inner_ends, metric, metric_ends, terms, lf, last, at_start, at_end, before, dt):
    shape = (ROWS, COLS)
    t, left = lanes(shape) & 7, lanes(shape) < 64
    near = t < 4

    def join(p, own):
        return jnp.where(left, jnp.where(near, shift_lanes(p, -2), own), jnp.where(near, own, shift_lanes(p, 2)))

    fields = [join(lines1[ch], inner[ch]) for ch in range(5)]
    gbx, gby = join(lines1[5], metric[2]), join(lines1[6], metric[3])
    gax, gay, inv, rw, cw = (metric[n] for n in (0, 1, 4, 5, 6))
    prim = primitives(*fields, dt)
    curved = prim[5]
    for n, f in enumerate(flux(*fields[:4], prim, gax, gay) + curved):
        lf[n, CHUNK : CHUNK + ROWS, :] = f
    few = slice(0, 4)
    te, le = lanes((4, COLS)) & 7, lanes((4, COLS)) < 64

    def place(e):
        here = jnp.where(le & ((te >> 1) == 1), shift_lanes(e, -2), 0.0)
        return jnp.where(jnp.logical_not(le) & ((te >> 1) == 2), shift_lanes(e, 66), here)

    inv_e, cw_e = metric_ends[2, few, :], metric_ends[3, few, :]
    ends = []
    for ch in range(5):
        h = inner_ends[ch, few, :] - place(terms[ch]) * ((before / 12.0) * inv_e)
        if ch > 0:
            h = h + cw_e * place(terms[4 + ch])
        sign = -1.0 if 1 <= ch <= 3 else 1.0
        f = fields[ch]
        wall = jnp.concatenate([sign * f[1:2], sign * f[0:1], f[31:32], f[30:31]], axis=0)
        r = rows_of((4, COLS))
        use = jnp.where(at_start, 1, 0) * jnp.where(r < 2, 1, 0) + jnp.where(at_end, 1, 0) * jnp.where(r >= 2, 1, 0)
        ends.append(jnp.where(use > 0, wall, h))
    end_prim = primitives(*ends, dt)
    for n, f in enumerate(
        flux(*ends[:4], end_prim, metric_ends[0, few, :], metric_ends[1, few, :]) + end_prim[5]
    ):
        lf[n, LOW, :] = f[0:2]
        lf[n, HIGH, :] = f[2:4]
    iv = (dt / 12.0) * inv
    center = -30.0 * (rw + cw + 1.0)
    fj = flux(*fields[:4], prim, gbx, gby)
    fk = flux_planes(*fields[1:4], prim)
    for ch in range(5):
        value = 0.5 * fields[ch] + row_rate(lf, iv, rw, ch) + cross_rate(fj, fk, curved, iv, cw, center, ch, dt)
        last[ch] = jnp.where((t >= 2) & (t < 6), value, shift_lanes(value, -68))


def row_rate(lf, iv, rw, ch):
    value = -(slope(*(lf[ch, CHUNK + d : CHUNK + d + ROWS, :] for d in (-2, -1, 1, 2))) * iv)
    if ch > 0:
        value = value + rw * curve(*(lf[4 + ch, CHUNK + d : CHUNK + d + ROWS, :] for d in (-2, -1, 1, 2)))
    return value


def cross_rate(fj, fk, curved, iv, cw, center, ch, dt):
    dj = slope(*(shift_lanes(fj[ch], by) for by in (2, 1, -1, -2)))
    dk = slope(*(line_planes(fk[ch], by) for by in (-2, -1, 1, 2)))
    value = -(dj * iv) - (dt / 12.0) * dk
    if ch > 0:
        w = curved[ch - 1]
        sj = curve(*(shift_lanes(w, by) for by in (2, 1, -1, -2)))
        sk = curve(*(line_planes(w, by) for by in (-2, -1, 1, 2)))
        value = value + cw * sj + sk + center * w
    return value


def flip(x):
    t = lanes(x.shape) & 7
    for d in (4, 2, 1):
        x = jnp.where((t & d) == 0, shift_lanes(x, -d), shift_lanes(x, d))
    return x


def peers_first(y, z, c, s):
    out = []
    for dz in range(Z):
        for m in range(2):
            blk = (y * Z + lax.rem(z + dz, Z)) * CORES + c
            out.append({"blk": blk, "ij": (IJ - 1 - s) if m else s})
    return out


def peers_second(y, z, c, s):
    out = []
    for dy in range(Y):
        for dc in range(2):
            blk = (lax.rem(y + dy, Y) * Z + z) * CORES + (1 - c if dc else c)
            out.append({"blk": blk, "ij": s})
    return out


def routes(placed, neighbour, face, orient, targets):
    ids = [placed[t["blk"]] for t in targets]
    wanted = [(b, f) for b in ids for f in range(2)]
    nids = [neighbour[f, b] for b, f in wanted]

    def find(p, found):
        held = placed[p]
        return tuple(jnp.where(n == held, p, a) for n, a in zip(nids, found))

    found = lax.fori_loop(0, BLOCKS, find, tuple(jnp.int32(0) for _ in nids))
    return [(q, face[f, b], orient[f, b]) for q, (b, f) in zip(found, wanted)]


def body(
    placed_hbm, neighbour_hbm, face_hbm, orient_hbm, dens_hbm, mom_hbm, ener_hbm, met_hbm, vol_hbm,
    out_d, out_m, out_e,
    placed, neighbour, face, orient, load,
    ex, exm, sec, fi, wi, part, lf, lf2, lines1, last, inner, inner_ends, metric, metric_ends,
    held, held_ends, keep,
    strips, relay, arrived, got, both, picked, got2, both_e, picked_e, got2_e, ghost,
    send1, recv1, send_h, recv_h, send2, recv2, send_f, recv_f, send_e, recv_e, send_r, recv_r, send_m, recv_m,
):
    inside = pl.ds(CHUNK, ROWS)
    fetch = [
        pltpu.make_async_copy(src, dst, load.at[n])
        for n, (src, dst) in enumerate(
            (
                (mom_hbm.at[0], ex.at[pl.ds(1, 3), :, inside]),
                (dens_hbm.at[0], ex.at[0, :, inside]),
                (ener_hbm.at[0], ex.at[4, :, inside]),
                (met_hbm.at[0], exm.at[pl.ds(0, 4), inside]),
                (vol_hbm.at[0], exm.at[4, inside]),
                (placed_hbm, placed),
                (neighbour_hbm, neighbour),
                (face_hbm, face),
                (orient_hbm, orient),
            )
        )
    ]
    for copy in fetch:
        copy.start()
    b, s = lax.axis_index("blk"), lax.axis_index("ij")
    c = lax.rem(b, CORES)
    z = lax.rem(b // CORES, Z)
    y = b // (CORES * Z)
    first, second = peers_first(y, z, c, s), peers_second(y, z, c, s)
    below = {"blk": b, "ij": lax.rem(s + IJ - 1, IJ)}
    above = {"blk": b, "ij": lax.rem(s + 1, IJ)}
    everyone = first[1:] + second[1:] + [below, above]
    barrier = pltpu.get_barrier_semaphore()
    for peer in everyone:
        pl.semaphore_signal(barrier, inc=1, device_id=peer, device_id_type=MESH)
    at_start, at_end = s == 0, s == IJ - 1
    for copy in fetch:
        copy.wait()
    pack(ex, exm, strips, relay)
    pl.semaphore_wait(barrier, len(everyone))

    def send(src, dst, out_sem, in_sem, peer):
        copy = pltpu.make_async_remote_copy(
            src_ref=src, dst_ref=dst, send_sem=out_sem, recv_sem=in_sem,
            device_id=peer, device_id_type=MESH,
        )
        copy.start()
        return copy

    main, ends = pl.ds(0, 72), pl.ds(72, 16)
    beside = (below, above)
    order = (2, 4, 1, 3, 5, 6, 7)
    edges = [
        send(relay.at[n], arrived.at[1 - n], send_e.at[n], recv_e.at[1 - n], beside[n]) for n in range(2)
    ]
    hop1 = {
        k: send(strips.at[k % 2, main], got.at[k, main], send1.at[k], recv1.at[k], first[k]) for k in order
    }
    table = routes(placed, neighbour, face, orient, second)
    before_ghosts(ex, exm, fi, wi, part, time_step, range(4))
    for copy in edges:
        copy.wait_send()
    for n in range(2):
        pltpu.make_async_remote_copy(
            src_ref=relay.at[n], dst_ref=arrived.at[n], send_sem=send_e.at[n], recv_sem=recv_e.at[n],
            device_id=beside[n], device_id_type=MESH,
        ).wait_recv()
    pack_ends(relay, arrived, strips, at_start, at_end)
    hop_ends = {
        k: send(strips.at[k % 2, ends], got.at[k, ends], send_h.at[k], recv_h.at[k], first[k]) for k in order
    }
    slide = []
    for n in range(2):
        src, dst = pl.ds((CHUNK, ROWS + 4)[n], 4), pl.ds((CHUNK + ROWS, 4)[n], 4)
        slide.append(send(exm.at[:, src], exm.at[:, dst], send_m.at[n], recv_m.at[1 - n], beside[n]))
        slide.append(send(ex.at[:, :, src], ex.at[:, :, dst], send_r.at[n], recv_r.at[1 - n], beside[n]))
    main_sign = jnp.where((rows_of((72, COLS)) >= 32) & (rows_of((72, COLS)) < 64) & (lanes((72, COLS)) >= 112), -1.0, 1.0)
    ends_sign = jnp.where(
        (rows_of((16, COLS)) >= 4) & (rows_of((16, COLS)) < 8) & (lanes((16, COLS)) >= 112), -1.0, 1.0
    )
    slots = []
    for q, g, o in table:
        slots.append((lax.rem(z - lax.rem(q // CORES, Z) + Z, Z) * 2 + o, g))
    near = (lanes((72, COLS)) & 7) < 4
    hop2 = []
    for piece, size, sign, copies, variants, chosen, landed, sems in (
        (slice(0, 72), 72, main_sign, hop1, both, picked, got2, (send2, recv2)),
        (slice(72, 88), 16, ends_sign, hop_ends, both_e, picked_e, got2_e, (send_f, recv_f)),
    ):
        for k in (0, 1, 2, 3, 6, 7, 4, 5):
            if k > 0:
                copies[k].wait_recv()
                x = got[k, piece, :]
            else:
                x = strips[0, piece, :]
            variants[k] = x
            variants[8 + k] = flip(x) * sign
        for k in (4, 5, 2, 3, 6, 7, 1, 0):
            parts = []
            for f in range(2):
                slot, g = slots[2 * k + f]
                parts.append(variants[jnp.where(g == f, 8, 0) + slot])
            message = jnp.where(near[:size], parts[0], parts[1])
            if k == 0:
                landed[0] = message
            else:
                chosen[k] = message
                hop2.append(send(chosen.at[k], landed.at[k], sems[0].at[k], sems[1].at[k], second[k]))
    for copy in slide:
        copy.wait_send()
    for n in range(2):
        dst = pl.ds((4, CHUNK + ROWS)[n], 4)
        pltpu.make_async_remote_copy(
            src_ref=exm.at[:, dst], dst_ref=exm.at[:, dst], send_sem=send_m.at[n], recv_sem=recv_m.at[n],
            device_id=beside[n], device_id_type=MESH,
        ).wait_recv()
        pltpu.make_async_remote_copy(
            src_ref=ex.at[:, :, dst], dst_ref=ex.at[:, :, dst], send_sem=send_r.at[n], recv_sem=recv_r.at[n],
            device_id=beside[n], device_id_type=MESH,
        ).wait_recv()
    walls(ex, at_start, at_end)
    metric_walls(exm, at_start, at_end)
    before_ghosts(ex, exm, fi, wi, part, time_step, (-1, 4))
    for n in range(-1, 5):
        for ch in range(5):
            sec[ch, :, span(n), :] = ex[ch, :, span(n), :] + row_terms(exm, fi, wi, part, n, ch, time_step)
    walls(sec, at_start, at_end)
    half = 0.5 * time_step
    line_prepare(sec, exm, inner, inner_ends, metric, metric_ends)
    before_ghosts(sec, exm, fi, wi, part, half, range(4))
    halo_rows(sec, exm, fi, wi, half)

    def output(ch, plane, rows):
        if ch == 0:
            return out_d.at[0, plane, rows]
        if ch == 4:
            return out_e.at[0, plane, rows]
        return out_m.at[0, ch - 1, plane, rows]

    for n in range(4):
        rows = slice(n * CHUNK, (n + 1) * CHUNK)
        for ch in range(5):
            value = 0.5 * (ex[ch, :, span(n), :] + sec[ch, :, span(n), :])
            output(ch, slice(None), rows)[...] = value + row_terms(exm, fi, wi, part, n, ch, half)
    origin = []
    for f in range(2):
        q, g, o = table[f]
        dy = lax.rem(y - q // (CORES * Z) + Y, Y)
        dc = jnp.where(lax.rem(q, CORES) == c, 0, 1)
        origin.append(2 * dy + dc)
    line_own(strips.at[0], held, held_ends, time_step)
    for copy in hop2[:7]:
        copy.wait_recv()
    ghost[0:72, :] = jnp.where(near, got2[origin[0]], got2[origin[1]])
    section_main(ghost, held, lf, lines1, keep, time_step)
    for copy in hop2[7:]:
        copy.wait_recv()
    ghost[72:88, :] = jnp.where(near[:16], got2_e[origin[0]], got2_e[origin[1]])
    terms = section_ends(ghost, held_ends, lf, lines1, keep, time_step)
    line_result(
        lines1, inner, inner_ends, metric, metric_ends, terms, lf2, last, at_start, at_end, time_step, half
    )
    at = lanes((CHUNK, COLS))
    border = (at < 4) | (at >= COLS - 4)
    for ch in range(5):
        for n in range(4):
            rows = slice(n * CHUNK, (n + 1) * CHUNK)
            for k in range(PLANES):
                x = shift_lanes(last[ch, rows, :], -8 * k - 2) + 0.5 * ex[ch, k, span(n), :]
                ref = output(ch, k, rows)
                ref[...] = jnp.where(border, x, ref[...])
    for copy in list(hop1.values()) + list(hop_ends.values()) + hop2:
        copy.wait_send()


def hand_over(d, m, e, out_d, out_m, out_e, sems):
    copies = [
        pltpu.make_async_copy(src, dst, sems.at[n])
        for n, (src, dst) in enumerate(((m, out_m), (d, out_d), (e, out_e)))
    ]
    for copy in copies:
        copy.start()
    for copy in copies:
        copy.wait()


def local(density, momentum, energy, metrics, volume, placed, neighbour, face, orient):
    smem, vmem, i32, f32 = pltpu.SMEM, pltpu.VMEM, jnp.int32, jnp.float32
    anywhere = pl.BlockSpec(memory_space=pltpu.HBM)
    inside = pl.BlockSpec(memory_space=pltpu.VMEM)
    dma = pltpu.SemaphoreType.DMA
    padded = ROWS + 2 * CHUNK
    shapes = tuple(jax.ShapeDtypeStruct(x.shape, f32) for x in (density, momentum, energy))
    results = pl.pallas_call(
        body,
        out_shape=shapes,
        in_specs=[anywhere] * 9,
        out_specs=(inside,) * 3,
        scratch_shapes=[
            smem((BLOCKS,), i32), smem((2, BLOCKS), i32), smem((2, BLOCKS), i32), smem((2, BLOCKS), i32),
            dma((9,)),
            vmem((5, PLANES, padded, COLS), f32),
            vmem((5, padded, COLS), f32),
            vmem((5, PLANES, padded, COLS), f32),
            vmem((5, PLANES, padded + 2 * CHUNK, COLS), f32),
            vmem((4, PLANES, padded + 2 * CHUNK, COLS), f32),
            vmem((5, PLANES, padded, COLS), f32),
            vmem((9, padded, COLS), f32),
            vmem((9, padded, COLS), f32),
            vmem((7, ROWS, COLS), f32),
            vmem((5, ROWS, COLS), f32),
            vmem((5, ROWS, COLS), f32),
            vmem((5, CHUNK, COLS), f32),
            vmem((7, ROWS, COLS), f32),
            vmem((4, CHUNK, COLS), f32),
            vmem((10, ROWS, COLS), f32),
            vmem((16, CHUNK, COLS), f32),
            vmem((2, ROWS, COLS), f32),
            vmem((2, 88, COLS), f32),
            vmem((2, CHUNK, COLS), f32),
            vmem((2, CHUNK, COLS), f32),
            vmem((8, 88, COLS), f32),
            vmem((16, 72, COLS), f32),
            vmem((8, 72, COLS), f32),
            vmem((8, 72, COLS), f32),
            vmem((16, 16, COLS), f32),
            vmem((8, 16, COLS), f32),
            vmem((8, 16, COLS), f32),
            vmem((88, COLS), f32),
            dma((8,)), dma((8,)), dma((8,)), dma((8,)), dma((8,)), dma((8,)), dma((8,)), dma((8,)),
            dma((2,)), dma((2,)), dma((2,)), dma((2,)), dma((2,)), dma((2,)),
        ],
        compiler_params=pltpu.CompilerParams(
            collective_id=0, has_side_effects=True, vmem_limit_bytes=48 << 20
        ),
    )(
        *(
            pltpu.with_memory_space_constraint(x, pltpu.HBM)
            for x in (placed, neighbour.T, face.T, orient.T, density, momentum, energy, metrics, volume)
        )
    )
    return pl.pallas_call(
        hand_over,
        out_shape=shapes,
        in_specs=[inside] * 3,
        out_specs=(anywhere,) * 3,
        scratch_shapes=[dma((3,))],
    )(*(pltpu.with_memory_space_constraint(x, pltpu.VMEM) for x in results))


def solution(mesh):
    return jax.shard_map(
        local,
        mesh=mesh,
        in_specs=(
            P("blk", None, "ij", None),
            P("blk", None, None, "ij", None),
            P("blk", None, "ij", None),
            P("blk", None, "ij", None),
            P("blk", "ij", None),
            P(),
            P(),
            P(),
            P(),
        ),
        out_specs=(
            P("blk", None, "ij", None),
            P("blk", None, None, "ij", None),
            P("blk", None, "ij", None),
        ),
        check_vma=False,
    )
```

```python
import functools

import jax
import jax.numpy as jnp
from jax import lax
from jax.experimental import pallas as pl
from jax.experimental.pallas import tpu as pltpu
from jax.sharding import PartitionSpec as P

MESH = pl.DeviceIdType.MESH
pressure_factor = 0.4
viscosity = 0.05
conduction = 0.1
time_step = 0.03
ROWS, COLS, PLANES, CHUNK = 32, 128, 6, 8
Y, Z, CORES, IJ, BLOCKS = 4, 4, 2, 8, 32
LOW, HIGH = slice(6, 8), slice(40, 42)


def lanes(shape):
    return lax.broadcasted_iota(jnp.int32, shape, len(shape) - 1)


def rows_of(shape):
    return lax.broadcasted_iota(jnp.int32, shape, len(shape) - 2)


def shift_lanes(x, by):
    by = by % COLS
    return x if by == 0 else pltpu.roll(x, by, x.ndim - 1)


def primitives(rho, m1, m2, m3, energy, dt):
    inv = 1.0 / rho
    u1, u2, u3 = m1 * inv, m2 * inv, m3 * inv
    kinetic = 0.5 * (m1 * u1 + m2 * u2 + m3 * u3)
    p = pressure_factor * (energy - kinetic)
    head = energy + p
    soft = dt * viscosity / 12.0
    warm = dt * conduction / 12.0
    curved = (soft * u1, soft * u2, soft * u3, inv * (soft * kinetic + warm * p))
    return u1, u2, u3, p, head, curved


def flux(rho, m1, m2, m3, prim, gx, gy):
    u1, u2, u3, p, head, _ = prim
    speed = gx * u1 + gy * u2
    return (rho * speed, m1 * speed + gx * p, m2 * speed + gy * p, m3 * speed, head * speed)


def flux_planes(m1, m2, m3, prim):
    u1, u2, u3, p, head, _ = prim
    return (m3, m1 * u3, m2 * u3, m3 * u3 + p, head * u3)


def slope(b2, b1, a1, a2):
    return 8.0 * (a1 - b1) - (a2 - b2)


def curve(b2, b1, a1, a2):
    return 16.0 * (a1 + b1) - (a2 + b2)


def plane_shift(f, by):
    by = by % PLANES
    return jnp.concatenate([f[by:], f[:by]], axis=0)


def span(c):
    return slice(CHUNK + c * CHUNK, 2 * CHUNK + c * CHUNK)


def chunk_metrics(exm, c, dt):
    ax, ay, bx, by, v = (exm[n, span(c), :] for n in range(5))
    return (v * ax, v * ay, v * bx, v * by, (dt / 12.0) / v, ax * ax + ay * ay, bx * bx + by * by)


def before_ghosts(state, exm, fi, wi, part, dt, chunks):
    for c in chunks:
        gax, gay, gbx, gby, iv, rw, cw = chunk_metrics(exm, c, dt)
        center = -30.0 * (rw + cw + 1.0)
        rho, m1, m2, m3, energy = (state[ch, :, span(c), :] for ch in range(5))
        prim = primitives(rho, m1, m2, m3, energy, dt)
        curved = prim[5]
        inner = span(c + 1)
        for ch, f in enumerate(flux(rho, m1, m2, m3, prim, gax, gay)):
            fi[ch, :, inner, :] = f
        for n, w in enumerate(curved):
            wi[n, :, inner, :] = w
        fj = flux(rho, m1, m2, m3, prim, gbx, gby)
        fk = flux_planes(m1, m2, m3, prim)
        for ch in range(5):
            f, g = fj[ch], fk[ch]
            dj = slope(*(shift_lanes(f, by) for by in (2, 1, -1, -2)))
            dk = slope(*(plane_shift(g, by) for by in (-2, -1, 1, 2)))
            total = -(dj * iv) - (dt / 12.0) * dk
            if ch > 0:
                w = curved[ch - 1]
                sj = curve(*(shift_lanes(w, by) for by in (2, 1, -1, -2)))
                sk = curve(*(plane_shift(w, by) for by in (-2, -1, 1, 2)))
                total = total + cw * sj + sk + center * w
            part[ch, :, span(c), :] = total


def row_terms(exm, fi, wi, part, c, ch, dt):
    gax, gay, gbx, gby, iv, rw, cw = chunk_metrics(exm, c, dt)
    base = 2 * CHUNK + c * CHUNK
    di = slope(*(fi[ch, :, base + d : base + d + CHUNK, :] for d in (-2, -1, 1, 2)))
    total = part[ch, :, span(c), :] - di * iv
    if ch > 0:
        si = curve(*(wi[ch - 1, :, base + d : base + d + CHUNK, :] for d in (-2, -1, 1, 2)))
        total = total + rw * si
    return total


def apart(a, b):
    third = jnp.where(lanes(a.shape) < 32, shift_lanes(a, -96), shift_lanes(b, 32))
    return [a, shift_lanes(a, -48), third, shift_lanes(b, -16), shift_lanes(b, -64)]


def spread(x):
    x = jnp.where((lanes(x.shape) & 63) < 8, x, 0.0)
    pair = x + shift_lanes(x, 8)
    return pair + shift_lanes(pair, 16) + shift_lanes(pair, 32)


def lines(own, ghost):
    near = (lanes(own.shape) & 7) < 4
    first = jnp.where(near, ghost, own)
    second = jnp.where(near, own, ghost)
    return jnp.where(lanes(own.shape) < 64, first, shift_lanes(second, 64))


def line_planes(x, by):
    m = lanes(x.shape) & 63
    if by > 0:
        return jnp.where(m < 48 - 8 * by, shift_lanes(x, -8 * by), shift_lanes(x, 48 - 8 * by))
    return jnp.where(m >= -8 * by, shift_lanes(x, -8 * by), shift_lanes(x, -48 - 8 * by))


def edge_terms(mine, theirs):
    upper = (lanes(mine[0].shape) & 7) >= 4
    out = []
    for n in range(9):
        h = theirs[n] - mine[n]
        high, low = jnp.where(upper, h, 0.0), jnp.where(upper, 0.0, h)
        if n < 5:
            left = 8.0 * shift_lanes(high, -1) - shift_lanes(high, -2)
            right = shift_lanes(low, 2) - 8.0 * shift_lanes(low, 1)
        else:
            left = 16.0 * shift_lanes(high, -1) - shift_lanes(high, -2)
            right = 16.0 * shift_lanes(low, 1) - shift_lanes(low, 2)
        out.append(jnp.where(upper, right, left))
    return out


def edge_values(fields, gx, gy, dt):
    rho, m1, m2, m3, energy = fields
    prim = primitives(rho, m1, m2, m3, energy, dt)
    return flux(rho, m1, m2, m3, prim, gx, gy) + prim[5]


def column_metric(c, e):
    return jnp.concatenate([shift_lanes(c, -32 * g - 8 * e) for g in range(4)], axis=0)


def line_own(own, held, held_ends, dt):
    oa, ob, oc = own[0:32, :], own[32:64, :], own[64:72, :]
    for n, x in enumerate(apart(oa, ob)):
        held[n] = x
    held[5], held[6] = shift_lanes(ob, -112), shift_lanes(ob, -120)
    for e in range(3):
        held[7 + e] = column_metric(oc, e)
    few = slice(0, 4)
    oa, ob, od = own[72:76, :], own[76:80, :], own[80:84, :]
    mine = apart(oa, ob)
    values = edge_values(mine, *(spread(shift_lanes(ob, -n)) for n in (112, 120)), dt)
    for n, x in enumerate(tuple(mine) + (od, shift_lanes(od, -8)) + tuple(values)):
        held_ends[n, few, :] = x


def section_main(ghost, held, lf, lines1, keep, dt):
    ga, gb, gc = ghost[0:32, :], ghost[32:64, :], ghost[64:72, :]
    fields = [lines(held[n], x) for n, x in enumerate(apart(ga, gb))]
    gbx, gby = (spread(lines(held[5 + n], shift_lanes(gb, -112 - 8 * n))) for n in range(2))
    gax, gay, v = (spread(lines(held[7 + e], column_metric(gc, e))) for e in range(3))
    prim = primitives(*fields, dt)
    curved = prim[5]
    for n, f in enumerate(flux(*fields[:4], prim, gax, gay) + curved):
        lf[n, CHUNK : CHUNK + ROWS, :] = f
    inv = 1.0 / v
    iv = (dt / 12.0) * inv
    rw = (gax * gax + gay * gay) * (inv * inv)
    cw = (gbx * gbx + gby * gby) * (inv * inv)
    center = -30.0 * (rw + cw + 1.0)
    fj = flux(*fields[:4], prim, gbx, gby)
    fk = flux_planes(*fields[1:4], prim)
    for ch in range(5):
        lines1[ch] = fields[ch] + cross_rate(fj, fk, curved, iv, cw, center, ch, dt)
    lines1[5], lines1[6] = gbx, gby
    keep[0], keep[1] = iv, rw


def section_ends(ghost, held_ends, lf, lines1, keep, dt):
    few = slice(0, 4)
    ga, gb, gd = ghost[72:76, :], ghost[76:80, :], ghost[80:84, :]
    theirs = apart(ga, gb)
    hax, hay = (spread(lines(held_ends[5 + n, few, :], shift_lanes(gd, -8 * n))) for n in range(2))
    ends = [lines(held_ends[n, few, :], x) for n, x in enumerate(theirs)]
    prim = primitives(*ends, dt)
    for n, f in enumerate(flux(*ends[:4], prim, hax, hay) + prim[5]):
        lf[n, LOW, :] = f[0:2]
        lf[n, HIGH, :] = f[2:4]
    for ch in range(5):
        lines1[ch] = lines1[ch] + row_rate(lf, keep[0], keep[1], ch)
    return edge_terms(
        [held_ends[7 + n, few, :] for n in range(9)],
        edge_values(theirs, *(spread(shift_lanes(gb, -n)) for n in (112, 120)), dt),
    )


def pack(ex, exm, strips, relay):
    at = lanes((ROWS, COLS)) >> 3
    inside = slice(CHUNK, CHUNK + ROWS)
    v = exm[4, inside, :]
    for half in range(2):
        acc = jnp.zeros((ROWS, COLS), jnp.float32)
        for n in range(16):
            q = 16 * half + n
            x = ex[q // 6, q % 6, inside, :] if q < 30 else v * exm[q - 28, inside, :]
            acc = jnp.where(at == n, shift_lanes(x, 4 + 8 * n), acc)
        strips[0, 32 * half : 32 * half + 32, :] = acc
    slot = lanes((CHUNK, COLS)) >> 3
    acc = jnp.zeros((CHUNK, COLS), jnp.float32)
    for g in range(4):
        part = exm[4, span(g), :]
        for e in range(3):
            x = part * exm[e, span(g), :] if e < 2 else part
            acc = jnp.where(slot == 4 * g + e, shift_lanes(x, 4 + 32 * g + 8 * e), acc)
    strips[0, 64:72, :] = acc
    for side, r in ((0, 0), (1, ROWS - 2)):
        relay[side, 0:2, :] = strips[0, r : r + 2, :]
        relay[side, 2:4, :] = strips[0, 32 + r : 34 + r, :]
        relay[side, 4:6, :] = shift_lanes(acc[r % CHUNK : r % CHUNK + 2], -32 * (r // CHUNK))
        relay[side, 6:8, :] = jnp.zeros((2, COLS), jnp.float32)
    return acc


def turn_strips(strips, acc):
    for r in range(ROWS):
        for half in (0, 32):
            strips[1, half + 31 - r : half + 32 - r, :] = strips[0, half + r : half + r + 1, :]
    turned = jnp.where((lanes(acc.shape) & 32) == 0, shift_lanes(acc, 32), shift_lanes(acc, -32))
    turned = jnp.where((lanes(acc.shape) & 31) < 16, -turned, turned)
    for r in range(CHUNK):
        strips[1, 71 - r : 72 - r, :] = turned[r : r + 1, :]


def pack_ends(relay, arrived, strips, at_start, at_end):
    turn = lanes((1, COLS))
    signs = (
        jnp.where(turn >= 48, -1.0, 1.0),
        jnp.where(turn < 64, -1.0, 1.0),
        jnp.ones((1, COLS), jnp.float32),
    )
    for n in range(3):
        base = 72 + 4 * n
        for r in range(4):
            near = 2 * n + r % 2
            wall = 2 * n + 1 - r % 2
            side = r // 2
            mirror = relay[side, wall : wall + 1, :]
            if side == 0:
                row = jnp.where(at_start, signs[n] * mirror, arrived[side, near : near + 1, :])
            else:
                row = jnp.where(at_end, mirror, arrived[side, near : near + 1, :])
            strips[0, base + r : base + r + 1, :] = row
            strips[1, base + 3 - r : base + 4 - r, :] = -row if n == 2 else row
    for m in range(2):
        strips[m, 84:88, :] = jnp.zeros((4, COLS), jnp.float32)


def walls(state, at_start, at_end):
    for ch in range(5):
        sign = -1.0 if 1 <= ch <= 3 else 1.0
        for r in range(2):
            low, high = slice(7 - r, 8 - r), slice(40 + r, 41 + r)
            mirror = state[ch, :, 8 + r : 9 + r, :]
            state[ch, :, low, :] = jnp.where(at_start, sign * mirror, state[ch, :, low, :])
            mirror = state[ch, :, 39 - r : 40 - r, :]
            state[ch, :, high, :] = jnp.where(at_end, mirror, state[ch, :, high, :])


def metric_walls(exm, at_start, at_end):
    for r in range(2):
        low, high = slice(7 - r, 8 - r), slice(40 + r, 41 + r)
        exm[:, low, :] = jnp.where(at_start, exm[:, 8 + r : 9 + r, :], exm[:, low, :])
        exm[:, high, :] = jnp.where(at_end, exm[:, 39 - r : 40 - r, :], exm[:, high, :])


def halo_rows(state, exm, fi, wi, dt):
    for rows in (LOW, HIGH):
        rho, m1, m2, m3, energy = (state[ch, :, rows, :] for ch in range(5))
        v = exm[4, rows, :]
        prim = primitives(rho, m1, m2, m3, energy, dt)
        target = slice(rows.start + CHUNK, rows.stop + CHUNK)
        for ch, f in enumerate(flux(rho, m1, m2, m3, prim, v * exm[0, rows, :], v * exm[1, rows, :])):
            fi[ch, :, target, :] = f
        for n, w in enumerate(prim[5]):
            wi[n, :, target, :] = w


def gather_lines(planes, shape):
    at = lanes(shape) >> 3
    acc = jnp.zeros(shape, jnp.float32)
    for k, x in enumerate(planes):
        acc = jnp.where(at == k, shift_lanes(x, 8 * k + 2), acc)
        acc = jnp.where(at == 8 + k, shift_lanes(x, 8 * k - 58), acc)
    return acc


def metric_line(x):
    return spread(jnp.where(lanes(x.shape) < 64, shift_lanes(x, 2), shift_lanes(x, -58)))


def line_prepare(sec, exm, inner, inner_ends, metric, metric_ends):
    inside = slice(CHUNK, CHUNK + ROWS)
    for ch in range(5):
        inner[ch] = gather_lines([sec[ch, k, inside, :] for k in range(PLANES)], (ROWS, COLS))
    ax, ay, bx, by, v = (exm[n, inside, :] for n in range(5))
    values = (v * ax, v * ay, v * bx, v * by, 1.0 / v, ax * ax + ay * ay, bx * bx + by * by)
    for n, x in enumerate(values):
        metric[n] = metric_line(x)
    for side, rows in enumerate((LOW, HIGH)):
        at = slice(2 * side, 2 * side + 2)
        for ch in range(5):
            inner_ends[ch, at, :] = gather_lines([sec[ch, k, rows, :] for k in range(PLANES)], (2, COLS))
        ax, ay, bx, by, v = (exm[n, rows, :] for n in range(5))
        for n, x in enumerate((v * ax, v * ay, 1.0 / v, bx * bx + by * by)):
            metric_ends[n, at, :] = metric_line(x)


def line_result(lines1, inner, inner_ends, metric, metric_ends, terms, lf, last, at_start, at_end, before, dt):
    shape = (ROWS, COLS)
    t, left = lanes(shape) & 7, lanes(shape) < 64
    near = t < 4

    def join(p, own):
        return jnp.where(left, jnp.where(near, shift_lanes(p, -2), own), jnp.where(near, own, shift_lanes(p, 2)))

    fields = [join(lines1[ch], inner[ch]) for ch in range(5)]
    gbx, gby = join(lines1[5], metric[2]), join(lines1[6], metric[3])
    gax, gay, inv, rw, cw = (metric[n] for n in (0, 1, 4, 5, 6))
    prim = primitives(*fields, dt)
    curved = prim[5]
    for n, f in enumerate(flux(*fields[:4], prim, gax, gay) + curved):
        lf[n, CHUNK : CHUNK + ROWS, :] = f
    few = slice(0, 4)
    te, le = lanes((4, COLS)) & 7, lanes((4, COLS)) < 64

    def place(e):
        here = jnp.where(le & ((te >> 1) == 1), shift_lanes(e, -2), 0.0)
        return jnp.where(jnp.logical_not(le) & ((te >> 1) == 2), shift_lanes(e, 66), here)

    inv_e, cw_e = metric_ends[2, few, :], metric_ends[3, few, :]
    ends = []
    for ch in range(5):
        h = inner_ends[ch, few, :] - place(terms[ch]) * ((before / 12.0) * inv_e)
        if ch > 0:
            h = h + cw_e * place(terms[4 + ch])
        sign = -1.0 if 1 <= ch <= 3 else 1.0
        f = fields[ch]
        wall = jnp.concatenate([sign * f[1:2], sign * f[0:1], f[31:32], f[30:31]], axis=0)
        r = rows_of((4, COLS))
        use = jnp.where(at_start, 1, 0) * jnp.where(r < 2, 1, 0) + jnp.where(at_end, 1, 0) * jnp.where(r >= 2, 1, 0)
        ends.append(jnp.where(use > 0, wall, h))
    end_prim = primitives(*ends, dt)
    for n, f in enumerate(
        flux(*ends[:4], end_prim, metric_ends[0, few, :], metric_ends[1, few, :]) + end_prim[5]
    ):
        lf[n, LOW, :] = f[0:2]
        lf[n, HIGH, :] = f[2:4]
    iv = (dt / 12.0) * inv
    center = -30.0 * (rw + cw + 1.0)
    fj = flux(*fields[:4], prim, gbx, gby)
    fk = flux_planes(*fields[1:4], prim)
    for ch in range(5):
        value = 0.5 * fields[ch] + row_rate(lf, iv, rw, ch) + cross_rate(fj, fk, curved, iv, cw, center, ch, dt)
        last[ch] = jnp.where((t >= 2) & (t < 6), value, shift_lanes(value, -68))


def row_rate(lf, iv, rw, ch):
    value = -(slope(*(lf[ch, CHUNK + d : CHUNK + d + ROWS, :] for d in (-2, -1, 1, 2))) * iv)
    if ch > 0:
        value = value + rw * curve(*(lf[4 + ch, CHUNK + d : CHUNK + d + ROWS, :] for d in (-2, -1, 1, 2)))
    return value


def cross_rate(fj, fk, curved, iv, cw, center, ch, dt):
    dj = slope(*(shift_lanes(fj[ch], by) for by in (2, 1, -1, -2)))
    dk = slope(*(line_planes(fk[ch], by) for by in (-2, -1, 1, 2)))
    value = -(dj * iv) - (dt / 12.0) * dk
    if ch > 0:
        w = curved[ch - 1]
        sj = curve(*(shift_lanes(w, by) for by in (2, 1, -1, -2)))
        sk = curve(*(line_planes(w, by) for by in (-2, -1, 1, 2)))
        value = value + cw * sj + sk + center * w
    return value


def exchange_lanes(x, distances):
    t = lanes(x.shape) & 7
    for d in distances:
        x = jnp.where((t & d) == 0, shift_lanes(x, -d), shift_lanes(x, d))
    return x


def settle(x, sign, table):
    same = [jnp.where(table[f][1] == f, 1, 0) for f in range(2)]
    turned = jnp.where((lanes(x.shape) & 7) < 4, same[0], same[1]) > 0
    return jnp.where(turned, exchange_lanes(x, (2, 1)) * sign, x)


def peers_first(y, z, c, s):
    out = []
    for dy in range(Y):
        for m in range(2):
            blk = (lax.rem(y + dy, Y) * Z + z) * CORES + c
            out.append({"blk": blk, "ij": (IJ - 1 - s) if m else s})
    return out


def peers_second(y, z, c, s):
    out = []
    for dz in range(Z):
        for dc in range(2):
            blk = (y * Z + lax.rem(z + dz, Z)) * CORES + (1 - c if dc else c)
            out.append({"blk": blk, "ij": s})
    return out


def routes(placed, neighbour, face, orient, targets):
    ids = [placed[t["blk"]] for t in targets]
    wanted = [(b, f) for b in ids for f in range(2)]
    nids = [neighbour[f, b] for b, f in wanted]

    def find(p, found):
        held = placed[p]
        return tuple(jnp.where(n == held, p, a) for n, a in zip(nids, found))

    found = lax.fori_loop(0, BLOCKS, find, tuple(jnp.int32(0) for _ in nids))
    return [(q, face[f, b], orient[f, b]) for q, (b, f) in zip(found, wanted)]


def body(
    placed_hbm, neighbour_hbm, face_hbm, orient_hbm, dens_hbm, mom_hbm, ener_hbm, met_hbm, vol_hbm,
    out_d, out_m, out_e, last,
    placed, neighbour, face, orient, load,
    ex, exm, sec, fi, wi, part, lf, lf2, lines1, inner, inner_ends, metric, metric_ends,
    held, held_ends, keep,
    strips, relay, arrived, got, both, picked, got2, both_e, picked_e, got2_e, ghost,
    send1, recv1, send_h, recv_h, send2, recv2, send_f, recv_f, send_e, recv_e, send_r, recv_r, send_m, recv_m,
):
    inside = pl.ds(CHUNK, ROWS)
    fetch = [
        pltpu.make_async_copy(src, dst, load.at[n])
        for n, (src, dst) in enumerate(
            (
                (mom_hbm.at[0], ex.at[pl.ds(1, 3), :, inside]),
                (dens_hbm.at[0], ex.at[0, :, inside]),
                (ener_hbm.at[0], ex.at[4, :, inside]),
                (met_hbm.at[0], exm.at[pl.ds(0, 4), inside]),
                (vol_hbm.at[0], exm.at[4, inside]),
                (placed_hbm, placed),
                (neighbour_hbm, neighbour),
                (face_hbm, face),
                (orient_hbm, orient),
            )
        )
    ]
    for copy in fetch:
        copy.start()
    b, s = lax.axis_index("blk"), lax.axis_index("ij")
    c = lax.rem(b, CORES)
    z = lax.rem(b // CORES, Z)
    y = b // (CORES * Z)
    first, second = peers_first(y, z, c, s), peers_second(y, z, c, s)
    below = {"blk": b, "ij": lax.rem(s + IJ - 1, IJ)}
    above = {"blk": b, "ij": lax.rem(s + 1, IJ)}
    everyone = first[1:] + second[1:] + [below, above]
    barrier = pltpu.get_barrier_semaphore()
    for peer in everyone:
        pl.semaphore_signal(barrier, inc=1, device_id=peer, device_id_type=MESH)
    at_start, at_end = s == 0, s == IJ - 1
    for copy in fetch[:5]:
        copy.wait()
    acc = pack(ex, exm, strips, relay)
    pl.semaphore_wait(barrier, len(everyone))

    def send(src, dst, out_sem, in_sem, peer):
        copy = pltpu.make_async_remote_copy(
            src_ref=src, dst_ref=dst, send_sem=out_sem, recv_sem=in_sem,
            device_id=peer, device_id_type=MESH,
        )
        copy.start()
        return copy

    main, ends = pl.ds(0, 72), pl.ds(72, 16)
    beside = (below, above)
    order = (2, 4, 1, 3, 5, 6, 7)
    edges = [
        send(relay.at[n], arrived.at[1 - n], send_e.at[n], recv_e.at[1 - n], beside[n]) for n in range(2)
    ]
    hop1 = {}
    for k in (4, 2, 6, 5, 3, 7, 1):
        if k == 5:
            turn_strips(strips, acc)
        hop1[k] = send(strips.at[k % 2, main], got.at[k, main], send1.at[k], recv1.at[k], first[k])
    for copy in fetch[5:]:
        copy.wait()
    table = routes(placed, neighbour, face, orient, second)
    before_ghosts(ex, exm, fi, wi, part, time_step, range(4))
    for copy in edges:
        copy.wait_send()
    for n in range(2):
        pltpu.make_async_remote_copy(
            src_ref=relay.at[n], dst_ref=arrived.at[n], send_sem=send_e.at[n], recv_sem=recv_e.at[n],
            device_id=beside[n], device_id_type=MESH,
        ).wait_recv()
    pack_ends(relay, arrived, strips, at_start, at_end)
    hop_ends = {
        k: send(strips.at[k % 2, ends], got.at[k, ends], send_h.at[k], recv_h.at[k], first[k]) for k in order
    }
    slide = []
    for n in range(2):
        src, dst = pl.ds((CHUNK, ROWS + 4)[n], 4), pl.ds((CHUNK + ROWS, 4)[n], 4)
        slide.append(send(exm.at[:, src], exm.at[:, dst], send_m.at[n], recv_m.at[1 - n], beside[n]))
        slide.append(send(ex.at[:, :, src], ex.at[:, :, dst], send_r.at[n], recv_r.at[1 - n], beside[n]))
    main_sign = jnp.where((rows_of((72, COLS)) >= 32) & (rows_of((72, COLS)) < 64) & (lanes((72, COLS)) >= 112), -1.0, 1.0)
    ends_sign = jnp.where(
        (rows_of((16, COLS)) >= 4) & (rows_of((16, COLS)) < 8) & (lanes((16, COLS)) >= 112), -1.0, 1.0
    )
    slots = []
    for q, g, o in table:
        slots.append((lax.rem(y - q // (CORES * Z) + Y, Y) * 2 + o, g))
    near = (lanes((72, COLS)) & 7) < 4
    hop2 = []
    for piece, size, copies, variants, chosen, landed, sems in (
        (slice(0, 72), 72, hop1, both, picked, got2, (send2, recv2)),
        (slice(72, 88), 16, hop_ends, both_e, picked_e, got2_e, (send_f, recv_f)),
    ):
        for k in (0, 1, 2, 3, 6, 7, 4, 5):
            if k > 0:
                copies[k].wait_recv()
                x = got[k, piece, :]
            else:
                x = strips[0, piece, :]
            variants[k] = x
            variants[8 + k] = exchange_lanes(x, (4,))
        for k in (4, 5, 2, 3, 6, 7, 1, 0):
            parts = []
            for f in range(2):
                slot, g = slots[2 * k + f]
                parts.append(variants[jnp.where(g == f, 8, 0) + slot])
            message = jnp.where(near[:size], parts[0], parts[1])
            if k == 0:
                landed[0] = message
            else:
                chosen[k] = message
                hop2.append(send(chosen.at[k], landed.at[k], sems[0].at[k], sems[1].at[k], second[k]))
    for copy in slide:
        copy.wait_send()
    for n in range(2):
        dst = pl.ds((4, CHUNK + ROWS)[n], 4)
        pltpu.make_async_remote_copy(
            src_ref=exm.at[:, dst], dst_ref=exm.at[:, dst], send_sem=send_m.at[n], recv_sem=recv_m.at[n],
            device_id=beside[n], device_id_type=MESH,
        ).wait_recv()
        pltpu.make_async_remote_copy(
            src_ref=ex.at[:, :, dst], dst_ref=ex.at[:, :, dst], send_sem=send_r.at[n], recv_sem=recv_r.at[n],
            device_id=beside[n], device_id_type=MESH,
        ).wait_recv()
    walls(ex, at_start, at_end)
    metric_walls(exm, at_start, at_end)
    before_ghosts(ex, exm, fi, wi, part, time_step, (-1, 4))
    for n in range(-1, 5):
        for ch in range(5):
            sec[ch, :, span(n), :] = ex[ch, :, span(n), :] + row_terms(exm, fi, wi, part, n, ch, time_step)
    walls(sec, at_start, at_end)
    half = 0.5 * time_step
    line_prepare(sec, exm, inner, inner_ends, metric, metric_ends)
    before_ghosts(sec, exm, fi, wi, part, half, range(4))
    halo_rows(sec, exm, fi, wi, half)

    def output(ch, plane, rows):
        if ch == 0:
            return out_d.at[0, plane, rows]
        if ch == 4:
            return out_e.at[0, plane, rows]
        return out_m.at[0, ch - 1, plane, rows]

    for n in range(4):
        rows = slice(n * CHUNK, (n + 1) * CHUNK)
        for ch in range(5):
            value = 0.5 * (ex[ch, :, span(n), :] + sec[ch, :, span(n), :])
            value = value + row_terms(exm, fi, wi, part, n, ch, half)
            at = lanes(value.shape)
            border = (at < 4) | (at >= COLS - 4)
            output(ch, slice(None), rows)[...] = jnp.where(border, 0.5 * ex[ch, :, span(n), :], value)
    origin = []
    for f in range(2):
        q, g, o = table[f]
        dz = lax.rem(z - lax.rem(q // CORES, Z) + Z, Z)
        dc = jnp.where(lax.rem(q, CORES) == c, 0, 1)
        origin.append(2 * dz + dc)
    line_own(strips.at[0], held, held_ends, time_step)
    for copy in hop2[:7]:
        copy.wait_recv()
    ghost[0:72, :] = settle(jnp.where(near, got2[origin[0]], got2[origin[1]]), main_sign, table)
    section_main(ghost, held, lf, lines1, keep, time_step)
    for copy in hop2[7:]:
        copy.wait_recv()
    ghost[72:88, :] = settle(jnp.where(near[:16], got2_e[origin[0]], got2_e[origin[1]]), ends_sign, table)
    terms = section_ends(ghost, held_ends, lf, lines1, keep, time_step)
    line_result(
        lines1, inner, inner_ends, metric, metric_ends, terms, lf2, last, at_start, at_end, time_step, half
    )
    for copy in list(hop1.values()) + list(hop_ends.values()) + hop2:
        copy.wait_send()


def hand_over(d, m, e, last, out_d, out_m, out_e, result, sems):
    at = lanes((ROWS, COLS))
    border = (at < 4) | (at >= COLS - 4)
    copies = []
    for ch in (1, 2, 3, 0, 4):
        source = d.at[0] if ch == 0 else e.at[0] if ch == 4 else m.at[0, ch - 1]
        target = out_d.at[0] if ch == 0 else out_e.at[0] if ch == 4 else out_m.at[0, ch - 1]
        for k in range(PLANES):
            x = shift_lanes(last[ch], -8 * k - 2)
            result[ch, k] = source[k] + jnp.where(border, x, 0.0)
        copies.append(pltpu.make_async_copy(result.at[ch], target, sems.at[ch]))
        copies[-1].start()
    for copy in copies:
        copy.wait()


def local(density, momentum, energy, metrics, volume, placed, neighbour, face, orient):
    smem, vmem, i32, f32 = pltpu.SMEM, pltpu.VMEM, jnp.int32, jnp.float32
    anywhere = pl.BlockSpec(memory_space=pltpu.HBM)
    inside = pl.BlockSpec(memory_space=pltpu.VMEM)
    dma = pltpu.SemaphoreType.DMA
    padded = ROWS + 2 * CHUNK
    shapes = tuple(jax.ShapeDtypeStruct(x.shape, f32) for x in (density, momentum, energy))
    results = pl.pallas_call(
        body,
        out_shape=shapes + (jax.ShapeDtypeStruct((5, ROWS, COLS), f32),),
        in_specs=[anywhere] * 9,
        out_specs=(inside,) * 4,
        scratch_shapes=[
            smem((BLOCKS,), i32), smem((2, BLOCKS), i32), smem((2, BLOCKS), i32), smem((2, BLOCKS), i32),
            dma((9,)),
            vmem((5, PLANES, padded, COLS), f32),
            vmem((5, padded, COLS), f32),
            vmem((5, PLANES, padded, COLS), f32),
            vmem((5, PLANES, padded + 2 * CHUNK, COLS), f32),
            vmem((4, PLANES, padded + 2 * CHUNK, COLS), f32),
            vmem((5, PLANES, padded, COLS), f32),
            vmem((9, padded, COLS), f32),
            vmem((9, padded, COLS), f32),
            vmem((7, ROWS, COLS), f32),
            vmem((5, ROWS, COLS), f32),
            vmem((5, CHUNK, COLS), f32),
            vmem((7, ROWS, COLS), f32),
            vmem((4, CHUNK, COLS), f32),
            vmem((10, ROWS, COLS), f32),
            vmem((16, CHUNK, COLS), f32),
            vmem((2, ROWS, COLS), f32),
            vmem((2, 88, COLS), f32),
            vmem((2, CHUNK, COLS), f32),
            vmem((2, CHUNK, COLS), f32),
            vmem((8, 88, COLS), f32),
            vmem((16, 72, COLS), f32),
            vmem((8, 72, COLS), f32),
            vmem((8, 72, COLS), f32),
            vmem((16, 16, COLS), f32),
            vmem((8, 16, COLS), f32),
            vmem((8, 16, COLS), f32),
            vmem((88, COLS), f32),
            dma((8,)), dma((8,)), dma((8,)), dma((8,)), dma((8,)), dma((8,)), dma((8,)), dma((8,)),
            dma((2,)), dma((2,)), dma((2,)), dma((2,)), dma((2,)), dma((2,)),
        ],
        compiler_params=pltpu.CompilerParams(
            collective_id=0, has_side_effects=True, vmem_limit_bytes=48 << 20
        ),
    )(
        *(
            pltpu.with_memory_space_constraint(x, pltpu.HBM)
            for x in (placed, neighbour.T, face.T, orient.T, density, momentum, energy, metrics, volume)
        )
    )
    return pl.pallas_call(
        hand_over,
        out_shape=shapes,
        in_specs=[inside] * 4,
        out_specs=(anywhere,) * 3,
        scratch_shapes=[vmem((5, PLANES, ROWS, COLS), f32), dma((5,))],
    )(*(pltpu.with_memory_space_constraint(x, pltpu.VMEM) for x in results))


def solution(mesh):
    return jax.shard_map(
        local,
        mesh=mesh,
        in_specs=(
            P("blk", None, "ij", None),
            P("blk", None, None, "ij", None),
            P("blk", None, "ij", None),
            P("blk", None, "ij", None),
            P("blk", "ij", None),
            P(),
            P(),
            P(),
            P(),
        ),
        out_specs=(
            P("blk", None, "ij", None),
            P("blk", None, None, "ij", None),
            P("blk", None, "ij", None),
        ),
        check_vma=False,
    )
```

```python
import functools

import jax
import jax.numpy as jnp
from jax import lax
from jax.experimental import pallas as pl
from jax.experimental.pallas import tpu as pltpu
from jax.sharding import PartitionSpec as P

MESH = pl.DeviceIdType.MESH
pressure_factor = 0.4
viscosity = 0.05
conduction = 0.1
time_step = 0.03
ROWS, COLS, PLANES, CHUNK = 32, 128, 6, 8
Y, Z, CORES, IJ, BLOCKS = 4, 4, 2, 8, 32
LOW, HIGH = slice(6, 8), slice(40, 42)


def lanes(shape):
    return lax.broadcasted_iota(jnp.int32, shape, len(shape) - 1)


def rows_of(shape):
    return lax.broadcasted_iota(jnp.int32, shape, len(shape) - 2)


def shift_lanes(x, by):
    by = by % COLS
    return x if by == 0 else pltpu.roll(x, by, x.ndim - 1)


def primitives(rho, m1, m2, m3, energy, dt):
    inv = 1.0 / rho
    u1, u2, u3 = m1 * inv, m2 * inv, m3 * inv
    kinetic = 0.5 * (m1 * u1 + m2 * u2 + m3 * u3)
    p = pressure_factor * (energy - kinetic)
    head = energy + p
    soft = dt * viscosity / 12.0
    warm = dt * conduction / 12.0
    curved = (soft * u1, soft * u2, soft * u3, inv * (soft * kinetic + warm * p))
    return u1, u2, u3, p, head, curved


def flux(rho, m1, m2, m3, prim, gx, gy):
    u1, u2, u3, p, head, _ = prim
    speed = gx * u1 + gy * u2
    return (rho * speed, m1 * speed + gx * p, m2 * speed + gy * p, m3 * speed, head * speed)


def flux_planes(m1, m2, m3, prim):
    u1, u2, u3, p, head, _ = prim
    return (m3, m1 * u3, m2 * u3, m3 * u3 + p, head * u3)


def slope(b2, b1, a1, a2):
    return 8.0 * (a1 - b1) - (a2 - b2)


def curve(b2, b1, a1, a2):
    return 16.0 * (a1 + b1) - (a2 + b2)


def plane_shift(f, by):
    by = by % PLANES
    return jnp.concatenate([f[by:], f[:by]], axis=0)


def span(c):
    return slice(CHUNK + c * CHUNK, 2 * CHUNK + c * CHUNK)


def chunk_metrics(exm, c, dt):
    ax, ay, bx, by, v = (exm[n, span(c), :] for n in range(5))
    return (v * ax, v * ay, v * bx, v * by, (dt / 12.0) / v, ax * ax + ay * ay, bx * bx + by * by)


def before_ghosts(state, exm, fi, wi, part, dt, chunks):
    for c in chunks:
        gax, gay, gbx, gby, iv, rw, cw = chunk_metrics(exm, c, dt)
        center = -30.0 * (rw + cw + 1.0)
        rho, m1, m2, m3, energy = (state[ch, :, span(c), :] for ch in range(5))
        prim = primitives(rho, m1, m2, m3, energy, dt)
        curved = prim[5]
        inner = span(c + 1)
        for ch, f in enumerate(flux(rho, m1, m2, m3, prim, gax, gay)):
            fi[ch, :, inner, :] = f
        for n, w in enumerate(curved):
            wi[n, :, inner, :] = w
        fj = flux(rho, m1, m2, m3, prim, gbx, gby)
        fk = flux_planes(m1, m2, m3, prim)
        for ch in range(5):
            f, g = fj[ch], fk[ch]
            dj = slope(*(shift_lanes(f, by) for by in (2, 1, -1, -2)))
            dk = slope(*(plane_shift(g, by) for by in (-2, -1, 1, 2)))
            total = -(dj * iv) - (dt / 12.0) * dk
            if ch > 0:
                w = curved[ch - 1]
                sj = curve(*(shift_lanes(w, by) for by in (2, 1, -1, -2)))
                sk = curve(*(plane_shift(w, by) for by in (-2, -1, 1, 2)))
                total = total + cw * sj + sk + center * w
            part[ch, :, span(c), :] = total


def row_terms(exm, fi, wi, part, c, ch, dt):
    gax, gay, gbx, gby, iv, rw, cw = chunk_metrics(exm, c, dt)
    base = 2 * CHUNK + c * CHUNK
    di = slope(*(fi[ch, :, base + d : base + d + CHUNK, :] for d in (-2, -1, 1, 2)))
    total = part[ch, :, span(c), :] - di * iv
    if ch > 0:
        si = curve(*(wi[ch - 1, :, base + d : base + d + CHUNK, :] for d in (-2, -1, 1, 2)))
        total = total + rw * si
    return total


def apart(a, b):
    third = jnp.where(lanes(a.shape) < 32, shift_lanes(a, -96), shift_lanes(b, 32))
    return [a, shift_lanes(a, -48), third, shift_lanes(b, -16), shift_lanes(b, -64)]


def spread(x):
    x = jnp.where((lanes(x.shape) & 63) < 8, x, 0.0)
    pair = x + shift_lanes(x, 8)
    return pair + shift_lanes(pair, 16) + shift_lanes(pair, 32)


def lines(own, ghost):
    near = (lanes(own.shape) & 7) < 4
    first = jnp.where(near, ghost, own)
    second = jnp.where(near, own, ghost)
    return jnp.where(lanes(own.shape) < 64, first, shift_lanes(second, 64))


def line_planes(x, by):
    m = lanes(x.shape) & 63
    if by > 0:
        return jnp.where(m < 48 - 8 * by, shift_lanes(x, -8 * by), shift_lanes(x, 48 - 8 * by))
    return jnp.where(m >= -8 * by, shift_lanes(x, -8 * by), shift_lanes(x, -48 - 8 * by))


def edge_terms(mine, theirs):
    upper = (lanes(mine[0].shape) & 7) >= 4
    out = []
    for n in range(9):
        h = theirs[n] - mine[n]
        high, low = jnp.where(upper, h, 0.0), jnp.where(upper, 0.0, h)
        if n < 5:
            left = 8.0 * shift_lanes(high, -1) - shift_lanes(high, -2)
            right = shift_lanes(low, 2) - 8.0 * shift_lanes(low, 1)
        else:
            left = 16.0 * shift_lanes(high, -1) - shift_lanes(high, -2)
            right = 16.0 * shift_lanes(low, 1) - shift_lanes(low, 2)
        out.append(jnp.where(upper, right, left))
    return out


def edge_values(fields, gx, gy, dt):
    rho, m1, m2, m3, energy = fields
    prim = primitives(rho, m1, m2, m3, energy, dt)
    return flux(rho, m1, m2, m3, prim, gx, gy) + prim[5]


def column_metric(c, e):
    return jnp.concatenate([shift_lanes(c, -32 * g - 8 * e) for g in range(4)], axis=0)


def line_own(own, held, held_ends, dt):
    oa, ob, oc = own[0:32, :], own[32:64, :], own[64:72, :]
    for n, x in enumerate(apart(oa, ob)):
        held[n] = x
    held[5], held[6] = shift_lanes(ob, -112), shift_lanes(ob, -120)
    for e in range(3):
        held[7 + e] = column_metric(oc, e)
    few = slice(0, 4)
    oa, ob, od = own[72:76, :], own[76:80, :], own[80:84, :]
    mine = apart(oa, ob)
    values = edge_values(mine, *(spread(shift_lanes(ob, -n)) for n in (112, 120)), dt)
    for n, x in enumerate(tuple(mine) + (od, shift_lanes(od, -8)) + tuple(values)):
        held_ends[n, few, :] = x


def section_main(ghost, held, lf, lines1, keep, dt):
    ga, gb, gc = ghost[0:32, :], ghost[32:64, :], ghost[64:72, :]
    fields = [lines(held[n], x) for n, x in enumerate(apart(ga, gb))]
    gbx, gby = (spread(lines(held[5 + n], shift_lanes(gb, -112 - 8 * n))) for n in range(2))
    gax, gay, v = (spread(lines(held[7 + e], column_metric(gc, e))) for e in range(3))
    prim = primitives(*fields, dt)
    curved = prim[5]
    for n, f in enumerate(flux(*fields[:4], prim, gax, gay) + curved):
        lf[n, CHUNK : CHUNK + ROWS, :] = f
    inv = 1.0 / v
    iv = (dt / 12.0) * inv
    rw = (gax * gax + gay * gay) * (inv * inv)
    cw = (gbx * gbx + gby * gby) * (inv * inv)
    center = -30.0 * (rw + cw + 1.0)
    fj = flux(*fields[:4], prim, gbx, gby)
    fk = flux_planes(*fields[1:4], prim)
    for ch in range(5):
        lines1[ch] = fields[ch] + cross_rate(fj, fk, curved, iv, cw, center, ch, dt)
    lines1[5], lines1[6] = gbx, gby
    keep[0], keep[1] = iv, rw


def section_ends(ghost, held_ends, lf, dt):
    few = slice(0, 4)
    ga, gb, gd = ghost[72:76, :], ghost[76:80, :], ghost[80:84, :]
    theirs = apart(ga, gb)
    hax, hay = (spread(lines(held_ends[5 + n, few, :], shift_lanes(gd, -8 * n))) for n in range(2))
    ends = [lines(held_ends[n, few, :], x) for n, x in enumerate(theirs)]
    prim = primitives(*ends, dt)
    for n, f in enumerate(flux(*ends[:4], prim, hax, hay) + prim[5]):
        lf[n, LOW, :] = f[0:2]
        lf[n, HIGH, :] = f[2:4]
    return edge_terms(
        [held_ends[7 + n, few, :] for n in range(9)],
        edge_values(theirs, *(spread(shift_lanes(gb, -n)) for n in (112, 120)), dt),
    )


def pack(ex, exm, strips, relay):
    at = lanes((ROWS, COLS)) >> 3
    inside = slice(CHUNK, CHUNK + ROWS)
    v = exm[4, inside, :]
    for half in range(2):
        acc = jnp.zeros((ROWS, COLS), jnp.float32)
        for n in range(16):
            q = 16 * half + n
            x = ex[q // 6, q % 6, inside, :] if q < 30 else v * exm[q - 28, inside, :]
            acc = jnp.where(at == n, shift_lanes(x, 4 + 8 * n), acc)
        strips[0, 32 * half : 32 * half + 32, :] = acc
    slot = lanes((CHUNK, COLS)) >> 3
    acc = jnp.zeros((CHUNK, COLS), jnp.float32)
    for g in range(4):
        part = exm[4, span(g), :]
        for e in range(3):
            x = part * exm[e, span(g), :] if e < 2 else part
            acc = jnp.where(slot == 4 * g + e, shift_lanes(x, 4 + 32 * g + 8 * e), acc)
    strips[0, 64:72, :] = acc
    for side, r in ((0, 0), (1, ROWS - 2)):
        relay[side, 0:2, :] = strips[0, r : r + 2, :]
        relay[side, 2:4, :] = strips[0, 32 + r : 34 + r, :]
        relay[side, 4:6, :] = shift_lanes(acc[r % CHUNK : r % CHUNK + 2], -32 * (r // CHUNK))
        relay[side, 6:8, :] = jnp.zeros((2, COLS), jnp.float32)
    return acc


def turn_strips(strips, acc):
    for r in range(ROWS):
        for half in (0, 32):
            strips[1, half + 31 - r : half + 32 - r, :] = strips[0, half + r : half + r + 1, :]
    turned = jnp.where((lanes(acc.shape) & 32) == 0, shift_lanes(acc, 32), shift_lanes(acc, -32))
    turned = jnp.where((lanes(acc.shape) & 31) < 16, -turned, turned)
    for r in range(CHUNK):
        strips[1, 71 - r : 72 - r, :] = turned[r : r + 1, :]


def pack_ends(relay, arrived, strips, at_start, at_end):
    turn = lanes((1, COLS))
    signs = (
        jnp.where(turn >= 48, -1.0, 1.0),
        jnp.where(turn < 64, -1.0, 1.0),
        jnp.ones((1, COLS), jnp.float32),
    )
    for n in range(3):
        base = 72 + 4 * n
        for r in range(4):
            near = 2 * n + r % 2
            wall = 2 * n + 1 - r % 2
            side = r // 2
            mirror = relay[side, wall : wall + 1, :]
            if side == 0:
                row = jnp.where(at_start, signs[n] * mirror, arrived[side, near : near + 1, :])
            else:
                row = jnp.where(at_end, mirror, arrived[side, near : near + 1, :])
            strips[0, base + r : base + r + 1, :] = row
            strips[1, base + 3 - r : base + 4 - r, :] = -row if n == 2 else row
    for m in range(2):
        strips[m, 84:88, :] = jnp.zeros((4, COLS), jnp.float32)


def walls(state, at_start, at_end):
    for ch in range(5):
        sign = -1.0 if 1 <= ch <= 3 else 1.0
        for r in range(2):
            low, high = slice(7 - r, 8 - r), slice(40 + r, 41 + r)
            mirror = state[ch, :, 8 + r : 9 + r, :]
            state[ch, :, low, :] = jnp.where(at_start, sign * mirror, state[ch, :, low, :])
            mirror = state[ch, :, 39 - r : 40 - r, :]
            state[ch, :, high, :] = jnp.where(at_end, mirror, state[ch, :, high, :])


def metric_walls(exm, at_start, at_end):
    for r in range(2):
        low, high = slice(7 - r, 8 - r), slice(40 + r, 41 + r)
        exm[:, low, :] = jnp.where(at_start, exm[:, 8 + r : 9 + r, :], exm[:, low, :])
        exm[:, high, :] = jnp.where(at_end, exm[:, 39 - r : 40 - r, :], exm[:, high, :])


def halo_rows(state, exm, fi, wi, dt):
    for rows in (LOW, HIGH):
        rho, m1, m2, m3, energy = (state[ch, :, rows, :] for ch in range(5))
        v = exm[4, rows, :]
        prim = primitives(rho, m1, m2, m3, energy, dt)
        target = slice(rows.start + CHUNK, rows.stop + CHUNK)
        for ch, f in enumerate(flux(rho, m1, m2, m3, prim, v * exm[0, rows, :], v * exm[1, rows, :])):
            fi[ch, :, target, :] = f
        for n, w in enumerate(prim[5]):
            wi[n, :, target, :] = w


def gather_lines(planes, shape):
    at = lanes(shape) >> 3
    acc = jnp.zeros(shape, jnp.float32)
    for k, x in enumerate(planes):
        acc = jnp.where(at == k, shift_lanes(x, 8 * k + 2), acc)
        acc = jnp.where(at == 8 + k, shift_lanes(x, 8 * k - 58), acc)
    return acc


def metric_line(x):
    return spread(jnp.where(lanes(x.shape) < 64, shift_lanes(x, 2), shift_lanes(x, -58)))


def line_prepare(sec, exm, inner, inner_ends, metric, metric_ends):
    inside = slice(CHUNK, CHUNK + ROWS)
    for ch in range(5):
        inner[ch] = gather_lines([sec[ch, k, inside, :] for k in range(PLANES)], (ROWS, COLS))
    ax, ay, bx, by, v = (exm[n, inside, :] for n in range(5))
    values = (v * ax, v * ay, v * bx, v * by, 1.0 / v, ax * ax + ay * ay, bx * bx + by * by)
    for n, x in enumerate(values):
        metric[n] = metric_line(x)
    for side, rows in enumerate((LOW, HIGH)):
        at = slice(2 * side, 2 * side + 2)
        for ch in range(5):
            inner_ends[ch, at, :] = gather_lines([sec[ch, k, rows, :] for k in range(PLANES)], (2, COLS))
        ax, ay, bx, by, v = (exm[n, rows, :] for n in range(5))
        for n, x in enumerate((v * ax, v * ay, 1.0 / v, bx * bx + by * by)):
            metric_ends[n, at, :] = metric_line(x)


def line_result(
    lines2, gb, inner, inner_ends, metric, metric_ends, terms, lf, last, at_start, at_end, before, dt, store, finish
):
    shape = (CHUNK, COLS)
    t, left = lanes(shape) & 7, lanes(shape) < 64
    near = t < 4

    def join(p, own):
        return jnp.where(left, jnp.where(near, shift_lanes(p, -2), own), jnp.where(near, own, shift_lanes(p, 2)))

    kept = {}
    for c in store:
        rows = slice(c * CHUNK, (c + 1) * CHUNK)
        fields = [join(lines2[ch, rows, :], inner[ch, rows, :]) for ch in range(5)]
        prim = primitives(*fields, dt)
        for n, f in enumerate(flux(*fields[:4], prim, metric[0, rows, :], metric[1, rows, :]) + prim[5]):
            lf[n, span(c), :] = f
        kept[c] = (rows, fields, prim)
    if terms is not None:
        few = slice(0, 4)
        te, le = lanes((4, COLS)) & 7, lanes((4, COLS)) < 64

        def place(e):
            here = jnp.where(le & ((te >> 1) == 1), shift_lanes(e, -2), 0.0)
            return jnp.where(jnp.logical_not(le) & ((te >> 1) == 2), shift_lanes(e, 66), here)

        inv_e, cw_e = metric_ends[2, few, :], metric_ends[3, few, :]
        ends = []
        for ch in range(5):
            h = inner_ends[ch, few, :] - place(terms[ch]) * ((before / 12.0) * inv_e)
            if ch > 0:
                h = h + cw_e * place(terms[4 + ch])
            sign = -1.0 if 1 <= ch <= 3 else 1.0
            f, g = kept[0][1][ch], kept[3][1][ch]
            wall = jnp.concatenate([sign * f[1:2], sign * f[0:1], g[7:8], g[6:7]], axis=0)
            r = rows_of((4, COLS))
            use = jnp.where(at_start, 1, 0) * jnp.where(r < 2, 1, 0) + jnp.where(at_end, 1, 0) * jnp.where(r >= 2, 1, 0)
            ends.append(jnp.where(use > 0, wall, h))
        end_prim = primitives(*ends, dt)
        for n, f in enumerate(
            flux(*ends[:4], end_prim, metric_ends[0, few, :], metric_ends[1, few, :]) + end_prim[5]
        ):
            lf[n, LOW, :] = f[0:2]
            lf[n, HIGH, :] = f[2:4]
    for c in finish:
        rows, fields, prim = kept[c]
        gbx, gby = (join(gb[5 + n, rows, :], metric[2 + n, rows, :]) for n in range(2))
        inv, rw, cw = (metric[n, rows, :] for n in (4, 5, 6))
        iv = (dt / 12.0) * inv
        center = -30.0 * (rw + cw + 1.0)
        fj = flux(*fields[:4], prim, gbx, gby)
        fk = flux_planes(*fields[1:4], prim)
        for ch in range(5):
            value = 0.5 * fields[ch] + row_rate(lf, iv, rw, ch, rows)
            value = value + cross_rate(fj, fk, prim[5], iv, cw, center, ch, dt)
            last[ch, rows, :] = jnp.where((t >= 2) & (t < 6), value, shift_lanes(value, -68))


def add_rows(lf, lines1, lines2, keep, chunks):
    for c in chunks:
        rows = slice(c * CHUNK, (c + 1) * CHUNK)
        for ch in range(5):
            lines2[ch, rows, :] = lines1[ch, rows, :] + row_rate(lf, keep[0, rows, :], keep[1, rows, :], ch, rows)


def row_rate(lf, iv, rw, ch, rows):
    base, size = CHUNK + rows.start, rows.stop - rows.start
    value = -(slope(*(lf[ch, base + d : base + d + size, :] for d in (-2, -1, 1, 2))) * iv)
    if ch > 0:
        value = value + rw * curve(*(lf[4 + ch, base + d : base + d + size, :] for d in (-2, -1, 1, 2)))
    return value


def cross_rate(fj, fk, curved, iv, cw, center, ch, dt):
    dj = slope(*(shift_lanes(fj[ch], by) for by in (2, 1, -1, -2)))
    dk = slope(*(line_planes(fk[ch], by) for by in (-2, -1, 1, 2)))
    value = -(dj * iv) - (dt / 12.0) * dk
    if ch > 0:
        w = curved[ch - 1]
        sj = curve(*(shift_lanes(w, by) for by in (2, 1, -1, -2)))
        sk = curve(*(line_planes(w, by) for by in (-2, -1, 1, 2)))
        value = value + cw * sj + sk + center * w
    return value


def exchange_lanes(x, distances):
    t = lanes(x.shape) & 7
    for d in distances:
        x = jnp.where((t & d) == 0, shift_lanes(x, -d), shift_lanes(x, d))
    return x


def settle(x, sign, table):
    same = [jnp.where(table[f][1] == f, 1, 0) for f in range(2)]
    turned = jnp.where((lanes(x.shape) & 7) < 4, same[0], same[1]) > 0
    return jnp.where(turned, exchange_lanes(x, (2, 1)) * sign, x)


def peers_first(y, z, c, s):
    out = []
    for dy in range(Y):
        for m in range(2):
            blk = (lax.rem(y + dy, Y) * Z + z) * CORES + c
            out.append({"blk": blk, "ij": (IJ - 1 - s) if m else s})
    return out


def peers_second(y, z, c, s):
    out = []
    for dz in range(Z):
        for dc in range(2):
            blk = (y * Z + lax.rem(z + dz, Z)) * CORES + (1 - c if dc else c)
            out.append({"blk": blk, "ij": s})
    return out


def routes(placed, neighbour, face, orient, targets):
    ids = [placed[t["blk"]] for t in targets]
    wanted = [(b, f) for b in ids for f in range(2)]
    nids = [neighbour[f, b] for b, f in wanted]

    def find(p, found):
        held = placed[p]
        return tuple(jnp.where(n == held, p, a) for n, a in zip(nids, found))

    found = lax.fori_loop(0, BLOCKS, find, tuple(jnp.int32(0) for _ in nids))
    return [(q, face[f, b], orient[f, b]) for q, (b, f) in zip(found, wanted)]


def body(
    placed_hbm, neighbour_hbm, face_hbm, orient_hbm, dens_hbm, mom_hbm, ener_hbm, met_hbm, vol_hbm,
    out_d, out_m, out_e, last,
    placed, neighbour, face, orient, load,
    ex, exm, sec, fi, wi, part, lf, lf2, lines1, lines2, inner, inner_ends, metric, metric_ends,
    held, held_ends, keep,
    strips, relay, arrived, got, both, picked, got2, both_e, picked_e, got2_e, ghost,
    send1, recv1, send_h, recv_h, send2, recv2, send_f, recv_f, send_e, recv_e, send_r, recv_r, send_m, recv_m,
):
    inside = pl.ds(CHUNK, ROWS)
    fetch = [
        pltpu.make_async_copy(src, dst, load.at[n])
        for n, (src, dst) in enumerate(
            (
                (mom_hbm.at[0], ex.at[pl.ds(1, 3), :, inside]),
                (dens_hbm.at[0], ex.at[0, :, inside]),
                (ener_hbm.at[0], ex.at[4, :, inside]),
                (met_hbm.at[0], exm.at[pl.ds(0, 4), inside]),
                (vol_hbm.at[0], exm.at[4, inside]),
                (placed_hbm, placed),
                (neighbour_hbm, neighbour),
                (face_hbm, face),
                (orient_hbm, orient),
            )
        )
    ]
    for copy in fetch:
        copy.start()
    b, s = lax.axis_index("blk"), lax.axis_index("ij")
    c = lax.rem(b, CORES)
    z = lax.rem(b // CORES, Z)
    y = b // (CORES * Z)
    first, second = peers_first(y, z, c, s), peers_second(y, z, c, s)
    below = {"blk": b, "ij": lax.rem(s + IJ - 1, IJ)}
    above = {"blk": b, "ij": lax.rem(s + 1, IJ)}
    everyone = first[1:] + second[1:] + [below, above]
    barrier = pltpu.get_barrier_semaphore()
    for peer in everyone:
        pl.semaphore_signal(barrier, inc=1, device_id=peer, device_id_type=MESH)
    at_start, at_end = s == 0, s == IJ - 1
    for copy in fetch[:5]:
        copy.wait()
    acc = pack(ex, exm, strips, relay)
    pl.semaphore_wait(barrier, len(everyone))

    def send(src, dst, out_sem, in_sem, peer):
        copy = pltpu.make_async_remote_copy(
            src_ref=src, dst_ref=dst, send_sem=out_sem, recv_sem=in_sem,
            device_id=peer, device_id_type=MESH,
        )
        copy.start()
        return copy

    main, ends = pl.ds(0, 72), pl.ds(72, 16)
    beside = (below, above)
    order = (2, 4, 1, 3, 5, 6, 7)
    edges = [
        send(relay.at[n], arrived.at[1 - n], send_e.at[n], recv_e.at[1 - n], beside[n]) for n in range(2)
    ]
    hop1 = {}
    for k in (4, 2, 6, 5, 3, 7, 1):
        if k == 5:
            turn_strips(strips, acc)
        hop1[k] = send(strips.at[k % 2, main], got.at[k, main], send1.at[k], recv1.at[k], first[k])
    for copy in fetch[5:]:
        copy.wait()
    table = routes(placed, neighbour, face, orient, second)
    before_ghosts(ex, exm, fi, wi, part, time_step, range(4))
    for copy in edges:
        copy.wait_send()
    for n in range(2):
        pltpu.make_async_remote_copy(
            src_ref=relay.at[n], dst_ref=arrived.at[n], send_sem=send_e.at[n], recv_sem=recv_e.at[n],
            device_id=beside[n], device_id_type=MESH,
        ).wait_recv()
    pack_ends(relay, arrived, strips, at_start, at_end)
    hop_ends = {
        k: send(strips.at[k % 2, ends], got.at[k, ends], send_h.at[k], recv_h.at[k], first[k]) for k in order
    }
    slide = []
    for n in range(2):
        src, dst = pl.ds((CHUNK, ROWS + 4)[n], 4), pl.ds((CHUNK + ROWS, 4)[n], 4)
        slide.append(send(exm.at[:, src], exm.at[:, dst], send_m.at[n], recv_m.at[1 - n], beside[n]))
        slide.append(send(ex.at[:, :, src], ex.at[:, :, dst], send_r.at[n], recv_r.at[1 - n], beside[n]))
    main_sign = jnp.where((rows_of((72, COLS)) >= 32) & (rows_of((72, COLS)) < 64) & (lanes((72, COLS)) >= 112), -1.0, 1.0)
    ends_sign = jnp.where(
        (rows_of((16, COLS)) >= 4) & (rows_of((16, COLS)) < 8) & (lanes((16, COLS)) >= 112), -1.0, 1.0
    )
    slots = []
    for q, g, o in table:
        slots.append((lax.rem(y - q // (CORES * Z) + Y, Y) * 2 + o, g))
    near = (lanes((72, COLS)) & 7) < 4
    hop2 = []
    for piece, size, copies, variants, chosen, landed, sems in (
        (slice(0, 72), 72, hop1, both, picked, got2, (send2, recv2)),
        (slice(72, 88), 16, hop_ends, both_e, picked_e, got2_e, (send_f, recv_f)),
    ):
        for k in (0, 1, 2, 3, 6, 7, 4, 5):
            if k > 0:
                copies[k].wait_recv()
                x = got[k, piece, :]
            else:
                x = strips[0, piece, :]
            variants[k] = x
            variants[8 + k] = exchange_lanes(x, (4,))
        for k in (4, 5, 2, 3, 6, 7, 1, 0):
            parts = []
            for f in range(2):
                slot, g = slots[2 * k + f]
                parts.append(variants[jnp.where(g == f, 8, 0) + slot])
            message = jnp.where(near[:size], parts[0], parts[1])
            if k == 0:
                landed[0] = message
            else:
                chosen[k] = message
                hop2.append(send(chosen.at[k], landed.at[k], sems[0].at[k], sems[1].at[k], second[k]))
    for copy in slide:
        copy.wait_send()
    for n in range(2):
        dst = pl.ds((4, CHUNK + ROWS)[n], 4)
        pltpu.make_async_remote_copy(
            src_ref=exm.at[:, dst], dst_ref=exm.at[:, dst], send_sem=send_m.at[n], recv_sem=recv_m.at[n],
            device_id=beside[n], device_id_type=MESH,
        ).wait_recv()
        pltpu.make_async_remote_copy(
            src_ref=ex.at[:, :, dst], dst_ref=ex.at[:, :, dst], send_sem=send_r.at[n], recv_sem=recv_r.at[n],
            device_id=beside[n], device_id_type=MESH,
        ).wait_recv()
    walls(ex, at_start, at_end)
    metric_walls(exm, at_start, at_end)
    before_ghosts(ex, exm, fi, wi, part, time_step, (-1, 4))
    for n in range(-1, 5):
        for ch in range(5):
            sec[ch, :, span(n), :] = ex[ch, :, span(n), :] + row_terms(exm, fi, wi, part, n, ch, time_step)
    walls(sec, at_start, at_end)
    half = 0.5 * time_step
    line_prepare(sec, exm, inner, inner_ends, metric, metric_ends)
    before_ghosts(sec, exm, fi, wi, part, half, range(4))
    halo_rows(sec, exm, fi, wi, half)

    def output(ch, plane, rows):
        if ch == 0:
            return out_d.at[0, plane, rows]
        if ch == 4:
            return out_e.at[0, plane, rows]
        return out_m.at[0, ch - 1, plane, rows]

    for n in range(4):
        rows = slice(n * CHUNK, (n + 1) * CHUNK)
        for ch in range(5):
            value = 0.5 * (ex[ch, :, span(n), :] + sec[ch, :, span(n), :])
            value = value + row_terms(exm, fi, wi, part, n, ch, half)
            at = lanes(value.shape)
            border = (at < 4) | (at >= COLS - 4)
            output(ch, slice(None), rows)[...] = jnp.where(border, 0.5 * ex[ch, :, span(n), :], value)
    origin = []
    for f in range(2):
        q, g, o = table[f]
        dz = lax.rem(z - lax.rem(q // CORES, Z) + Z, Z)
        dc = jnp.where(lax.rem(q, CORES) == c, 0, 1)
        origin.append(2 * dz + dc)
    line_own(strips.at[0], held, held_ends, time_step)
    for copy in hop2[:7]:
        copy.wait_recv()
    ghost[0:72, :] = settle(jnp.where(near, got2[origin[0]], got2[origin[1]]), main_sign, table)
    section_main(ghost, held, lf, lines1, keep, time_step)
    add_rows(lf, lines1, lines2, keep, range(4))
    line_result(
        lines2, lines1, inner, inner_ends, metric, metric_ends, None, lf2, last,
        at_start, at_end, time_step, half, range(4), (1, 2),
    )
    for copy in hop2[7:]:
        copy.wait_recv()
    ghost[72:88, :] = settle(jnp.where(near[:16], got2_e[origin[0]], got2_e[origin[1]]), ends_sign, table)
    terms = section_ends(ghost, held_ends, lf, time_step)
    add_rows(lf, lines1, lines2, keep, (0, 3))
    line_result(
        lines2, lines1, inner, inner_ends, metric, metric_ends, terms, lf2, last,
        at_start, at_end, time_step, half, (0, 3), (0, 3),
    )
    for copy in list(hop1.values()) + list(hop_ends.values()) + hop2:
        copy.wait_send()


def hand_over(d, m, e, last, out_d, out_m, out_e, result, sems):
    at = lanes((ROWS, COLS))
    border = (at < 4) | (at >= COLS - 4)
    copies = []
    for ch in (1, 2, 3, 0, 4):
        source = d.at[0] if ch == 0 else e.at[0] if ch == 4 else m.at[0, ch - 1]
        target = out_d.at[0] if ch == 0 else out_e.at[0] if ch == 4 else out_m.at[0, ch - 1]
        for k in range(PLANES):
            x = shift_lanes(last[ch], -8 * k - 2)
            result[ch, k] = source[k] + jnp.where(border, x, 0.0)
        copies.append(pltpu.make_async_copy(result.at[ch], target, sems.at[ch]))
        copies[-1].start()
    for copy in copies:
        copy.wait()


def local(density, momentum, energy, metrics, volume, placed, neighbour, face, orient):
    smem, vmem, i32, f32 = pltpu.SMEM, pltpu.VMEM, jnp.int32, jnp.float32
    anywhere = pl.BlockSpec(memory_space=pltpu.HBM)
    inside = pl.BlockSpec(memory_space=pltpu.VMEM)
    dma = pltpu.SemaphoreType.DMA
    padded = ROWS + 2 * CHUNK
    shapes = tuple(jax.ShapeDtypeStruct(x.shape, f32) for x in (density, momentum, energy))
    results = pl.pallas_call(
        body,
        out_shape=shapes + (jax.ShapeDtypeStruct((5, ROWS, COLS), f32),),
        in_specs=[anywhere] * 9,
        out_specs=(inside,) * 4,
        scratch_shapes=[
            smem((BLOCKS,), i32), smem((2, BLOCKS), i32), smem((2, BLOCKS), i32), smem((2, BLOCKS), i32),
            dma((9,)),
            vmem((5, PLANES, padded, COLS), f32),
            vmem((5, padded, COLS), f32),
            vmem((5, PLANES, padded, COLS), f32),
            vmem((5, PLANES, padded + 2 * CHUNK, COLS), f32),
            vmem((4, PLANES, padded + 2 * CHUNK, COLS), f32),
            vmem((5, PLANES, padded, COLS), f32),
            vmem((9, padded, COLS), f32),
            vmem((9, padded, COLS), f32),
            vmem((7, ROWS, COLS), f32),
            vmem((5, ROWS, COLS), f32),
            vmem((5, ROWS, COLS), f32),
            vmem((5, CHUNK, COLS), f32),
            vmem((7, ROWS, COLS), f32),
            vmem((4, CHUNK, COLS), f32),
            vmem((10, ROWS, COLS), f32),
            vmem((16, CHUNK, COLS), f32),
            vmem((2, ROWS, COLS), f32),
            vmem((2, 88, COLS), f32),
            vmem((2, CHUNK, COLS), f32),
            vmem((2, CHUNK, COLS), f32),
            vmem((8, 88, COLS), f32),
            vmem((16, 72, COLS), f32),
            vmem((8, 72, COLS), f32),
            vmem((8, 72, COLS), f32),
            vmem((16, 16, COLS), f32),
            vmem((8, 16, COLS), f32),
            vmem((8, 16, COLS), f32),
            vmem((88, COLS), f32),
            dma((8,)), dma((8,)), dma((8,)), dma((8,)), dma((8,)), dma((8,)), dma((8,)), dma((8,)),
            dma((2,)), dma((2,)), dma((2,)), dma((2,)), dma((2,)), dma((2,)),
        ],
        compiler_params=pltpu.CompilerParams(
            collective_id=0, has_side_effects=True, vmem_limit_bytes=48 << 20
        ),
    )(
        *(
            pltpu.with_memory_space_constraint(x, pltpu.HBM)
            for x in (placed, neighbour.T, face.T, orient.T, density, momentum, energy, metrics, volume)
        )
    )
    return pl.pallas_call(
        hand_over,
        out_shape=shapes,
        in_specs=[inside] * 4,
        out_specs=(anywhere,) * 3,
        scratch_shapes=[vmem((5, PLANES, ROWS, COLS), f32), dma((5,))],
    )(*(pltpu.with_memory_space_constraint(x, pltpu.VMEM) for x in results))


def solution(mesh):
    return jax.shard_map(
        local,
        mesh=mesh,
        in_specs=(
            P("blk", None, "ij", None),
            P("blk", None, None, "ij", None),
            P("blk", None, "ij", None),
            P("blk", None, "ij", None),
            P("blk", "ij", None),
            P(),
            P(),
            P(),
            P(),
        ),
        out_specs=(
            P("blk", None, "ij", None),
            P("blk", None, None, "ij", None),
            P("blk", None, "ij", None),
        ),
        check_vma=False,
    )
```
